32 devices in a mesh: head: 4 (over y, x), blk: 8 (over z, core).
Axes of the slice: x: 2, y: 2, z: 4, core: 2. Of those that a mesh axis runs over, the one named last changes fastest.
Arguments:
- tokens: bfloat16 [4096, 2048], P(('head', 'blk')), may hold values from -6 to 6
- query_weight: bfloat16 [2048, 2048], P(('head', 'blk')), may hold values from -0.125 to 0.125
- key_weight: bfloat16 [2048, 2048], P(('head', 'blk')), may hold values from -0.125 to 0.125
- value_weight: bfloat16 [2048, 2048], P(('head', 'blk')), may hold values from -0.125 to 0.125
- output_weight: bfloat16 [2048, 2048], P(('head', 'blk')), may hold values from -4 to 4
- mixing_gain: bfloat16 [2048], P(('head', 'blk')), may hold values from 0.5 to 1.5
- query_gain: bfloat16 [2048], P(('head', 'blk')), may hold values from 0.5 to 1.5
- key_gain: bfloat16 [2048], P(('head', 'blk')), may hold values from 0.5 to 1.5
- routing_gain: bfloat16 [2048], P(('head', 'blk')), may hold values from 0.5 to 1.5
- router_weight: bfloat16 [2048, 16], P(('head', 'blk')), may hold values from -0.125 to 0.125
- gate_weight: bfloat16 [16, 2048, 1024], P('blk', 'head'), may hold values from -0.125 to 0.125
- up_weight: bfloat16 [16, 2048, 1024], P('blk', 'head'), may hold values from -0.125 to 0.125
- down_weight: bfloat16 [16, 1024, 2048], P('blk', 'head'), may hold values from -3 to 3
- seq_lengths: int32 [3], replicated, may hold values from 1024 to 2048, as said below
- dealt_order: int32 [4096], replicated, may hold values from 0 to 4095, as said below
- expert_routes: int32 [4096, 8], P(('head', 'blk')), may hold values from 0 to 15, all different within a row
- slot_order: int32 [4096, 8], P(('head', 'blk')), may hold values from 0 to 1023, as said below
- cotangent: bfloat16 [4096, 2048], P(('head', 'blk')), may hold values from -6 to 6
Outputs:
- block_output: bfloat16 [4096, 2048], P(('head', 'blk'))
- tokens_grad: float32 [4096, 2048], P(('head', 'blk'))
- query_grad: float32 [2048, 2048], P(('head', 'blk'))
- key_grad: float32 [2048, 2048], P(('head', 'blk'))
- value_grad: float32 [2048, 2048], P(('head', 'blk'))
- output_grad: float32 [2048, 2048], P(('head', 'blk'))
- mixing_grad: float32 [2048], P(('head', 'blk'))
- querynorm_grad: float32 [2048], P(('head', 'blk'))
- keynorm_grad: float32 [2048], P(('head', 'blk'))
- routing_grad: float32 [2048], P(('head', 'blk'))
- router_grad: float32 [2048, 16], P(('head', 'blk'))
- gate_grad: float32 [16, 2048, 1024], P('blk', 'head')
- up_grad: float32 [16, 2048, 1024], P('blk', 'head')
- down_grad: float32 [16, 1024, 2048], P('blk', 'head')
The draws below stay inside these ranges and needn't reach their ends.
Inputs may be any that keep to these rules, and one draw needn't show every extreme that they name: `seq_lengths`: 3 lengths summing to 4096, the largest exactly 2048. `dealt_order`: a permutation of the stream; the rows of the devices of one index of blk, taken in head order, are two runs of 256 consecutive stream tokens, runs c and 15 - c. `expert_routes`: each row names 8 different experts. `slot_order`: within each aligned block of 128 rows the entries are 0 to 1023, each once.
All inputs are finite; a program needn't handle non-finite values.
Results may differ from the reference program's by a relative error of at most 0.022.
Values may be sent and summed in bfloat16 or wider, within the bound.
No kernel may reach another device: no remote copies, remote signals or barrier semaphores. Data moves between devices by JAX's collectives and lax.ppermute only.
A program may use at most 320 MiB of HBM per device.

```python
import math
import jax
import jax.numpy as jnp
from jax import lax

D = 2048
HEADS = 16
HDIM = 128
FF = 1024
TOP = 8
TOK_DEV = 128
MINLEN = 1024
TOKENS = 4096
E = 16
LONGEST = 2048
NSEQ = 3
SPAN = 256
CAP_SRC = 80


def draw_seq_lengths(key, part):
    others = NSEQ - 1
    spare = TOKENS - LONGEST - others * MINLEN
    shares = jax.random.randint(jax.random.fold_in(key, 11), (others,), 50, 100, dtype=jnp.int32)
    given = spare * shares // jnp.sum(shares)
    leftover = spare - jnp.sum(given)
    given = given + (jnp.arange(others, dtype=jnp.int32) < leftover).astype(jnp.int32)
    rest = MINLEN + given
    longest_at = jax.random.randint(jax.random.fold_in(key, 12), (), 0, NSEQ, dtype=jnp.int32)
    index = jnp.arange(NSEQ, dtype=jnp.int32)
    source = jnp.clip(index - (index > longest_at).astype(jnp.int32), 0, others - 1)
    shifted = jnp.take(rest, source)
    return jnp.where(index == longest_at, LONGEST, shifted).astype(jnp.int32)


def draw_dealt_order(key, part):
    groups = TOKENS // (2 * SPAN)
    pairing = jax.random.permutation(jax.random.fold_in(key, 21), groups).astype(jnp.int32)
    rows = jnp.arange(TOKENS, dtype=jnp.int32)
    block = rows // TOK_DEV
    inner = rows % TOK_DEV
    head_of = block // groups
    group_of = block % groups
    within = head_of * TOK_DEV + inner
    second = within // SPAN
    offset = within % SPAN
    chosen = pairing[group_of]
    run = jnp.where(second == 0, chosen, 2 * groups - 1 - chosen)
    return (run * SPAN + offset).astype(jnp.int32)


def draw_slot_order(key, part):
    blocks = TOKENS // TOK_DEV

    def one_block(index):
        return jax.random.permutation(jax.random.fold_in(jax.random.fold_in(key, 31), index), TOK_DEV * TOP).astype(jnp.int32)
    orders = jax.vmap(one_block)(jnp.arange(blocks, dtype=jnp.int32))
    return orders.reshape(TOKENS, TOP).astype(jnp.int32)


def steps_of(rng, extent, cuts, low, largest):
    def one(axis_at, shards_of):
        draws = jax.random.uniform(jax.random.fold_in(jax.random.fold_in(rng, 6), axis_at), (shards_of,), jnp.float32, low / len(cuts), largest / len(cuts))
        return jnp.repeat(jnp.exp(draws), extent[axis_at] // shards_of).reshape((-1,) + (1,) * (len(extent) - axis_at - 1))

    factor_of = one(*cuts[0])
    for cut in cuts[1:]:
        factor_of = factor_of * one(*cut)
    return factor_of


def choose_distinct(rng, rows, amount, top, lift):
    order = jax.random.permutation(jax.random.fold_in(rng, 1), amount)
    pull = order
    for power in range(3):
        pull = pull * pull // amount
    pull = pull * lift // amount
    chance = jax.random.randint(jax.random.fold_in(rng, 2), (rows, amount), 0, 4096) + pull
    holders = jax.random.permutation(jax.random.fold_in(rng, 3), rows)[jnp.arange(amount) % rows]
    chance = jnp.where(jnp.arange(rows)[:, None] == holders[None, :], 1 << 14, chance)
    merit = chance * amount + jnp.arange(amount)
    return lax.top_k(merit.astype(jnp.int32), top)[1].astype(jnp.int32)


def centred(stream_key, extent, width, most, shards=(), kind=jnp.bfloat16):
    values = width * jax.random.normal(stream_key, extent, jnp.float32)
    if shards:
        values = values * steps_of(stream_key, extent, shards, -0.22, 0.18)
    return jnp.clip(values, -most, most).astype(kind)


def setup_inputs(seed: int = 0) -> dict:
    key_list = jax.random.split(jax.random.key(seed), 19)
    return {
        "tokens": centred(key_list[0], (TOKENS, D), 1.0, 6.0, ((0, 32),)),
        "query_weight": centred(key_list[1], (D, D), D ** -0.5, 0.125, ((0, 32),)),
        "key_weight": centred(key_list[2], (D, D), D ** -0.5, 0.125, ((0, 32),)),
        "value_weight": centred(key_list[3], (D, D), D ** -0.5, 0.125, ((0, 32),)),
        "output_weight": centred(key_list[4], (D, D), 2 ** -0.5, 4.0, ((0, 32),)),
        "mixing_gain": jnp.clip(1.0 + 0.1 * jax.random.normal(key_list[5], (D,), jnp.float32), 0.5, 1.5).astype(jnp.bfloat16),
        "query_gain": jnp.clip(1.0 + 0.1 * jax.random.normal(key_list[6], (D,), jnp.float32), 0.5, 1.5).astype(jnp.bfloat16),
        "key_gain": jnp.clip(1.0 + 0.1 * jax.random.normal(key_list[7], (D,), jnp.float32), 0.5, 1.5).astype(jnp.bfloat16),
        "routing_gain": jnp.clip(1.0 + 0.1 * jax.random.normal(key_list[8], (D,), jnp.float32), 0.5, 1.5).astype(jnp.bfloat16),
        "router_weight": centred(key_list[9], (D, E), D ** -0.5, 0.125, ((0, 32),)),
        "gate_weight": centred(key_list[10], (E, D, FF), D ** -0.5, 0.125, ((0, 8), (1, 4))),
        "up_weight": centred(key_list[11], (E, D, FF), D ** -0.5, 0.125, ((0, 8), (1, 4))),
        "down_weight": centred(key_list[12], (E, FF, D), (max(1, FF // 256)) ** -0.5, 3.0, ((0, 8), (1, 4))),
        "seq_lengths": draw_seq_lengths(jax.random.fold_in(key_list[18], 71), 0),
        "dealt_order": draw_dealt_order(jax.random.fold_in(key_list[18], 71), 0),
        "expert_routes": choose_distinct(key_list[15], TOKENS, E, TOP, 8192),
        "slot_order": draw_slot_order(jax.random.fold_in(key_list[18], 71), 0),
        "cotangent": centred(key_list[17], (TOKENS, D), 1.0, 6.0, ((0, 32),)),
    }


@jax.custom_vjp
def low(v):
    return lax.optimization_barrier(v.astype(jnp.bfloat16)).astype(jnp.float32)

@jax.custom_vjp
def low_back(v):
    return v

def low_keep(v):
    return (low(v), None)

def low_pass(kept, grad):
    return (grad,)

def back_keep(v):
    return (v, None)

def back_low(kept, grad):
    return (low(grad),)
low.defvjp(low_keep, low_pass)
low_back.defvjp(back_keep, back_low)
norm_eps = 1e-05
rope_base = 10000.0

def matmul(left, right):
    return jnp.dot(left, right, precision=lax.Precision.HIGHEST)

def rmsnorm(value, gain):
    factor = lax.rsqrt(lax.optimization_barrier(jnp.mean(value * value, axis=-1, keepdims=True)) + norm_eps)
    return value * factor * gain

def rotate(value, position, head_size):
    half = head_size // 2
    heads = value.shape[1] // head_size
    freqs = rope_base ** (-(jnp.arange(half, dtype=jnp.float32) * 2.0) / head_size)
    angles = position.astype(jnp.float32)[:, None] * freqs[None, :]
    cosine = jnp.cos(angles)[:, None, :]
    sine_part = jnp.sin(angles)[:, None, :]
    shaped = value.reshape(value.shape[0], heads, head_size)
    former = shaped[:, :, :half]
    latter = shaped[:, :, half:]
    turned = jnp.concatenate([former * cosine - latter * sine_part, latter * cosine + former * sine_part], axis=-1)
    return turned.reshape(value.shape)

def stream_layout(seq_lengths, stream_index):
    ends = jnp.cumsum(seq_lengths).astype(jnp.int32)
    starts = (ends - seq_lengths).astype(jnp.int32)
    passed = (stream_index[:, None] >= ends[None, :]).astype(jnp.int32)
    sequence = lax.optimization_barrier(jnp.sum(passed, axis=1)).astype(jnp.int32)
    owner = sequence[:, None] == jnp.arange(seq_lengths.shape[0], dtype=jnp.int32)[None, :]
    opening = lax.optimization_barrier(jnp.sum(jnp.where(owner, starts[None, :], 0), axis=1)).astype(jnp.int32)
    return (sequence, (stream_index - opening).astype(jnp.int32))

def slot_ranks(routes, ordering, experts):
    flat_routes = routes.reshape(-1)
    flat_order = ordering.reshape(-1)
    onehot = (flat_routes[:, None] == jnp.arange(experts, dtype=jnp.int32)[None, :]).astype(jnp.int32)
    arranged = jnp.zeros_like(onehot).at[flat_order].set(onehot)
    before = jnp.cumsum(arranged, axis=0) - arranged
    ranking = lax.optimization_barrier(jnp.sum(before[flat_order] * onehot, axis=1))
    return ranking.reshape(routes.shape).astype(jnp.int32)

def attend(query, keys, values, sequence):
    block = math.gcd(TOKENS, 512)
    window = min(LONGEST + block, TOKENS)
    factor = 1.0 / math.sqrt(HDIM)

    def one_block(start):
        key_start = jnp.clip(start - LONGEST, 0, TOKENS - window).astype(jnp.int32)
        query_block = lax.dynamic_slice_in_dim(query, start, block, 0).reshape(block, HEADS, HDIM)
        key_block = lax.dynamic_slice_in_dim(keys, key_start, window, 0).reshape(window, HEADS, HDIM)
        value_block = lax.dynamic_slice_in_dim(values, key_start, window, 0).reshape(window, HEADS, HDIM)
        query_seq = lax.dynamic_slice_in_dim(sequence, start, block, 0)
        key_seq = lax.dynamic_slice_in_dim(sequence, key_start, window, 0)
        query_at = start + jnp.arange(block, dtype=jnp.int32)
        key_at = key_start + jnp.arange(window, dtype=jnp.int32)
        scores = low_back(jnp.einsum('qhd,khd->hqk', query_block, key_block, precision=lax.Precision.HIGHEST) * factor)
        allowed = (query_seq[:, None] == key_seq[None, :]) & (key_at[None, :] <= query_at[:, None])
        expo = jnp.where(allowed[None], jnp.exp(scores), 0.0)
        totals = lax.optimization_barrier(jnp.sum(expo, axis=-1))
        summed = low_back(jnp.einsum('hqk,khd->qhd', low(expo), value_block, precision=lax.Precision.HIGHEST))
        return (summed / jnp.transpose(totals)[:, :, None]).reshape(block, D)
    starts = jnp.arange(TOKENS // block, dtype=jnp.int32) * block
    return lax.map(jax.checkpoint(one_block), starts).reshape(TOKENS, D)

def run_experts(routed, gate_float, up_float, down_float, slot_rows, slot_live):

    def one_expert(operands):
        expert_rows, expert_live, gate_matrix, up_matrix, down_matrix = operands
        incoming = low_back(routed[expert_rows] * expert_live[:, None])
        gate = low_back(matmul(incoming, gate_matrix))
        upward = low_back(matmul(incoming, up_matrix))
        active = low(jax.nn.silu(gate) * upward)
        return low(low_back(matmul(active, down_matrix)))
    return lax.map(jax.checkpoint(one_expert), (slot_rows, slot_live, gate_float, up_float, down_float))

def block_ranks(routes, ordering):
    return slot_ranks(routes, ordering, E)

def reference(tokens, query_weight, key_weight, value_weight, output_weight, mixing_gain, query_gain, key_gain, routing_gain, router_weight, gate_weight, up_weight, down_weight, seq_lengths, dealt_order, expert_routes, slot_order, cotangent):
    stream = jnp.arange(TOKENS, dtype=jnp.int32)
    sequence, position = stream_layout(seq_lengths, stream)
    dealt_position = position[dealt_order]
    inverse = jnp.zeros((TOKENS,), jnp.int32).at[dealt_order].set(stream)
    blocks = TOKENS // TOK_DEV
    ranking = jax.vmap(block_ranks)(expert_routes.reshape(blocks, TOK_DEV, TOP), slot_order.reshape(blocks, TOK_DEV, TOP)).reshape(TOKENS, TOP)
    is_kept = ranking < CAP_SRC
    per_expert = blocks * CAP_SRC
    block_of = (stream // TOK_DEV)[:, None]
    slot_index = jnp.where(is_kept, expert_routes * per_expert + block_of * CAP_SRC + ranking, E * per_expert).astype(jnp.int32)
    row_of = jnp.broadcast_to(stream[:, None], (TOKENS, TOP))
    slot_rows = jnp.zeros((E * per_expert,), jnp.int32).at[slot_index.reshape(-1)].set(row_of.reshape(-1), mode='drop').reshape(E, per_expert)
    slot_live = jnp.zeros((E * per_expert,), jnp.float32).at[slot_index.reshape(-1)].set(1.0, mode='drop').reshape(E, per_expert)

    def forward(tokens_float, query_float, key_float, value_float, output_float, mixing_float, qnorm_float, knorm_float, routing_float, router_float, gate_float, up_float, down_float):
        normed = low(rmsnorm(tokens_float, mixing_float))
        query = low(low_back(rotate(rmsnorm(low_back(matmul(normed, query_float)), qnorm_float), dealt_position, HDIM)))
        keys = low(low_back(rotate(rmsnorm(low_back(matmul(normed, key_float)), knorm_float), dealt_position, HDIM)))
        values = low(low_back(matmul(normed, value_float)))
        attended = attend(query[inverse], keys[inverse], values[inverse], sequence)[dealt_order]
        context = low(low_back(attended))
        middle = tokens_float + low_back(matmul(context, output_float))
        routed = low(rmsnorm(middle, routing_float))
        probs = jax.nn.softmax(low_back(matmul(routed, router_float)), axis=-1)
        weights = jnp.take_along_axis(probs, expert_routes, axis=1)
        outputs = run_experts(routed, gate_float, up_float, down_float, slot_rows, slot_live).reshape(E * per_expert, D)
        combined = jnp.zeros_like(middle)
        for pick in range(TOP):
            picked = jnp.take(outputs, slot_index[:, pick], axis=0, mode='fill', fill_value=0.0)
            combined = combined + weights[:, pick:pick + 1] * picked
        return middle + combined
    floats = tuple((item.astype(jnp.float32) for item in (tokens, query_weight, key_weight, value_weight, output_weight, mixing_gain, query_gain, key_gain, routing_gain, router_weight, gate_weight, up_weight, down_weight)))
    result, pullback = jax.vjp(forward, *floats)
    grads = pullback(cotangent.astype(jnp.float32))
    return (result.astype(jnp.bfloat16), grads[0], grads[1], grads[2], grads[3], grads[4], grads[5], grads[6], grads[7], grads[8], grads[9], grads[10], grads[11], grads[12])
```

```python
from functools import partial
import math

import jax
import jax.numpy as jnp
from jax import lax
from jax.sharding import PartitionSpec as P

HDIM = 128


norm_eps = 1e-05
rope_base = 10000.0


def rms_factor(square_sum, width):
    return lax.rsqrt(square_sum / width + norm_eps)


def rope_tables(position, head_size):
    half = head_size // 2
    freqs = rope_base ** (-(jnp.arange(half, dtype=jnp.float32) * 2.0) / head_size)
    angles = position.astype(jnp.float32)[:, None] * freqs[None, :]
    return (jnp.cos(angles)[:, None, :], jnp.sin(angles)[:, None, :])


def rotate(value, cosine, sine_part):
    half = cosine.shape[-1]
    shaped = value.reshape(value.shape[0], -1, 2 * half)
    former = shaped[:, :, :half]
    latter = shaped[:, :, half:]
    turned = jnp.concatenate(
        [former * cosine - latter * sine_part, latter * cosine + former * sine_part], axis=-1
    )
    return turned.reshape(value.shape)


def slot_codes(routes, ordering, experts, capacity):
    expert_ids = jnp.arange(experts, dtype=jnp.int32)
    absent = jnp.int32(1 << 30)
    chosen = routes[:, :, None] == expert_ids[None, None, :]
    order = jnp.min(jnp.where(chosen, ordering[:, :, None], absent), axis=1)
    rank = jnp.sum((order[None, :, :] < order[:, None, :]).astype(jnp.int32), axis=1)
    return jnp.where((order < absent) & (rank < capacity), rank, -1)


def stream_layout(seq_lengths, stream_index):
    ends = jnp.cumsum(seq_lengths)
    starts = ends - seq_lengths
    passed = (stream_index[:, None] >= ends[None, :]).astype(jnp.int32)
    sequence = jnp.sum(passed, axis=1)
    owner = sequence[:, None] == jnp.arange(seq_lengths.shape[0], dtype=jnp.int32)[None, :]
    opening = jnp.sum(jnp.where(owner, starts[None, :], 0), axis=1)
    return (sequence, stream_index - opening)


def scores_of(queries, keys, head_size):
    heads = queries.shape[1] // head_size
    query_heads = queries.reshape(queries.shape[0], heads, head_size)
    key_heads = keys.reshape(keys.shape[0], heads, head_size)
    return jnp.einsum(
        "qhd,khd->hqk", query_heads, key_heads, preferred_element_type=jnp.float32
    ) * (1.0 / math.sqrt(head_size))


def allowed_pairs(query_index, query_seq, key_index, key_seq):
    return (query_seq[:, None] == key_seq[None, :]) & (key_index[None, :] <= query_index[:, None])


def any_allowed(query_index, query_seq, key_index, key_seq):
    early = jnp.min(key_index) <= jnp.max(query_index)
    above = jnp.max(key_seq) >= jnp.min(query_seq)
    below = jnp.min(key_seq) <= jnp.max(query_seq)
    return early & above & below


def pair_forward(head_size, operands):
    queries, keys, values, query_index, query_seq, key_index, key_seq = operands
    scores = scores_of(queries, keys, head_size)
    allowed = allowed_pairs(query_index, query_seq, key_index, key_seq)
    expo = jnp.where(allowed[None], jnp.exp(scores), 0.0)
    heads = scores.shape[0]
    value_heads = values.reshape(values.shape[0], heads, head_size)
    summed = jnp.einsum(
        "hqk,khd->qhd", expo.astype(jnp.bfloat16), value_heads, preferred_element_type=jnp.float32
    )
    return (summed.reshape(queries.shape[0], queries.shape[1]), jnp.sum(expo, axis=-1))


def pair_forward_skip(head_size, operands):
    queries = operands[0]
    heads = queries.shape[1] // head_size
    return (
        jnp.zeros(queries.shape, jnp.float32),
        jnp.zeros((heads, queries.shape[0]), jnp.float32),
    )


def pair_backward(head_size, operands):
    queries, keys, values, scaled_grad, correction, query_index, query_seq, key_index, key_seq = (
        operands
    )
    scores = scores_of(queries, keys, head_size)
    allowed = allowed_pairs(query_index, query_seq, key_index, key_seq)
    expo = jnp.where(allowed[None], jnp.exp(scores), 0.0)
    heads = scores.shape[0]
    query_count = queries.shape[0]
    key_count = keys.shape[0]
    query_heads = queries.reshape(query_count, heads, head_size)
    key_heads = keys.reshape(key_count, heads, head_size)
    value_heads = values.reshape(key_count, heads, head_size)
    grad_heads = scaled_grad.reshape(query_count, heads, head_size)
    prob_grad = jnp.einsum(
        "qhd,khd->hqk", grad_heads, value_heads, preferred_element_type=jnp.float32
    )
    score_grad = (expo * (prob_grad - correction[:, :, None])).astype(jnp.bfloat16)
    factor = 1.0 / math.sqrt(head_size)
    query_part = (
        jnp.einsum("hqk,khd->qhd", score_grad, key_heads, preferred_element_type=jnp.float32)
        * factor
    )
    key_part = (
        jnp.einsum("hqk,qhd->khd", score_grad, query_heads, preferred_element_type=jnp.float32)
        * factor
    )
    value_part = jnp.einsum(
        "hqk,qhd->khd", expo.astype(jnp.bfloat16), grad_heads, preferred_element_type=jnp.float32
    )
    return (
        query_part.reshape(queries.shape),
        key_part.reshape(keys.shape),
        value_part.reshape(keys.shape),
    )


def pair_backward_skip(head_size, operands):
    queries = operands[0]
    keys = operands[1]
    return (
        jnp.zeros(queries.shape, jnp.float32),
        jnp.zeros(keys.shape, jnp.float32),
        jnp.zeros(keys.shape, jnp.float32),
    )


def attend_forward(queries, keys, values, query_index, query_seq, key_index, key_seq, head_size):
    rows, columns = queries.shape
    heads = columns // head_size
    half_rows = rows // 2
    groups = keys.shape[0] // rows
    query_blocks = queries.reshape(2, half_rows, columns)
    query_marks = query_index.reshape(2, half_rows)
    query_seqs = query_seq.reshape(2, half_rows)
    key_stack = (
        keys.reshape(groups, 2, half_rows, columns),
        values.reshape(groups, 2, half_rows, columns),
        key_index.reshape(groups, 2, half_rows),
        key_seq.reshape(groups, 2, half_rows),
    )

    def visit(carry, group):
        sums, totals = carry
        group_keys, group_values, group_index, group_seq = group
        sum_list = []
        total_list = []
        for query_part in range(2):
            running = sums[query_part]
            counted = totals[query_part]
            for key_part in range(2):
                operands = (
                    query_blocks[query_part],
                    group_keys[key_part],
                    group_values[key_part],
                    query_marks[query_part],
                    query_seqs[query_part],
                    group_index[key_part],
                    group_seq[key_part],
                )
                living = any_allowed(
                    query_marks[query_part],
                    query_seqs[query_part],
                    group_index[key_part],
                    group_seq[key_part],
                )
                add_sum, add_total = lax.cond(
                    living,
                    partial(pair_forward, head_size),
                    partial(pair_forward_skip, head_size),
                    operands,
                )
                running = running + add_sum
                counted = counted + add_total
            sum_list.append(running)
            total_list.append(counted)
        return ((jnp.stack(sum_list), jnp.stack(total_list)), None)

    initial = (
        jnp.zeros((2, half_rows, columns), jnp.float32),
        jnp.zeros((2, heads, half_rows), jnp.float32),
    )
    (sums, totals), unused = lax.scan(visit, initial, key_stack)
    totals_rows = jnp.transpose(totals, (1, 0, 2)).reshape(heads, rows)
    attended = sums.reshape(rows, heads, head_size) / jnp.transpose(totals_rows)[:, :, None]
    return (attended.reshape(rows, columns), totals_rows)


def attend_backward(
    queries,
    keys,
    values,
    scaled_grad,
    correction,
    query_index,
    query_seq,
    key_index,
    key_seq,
    head_size,
):
    rows, columns = queries.shape
    heads = columns // head_size
    half_rows = rows // 2
    groups = keys.shape[0] // rows
    query_blocks = queries.reshape(2, half_rows, columns)
    scaled_blocks = scaled_grad.reshape(2, half_rows, columns)
    correction_blocks = jnp.transpose(correction.reshape(heads, 2, half_rows), (1, 0, 2))
    query_marks = query_index.reshape(2, half_rows)
    query_seqs = query_seq.reshape(2, half_rows)
    key_stack = (
        keys.reshape(groups, 2, half_rows, columns),
        values.reshape(groups, 2, half_rows, columns),
        key_index.reshape(groups, 2, half_rows),
        key_seq.reshape(groups, 2, half_rows),
    )

    def visit(carry, group):
        group_keys, group_values, group_index, group_seq = group
        key_list = [
            jnp.zeros((half_rows, columns), jnp.float32),
            jnp.zeros((half_rows, columns), jnp.float32),
        ]
        value_list = [
            jnp.zeros((half_rows, columns), jnp.float32),
            jnp.zeros((half_rows, columns), jnp.float32),
        ]
        query_list = []
        for query_part in range(2):
            running = carry[query_part]
            for key_part in range(2):
                operands = (
                    query_blocks[query_part],
                    group_keys[key_part],
                    group_values[key_part],
                    scaled_blocks[query_part],
                    correction_blocks[query_part],
                    query_marks[query_part],
                    query_seqs[query_part],
                    group_index[key_part],
                    group_seq[key_part],
                )
                living = any_allowed(
                    query_marks[query_part],
                    query_seqs[query_part],
                    group_index[key_part],
                    group_seq[key_part],
                )
                add_query, add_key, add_value = lax.cond(
                    living,
                    partial(pair_backward, head_size),
                    partial(pair_backward_skip, head_size),
                    operands,
                )
                running = running + add_query
                key_list[key_part] = key_list[key_part] + add_key
                value_list[key_part] = value_list[key_part] + add_value
            query_list.append(running)
        return (jnp.stack(query_list), (jnp.stack(key_list), jnp.stack(value_list)))

    query_grad, (key_grads, value_grads) = lax.scan(
        visit, jnp.zeros((2, half_rows, columns), jnp.float32), key_stack
    )
    return (
        query_grad.reshape(rows, columns),
        key_grads.reshape(groups * rows, columns),
        value_grads.reshape(groups * rows, columns),
    )


def on_device(
    tokens,
    query_weight,
    key_weight,
    value_weight,
    output_weight,
    mixing_gain,
    query_gain,
    key_gain,
    routing_gain,
    router_weight,
    gate_weight,
    up_weight,
    down_weight,
    seq_lengths,
    dealt_order,
    expert_routes,
    slot_order,
    cotangent,
):
    heads_axis = lax.axis_size("head")
    blocks = lax.axis_size("blk")
    head_at = lax.axis_index("head")
    block_at = lax.axis_index("blk")
    rows, width = tokens.shape
    picks = expert_routes.shape[1]
    total_rows = dealt_order.shape[0]
    group = rows * heads_axis
    columns = width // heads_axis
    part = query_weight.shape[0]
    head_size = HDIM
    heads_here = columns // head_size
    f32 = jnp.float32
    bf16 = jnp.bfloat16
    experts = router_weight.shape[1]
    local_experts = gate_weight.shape[0]
    capacity = 5 * rows * picks // (4 * experts)

    small = jnp.concatenate(
        [
            mixing_gain[:, None],
            query_gain[:, None],
            key_gain[:, None],
            routing_gain[:, None],
            router_weight,
        ],
        axis=1,
    ).reshape(1, -1)
    small_all = lax.all_gather(small, ("head", "blk"), axis=0, tiled=True).reshape(
        width, 4 + experts
    )
    mixing_scale = small_all[:, 0].astype(f32)
    routing_scale = small_all[:, 3].astype(f32)
    query_scale = lax.dynamic_slice_in_dim(small_all[:, 1], head_at * columns, columns).astype(f32)
    key_scale = lax.dynamic_slice_in_dim(small_all[:, 2], head_at * columns, columns).astype(f32)
    router_full = small_all[:, 4:]
    codes = slot_codes(expert_routes, slot_order, experts, capacity)
    codes_all = lax.all_gather(codes, "blk", axis=0, tiled=True).reshape(blocks, rows, experts)
    codes_here = lax.dynamic_slice_in_dim(codes_all, block_at * local_experts, local_experts, 2)

    key_index = jnp.transpose(
        dealt_order.reshape(heads_axis, blocks, rows), (1, 0, 2)
    ).reshape(total_rows)
    key_seq = stream_layout(seq_lengths, key_index)[0]
    query_index = lax.dynamic_slice_in_dim(key_index, block_at * group, group)
    query_seq, query_position = stream_layout(seq_lengths, query_index)
    cosine, sine_part = rope_tables(query_position, head_size)

    tokens_group = lax.all_gather(tokens, "head", axis=0, tiled=True).astype(f32)
    stacked = jnp.stack([query_weight, key_weight, value_weight])
    turned = lax.all_to_all(stacked, "head", split_axis=2, concat_axis=1, tiled=True)
    gathered = lax.all_gather(turned, "blk", axis=1, tiled=False)
    gathered = jnp.transpose(
        gathered.reshape(3, blocks, heads_axis, part, columns), (0, 2, 1, 3, 4)
    ).reshape(3, width, columns)
    output_rows = lax.all_gather(output_weight, "blk", axis=0, tiled=True)
    cot_all = lax.all_gather(cotangent, "blk", axis=0, tiled=True).reshape(blocks, rows, width)
    token_factor = rms_factor(jnp.sum(tokens_group * tokens_group, axis=-1, keepdims=True), width)
    normed = (tokens_group * token_factor * mixing_scale).astype(bf16)
    query_raw = jnp.dot(normed, gathered[0], preferred_element_type=f32)
    key_raw = jnp.dot(normed, gathered[1], preferred_element_type=f32)
    value_heads = jnp.dot(normed, gathered[2], preferred_element_type=f32).astype(bf16)
    squares = lax.psum(
        jnp.stack([jnp.sum(query_raw * query_raw, axis=-1), jnp.sum(key_raw * key_raw, axis=-1)]),
        "head",
    )
    query_factor = rms_factor(squares[0][:, None], width)
    key_factor = rms_factor(squares[1][:, None], width)
    query_heads = rotate(query_raw * query_factor * query_scale, cosine, sine_part).astype(bf16)
    key_heads = rotate(key_raw * key_factor * key_scale, cosine, sine_part).astype(bf16)
    keys_all = lax.all_gather(key_heads, "blk", axis=0, tiled=True)
    values_all = lax.all_gather(value_heads, "blk", axis=0, tiled=True)
    attended, totals = attend_forward(
        query_heads, keys_all, values_all, query_index, query_seq, key_index, key_seq, head_size
    )
    context = attended.astype(bf16)
    branch = jnp.dot(context, output_rows, preferred_element_type=f32).astype(bf16)
    branch_parts = lax.all_to_all(
        branch.reshape(heads_axis, rows, width), "head", split_axis=0, concat_axis=0, tiled=True
    )
    own_tokens = tokens.astype(f32)
    middle = own_tokens + jnp.sum(branch_parts.astype(f32), axis=0)
    middle_factor = rms_factor(jnp.sum(middle * middle, axis=-1, keepdims=True), width)
    routed = (middle * middle_factor * routing_scale).astype(bf16)
    probs = jax.nn.softmax(jnp.dot(routed, router_full, preferred_element_type=f32), axis=-1)

    routed_all = lax.all_gather(routed, "blk", axis=0, tiled=True)
    probs_all = jax.nn.softmax(
        jnp.dot(routed_all, router_full, preferred_element_type=f32), axis=-1
    )
    weight_here = lax.dynamic_slice_in_dim(
        probs_all, block_at * local_experts, local_experts, 1
    ).reshape(blocks, rows, local_experts)
    routed_all = routed_all.reshape(blocks, rows, width)
    slot_ids = jnp.arange(capacity, dtype=jnp.int32)
    placed = (
        jnp.transpose(codes_here, (2, 0, 1))[:, :, None, :] == slot_ids[None, None, :, None]
    )
    place = placed.astype(bf16)
    slot_weight = jnp.sum(
        jnp.where(placed, jnp.transpose(weight_here, (2, 0, 1))[:, :, None, :], 0.0), axis=-1
    )
    slots = blocks * capacity
    arrived = jnp.einsum("lsrt,std->lsrd", place, routed_all).reshape(local_experts, slots, width)
    arrived_cot = jnp.einsum("lsrt,std->lsrd", place, cot_all).reshape(local_experts, slots, width)
    slot_weight = slot_weight.reshape(local_experts, slots, 1)
    gate_all = lax.all_gather(gate_weight, "head", axis=1, tiled=True)
    up_all = lax.all_gather(up_weight, "head", axis=1, tiled=True)
    down_all = lax.all_gather(down_weight, "head", axis=1, tiled=True)
    gate = jnp.einsum("esd,edf->esf", arrived, gate_all, preferred_element_type=f32)
    upward = jnp.einsum("esd,edf->esf", arrived, up_all, preferred_element_type=f32)
    sigmoid = jax.nn.sigmoid(gate)
    active = (gate * sigmoid * upward).astype(bf16)
    produced = jnp.einsum("esf,efd->esd", active, down_all, preferred_element_type=f32).astype(bf16)
    cot_float = arrived_cot.astype(f32)
    produced_float = produced.astype(f32)
    weighted = (slot_weight * produced_float).astype(bf16).reshape(
        local_experts, blocks, capacity, width
    )
    combined = jnp.einsum("lsrt,lsrd->std", place, weighted, preferred_element_type=f32)
    combined = lax.psum_scatter(
        combined.astype(bf16).reshape(blocks * rows, width), "blk", scatter_dimension=0, tiled=True
    )
    block_output = (middle + combined.astype(f32)).astype(bf16)
    slot_grad = jnp.sum(cot_float * produced_float, axis=-1).reshape(
        local_experts, blocks, capacity, 1
    )
    weight_grad = jnp.transpose(
        jnp.sum(jnp.where(placed, slot_grad, 0.0), axis=2), (1, 2, 0)
    )
    prob_grad = lax.all_to_all(weight_grad, "blk", split_axis=0, concat_axis=2, tiled=True).reshape(
        rows, experts
    )
    produced_grad = (slot_weight * cot_float).astype(bf16)
    active_grad = jnp.einsum("esd,efd->esf", produced_grad, down_all, preferred_element_type=f32)
    gate_grad = (active_grad * upward * sigmoid * (1.0 + gate * (1.0 - sigmoid))).astype(bf16)
    up_grad = (active_grad * (gate * sigmoid)).astype(bf16)
    incoming = jnp.einsum("esf,edf->esd", gate_grad, gate_all, preferred_element_type=f32)
    incoming = incoming + jnp.einsum("esf,edf->esd", up_grad, up_all, preferred_element_type=f32)
    incoming = incoming.astype(bf16).reshape(local_experts, blocks, capacity, width)
    incoming = jnp.einsum("lsrt,lsrd->std", place, incoming, preferred_element_type=f32)
    routed_grad = lax.psum_scatter(
        incoming.astype(bf16).reshape(blocks * rows, width), "blk", scatter_dimension=0, tiled=True
    ).astype(f32)
    down_sum = jnp.einsum("esf,esd->efd", active, produced_grad, preferred_element_type=f32)
    gate_sum = jnp.einsum("esd,esf->edf", arrived, gate_grad, preferred_element_type=f32)
    up_sum = jnp.einsum("esd,esf->edf", arrived, up_grad, preferred_element_type=f32)
    gate_out, up_out, down_out = (
        lax.psum_scatter(item.astype(bf16), "head", scatter_dimension=1, tiled=True).astype(f32)
        for item in (gate_sum, up_sum, down_sum)
    )

    logit_grad = (
        probs * (prob_grad - jnp.sum(probs * prob_grad, axis=1, keepdims=True))
    ).astype(bf16)
    router_sum = jnp.dot(routed.T, logit_grad, preferred_element_type=f32)
    routed_grad = routed_grad + jnp.dot(logit_grad, router_full.T, preferred_element_type=f32)
    scaled = routed_grad * routing_scale
    inner = jnp.mean(scaled * middle, axis=-1, keepdims=True)
    middle_grad = (
        cotangent.astype(f32) + middle_factor * scaled - middle * (middle_factor**3 * inner)
    )
    routing_sum = jnp.sum(routed_grad * middle * middle_factor, axis=0)

    branch_grad = lax.all_gather(middle_grad.astype(bf16), "head", axis=0, tiled=True)
    context_grad = jnp.dot(branch_grad, output_rows.T, preferred_element_type=f32).astype(bf16)
    output_sum = jnp.dot(context.T, branch_grad, preferred_element_type=f32).astype(bf16)
    output_out = lax.psum_scatter(output_sum, "blk", scatter_dimension=0, tiled=True).astype(f32)
    context_float = context_grad.astype(f32).reshape(group, heads_here, head_size)
    scaled_grad = (
        (context_float / jnp.transpose(totals)[:, :, None]).astype(bf16).reshape(group, columns)
    )
    correction = (
        jnp.transpose(
            jnp.sum(context_float * attended.reshape(group, heads_here, head_size), axis=2)
        )
        / totals
    )
    query_grad_heads, key_grad_all, value_grad_all = attend_backward(
        query_heads,
        keys_all,
        values_all,
        scaled_grad,
        correction,
        query_index,
        query_seq,
        key_index,
        key_seq,
        head_size,
    )
    key_back = lax.psum_scatter(key_grad_all.astype(bf16), "blk", scatter_dimension=0, tiled=True)
    value_back = lax.psum_scatter(
        value_grad_all.astype(bf16), "blk", scatter_dimension=0, tiled=True
    )
    query_turn = rotate(query_grad_heads.astype(bf16).astype(f32), cosine, -sine_part)
    key_turn = rotate(key_back.astype(f32), cosine, -sine_part)
    query_scaled = query_turn * query_scale
    key_scaled = key_turn * key_scale
    inners = (
        lax.psum(
            jnp.stack(
                [jnp.sum(query_scaled * query_raw, axis=-1), jnp.sum(key_scaled * key_raw, axis=-1)]
            ),
            "head",
        )
        / width
    )
    query_raw_grad = (
        query_factor * query_scaled - query_raw * (query_factor**3 * inners[0][:, None])
    ).astype(bf16)
    key_raw_grad = (
        key_factor * key_scaled - key_raw * (key_factor**3 * inners[1][:, None])
    ).astype(bf16)
    querynorm_sum = jnp.sum(query_turn * query_raw * query_factor, axis=0)
    keynorm_sum = jnp.sum(key_turn * key_raw * key_factor, axis=0)
    normed_part = jnp.dot(query_raw_grad, gathered[0].T, preferred_element_type=f32)
    normed_part = normed_part + jnp.dot(key_raw_grad, gathered[1].T, preferred_element_type=f32)
    normed_part = normed_part + jnp.dot(value_back, gathered[2].T, preferred_element_type=f32)
    normed_parts = lax.all_to_all(
        normed_part.astype(bf16).reshape(heads_axis, rows, width),
        "head",
        split_axis=0,
        concat_axis=0,
        tiled=True,
    )
    normed_grad = jnp.sum(normed_parts.astype(f32), axis=0)
    own_factor = rms_factor(jnp.sum(own_tokens * own_tokens, axis=-1, keepdims=True), width)
    scaled = normed_grad * mixing_scale
    inner = jnp.mean(scaled * own_tokens, axis=-1, keepdims=True)
    tokens_grad = middle_grad + own_factor * scaled - own_tokens * (own_factor**3 * inner)
    mixing_sum = jnp.sum(normed_grad * own_tokens * own_factor, axis=0)
    raw_grads = jnp.stack([query_raw_grad, key_raw_grad, value_back])
    weight_sums = jnp.einsum("td,ntc->ndc", normed, raw_grads, preferred_element_type=f32).astype(
        bf16
    )
    weight_sums = jnp.transpose(
        weight_sums.reshape(3, heads_axis, blocks, part, columns), (2, 0, 1, 3, 4)
    ).reshape(blocks * 3 * heads_axis * part, columns)
    weight_sums = lax.psum_scatter(weight_sums, "blk", scatter_dimension=0, tiled=True)
    weight_sums = lax.all_to_all(
        weight_sums.reshape(3, heads_axis * part, columns),
        "head",
        split_axis=1,
        concat_axis=2,
        tiled=True,
    ).astype(f32)
    blank = jnp.zeros((heads_axis, columns), f32)
    query_line = lax.dynamic_update_slice(blank, querynorm_sum[None], (head_at, 0)).reshape(width)
    key_line = lax.dynamic_update_slice(blank, keynorm_sum[None], (head_at, 0)).reshape(width)
    lines = jnp.concatenate(
        [
            mixing_sum[:, None],
            query_line[:, None],
            key_line[:, None],
            routing_sum[:, None],
            router_sum,
        ],
        axis=1,
    )
    lines = jnp.pad(
        lines.reshape(heads_axis * blocks, -1), ((0, 0), (0, -part * (4 + experts) % 1024))
    ).reshape(-1, 128)
    lines = lax.psum_scatter(lines, ("head", "blk"), scatter_dimension=0, tiled=True).reshape(
        -1
    )[: part * (4 + experts)].reshape(part, 4 + experts)
    return (
        block_output,
        tokens_grad,
        weight_sums[0],
        weight_sums[1],
        weight_sums[2],
        output_out,
        lines[:, 0],
        lines[:, 1],
        lines[:, 2],
        lines[:, 3],
        lines[:, 4:],
        gate_out,
        up_out,
        down_out,
    )


def solution(mesh):
    in_specs = (
        P(("head", "blk"), None),
        P(("head", "blk"), None),
        P(("head", "blk"), None),
        P(("head", "blk"), None),
        P(("head", "blk"), None),
        P(("head", "blk")),
        P(("head", "blk")),
        P(("head", "blk")),
        P(("head", "blk")),
        P(("head", "blk"), None),
        P("blk", "head", None),
        P("blk", "head", None),
        P("blk", "head", None),
        P(),
        P(),
        P(("head", "blk"), None),
        P(("head", "blk"), None),
        P(("head", "blk"), None),
    )
    out_specs = (
        P(("head", "blk"), None),
        P(("head", "blk"), None),
        P(("head", "blk"), None),
        P(("head", "blk"), None),
        P(("head", "blk"), None),
        P(("head", "blk"), None),
        P(("head", "blk")),
        P(("head", "blk")),
        P(("head", "blk")),
        P(("head", "blk")),
        P(("head", "blk"), None),
        P("blk", "head", None),
        P("blk", "head", None),
        P("blk", "head", None),
    )
    return jax.shard_map(
        on_device, mesh=mesh, in_specs=in_specs, out_specs=out_specs, check_vma=False
    )
```

```python
from functools import partial
import math

import jax
import jax.numpy as jnp
from jax import lax
from jax.experimental import pallas as pl
from jax.experimental.pallas import tpu as pltpu
from jax.sharding import PartitionSpec as P

HDIM = 128
LOG2E = 1.4426950408889634
TILE = 256


norm_eps = 1e-05
rope_base = 10000.0


def rms_factor(square_sum, width):
    return lax.rsqrt(square_sum / width + norm_eps)


def rope_tables(position, head_size):
    half = head_size // 2
    freqs = rope_base ** (-(jnp.arange(half, dtype=jnp.float32) * 2.0) / head_size)
    angles = position.astype(jnp.float32)[:, None] * freqs[None, :]
    return (jnp.cos(angles)[:, None, :], jnp.sin(angles)[:, None, :])


def rotate(value, cosine, sine_part):
    half = cosine.shape[-1]
    shaped = value.reshape(value.shape[0], -1, 2 * half)
    former = shaped[:, :, :half]
    latter = shaped[:, :, half:]
    turned = jnp.concatenate(
        [former * cosine - latter * sine_part, latter * cosine + former * sine_part], axis=-1
    )
    return turned.reshape(value.shape)


def slot_codes(routes, ordering, experts, capacity):
    expert_ids = jnp.arange(experts, dtype=jnp.int32)
    absent = jnp.int32(1 << 30)
    chosen = routes[:, :, None] == expert_ids[None, None, :]
    order = jnp.min(jnp.where(chosen, ordering[:, :, None], absent), axis=1)
    rank = jnp.sum((order[None, :, :] < order[:, None, :]).astype(jnp.int32), axis=1)
    return jnp.where((order < absent) & (rank < capacity), rank, -1)


def stream_layout(seq_lengths, stream_index):
    ends = jnp.cumsum(seq_lengths)
    starts = ends - seq_lengths
    passed = (stream_index[:, None] >= ends[None, :]).astype(jnp.int32)
    sequence = jnp.sum(passed, axis=1)
    owner = sequence[:, None] == jnp.arange(seq_lengths.shape[0], dtype=jnp.int32)[None, :]
    opening = jnp.sum(jnp.where(owner, starts[None, :], 0), axis=1)
    return (sequence, stream_index - opening)


def tile_lists(query_index, query_seq, key_index, key_seq, tile):
    query_tiles = query_index.shape[0] // tile
    key_tiles = key_index.shape[0] // tile
    query_marks = query_index.reshape(query_tiles, tile)
    query_seqs = query_seq.reshape(query_tiles, tile)
    key_marks = key_index.reshape(key_tiles, tile)
    key_seqs = key_seq.reshape(key_tiles, tile)
    early = jnp.min(key_marks, axis=1)[None, :] <= jnp.max(query_marks, axis=1)[:, None]
    above = jnp.max(key_seqs, axis=1)[None, :] >= jnp.min(query_seqs, axis=1)[:, None]
    below = jnp.min(key_seqs, axis=1)[None, :] <= jnp.max(query_seqs, axis=1)[:, None]
    live = (early & above & below).astype(jnp.int32)
    order = jnp.cumsum(live, axis=1) - 1
    numbers = jnp.arange(key_tiles, dtype=jnp.int32)
    hits = (order[:, :, None] == numbers[None, None, :]) & (live[:, :, None] > 0)
    listed = jnp.sum(jnp.where(hits, numbers[None, :, None], 0), axis=1)
    return (listed.astype(jnp.int32), jnp.sum(live, axis=1).astype(jnp.int32), live)


def spread(vector):
    return jnp.broadcast_to(vector[:, None], (vector.shape[0], 128))


def twice(value, count):
    return value if count == 1 else jnp.concatenate([value] * count, axis=1)


def forward_kernel(
    listed, counts, query, key, value, at, opening, key_at, attended, context, totals, total, acc, *, tile
):
    lanes = 128
    copies = tile // lanes
    factor = LOG2E / math.sqrt(HDIM)
    for step in range(query.shape[0] // tile):
        span = slice(step * tile, (step + 1) * tile)
        acc[...] = jnp.zeros_like(acc)
        total[...] = jnp.zeros_like(total)

        def visit(turn, carry):
            number = listed[step, turn]
            start = pl.multiple_of(number * tile, tile)
            scores = lax.dot_general(
                query[span, :],
                key[pl.ds(start, tile), :],
                (((1,), (1,)), ((), ())),
                preferred_element_type=jnp.float32,
            )
            marks = key_at[pl.ds(number, 1), :]
            allowed = (marks <= twice(at[span, :], copies)) & (
                marks >= twice(opening[span, :], copies)
            )
            expo = jnp.where(allowed, jnp.exp2(scores * factor), 0.0)
            partial_sum = expo[:, :lanes]
            for copy in range(1, copies):
                partial_sum = partial_sum + expo[:, copy * lanes : (copy + 1) * lanes]
            total[...] += partial_sum
            acc[...] += jnp.dot(
                expo.astype(jnp.bfloat16),
                value[pl.ds(start, tile), :],
                preferred_element_type=jnp.float32,
            )
            return carry

        lax.fori_loop(0, counts[step], visit, 0)
        full = jnp.sum(total[...], axis=1, keepdims=True)
        result = acc[...] / full
        attended[span, :] = result
        context[span, :] = result.astype(jnp.bfloat16)
        totals[span, :] = jnp.broadcast_to(full, (tile, lanes))


def attend_forward(queries, keys, values, marks, tables, tile):
    group, columns = queries.shape
    total_rows = keys.shape[0]
    listed, counts, unused = tables
    at, opening, key_at = marks[0], marks[1], marks[2]
    heads = columns // HDIM
    lane = lambda rows: pl.BlockSpec((rows, HDIM), lambda h, *refs: (0, h))
    fixed = lambda array: pl.BlockSpec(array.shape, lambda h, *refs: (0, 0))
    return pl.pallas_call(
        partial(forward_kernel, tile=tile),
        grid_spec=pltpu.PrefetchScalarGridSpec(
            num_scalar_prefetch=2,
            grid=(heads,),
            in_specs=[
                lane(group),
                lane(total_rows),
                lane(total_rows),
                fixed(at),
                fixed(opening),
                fixed(key_at),
            ],
            out_specs=[lane(group), lane(group), lane(group)],
            scratch_shapes=[
                pltpu.VMEM((tile, HDIM), jnp.float32),
                pltpu.VMEM((tile, HDIM), jnp.float32),
            ],
        ),
        out_shape=[
            jax.ShapeDtypeStruct((group, columns), jnp.float32),
            jax.ShapeDtypeStruct((group, columns), jnp.bfloat16),
            jax.ShapeDtypeStruct((group, columns), jnp.float32),
        ],
        name="attend_forward",
    )(listed, counts, queries, keys, values, at, opening, key_at)


def backward_kernel(
    live,
    query,
    key,
    value,
    grad,
    attended,
    totals,
    at_row,
    opening_row,
    key_col,
    query_out,
    key_out,
    value_out,
    scaled,
    offset,
    query_acc,
    key_acc,
    value_acc,
    *,
    tile,
):
    copies = tile // 128
    steps = query.shape[0] // tile
    factor = 1.0 / math.sqrt(HDIM)
    grads = grad[...].astype(jnp.float32)
    scaled[...] = (grads / totals[...]).astype(jnp.bfloat16)
    sums = jnp.sum(grads * attended[...], axis=1, keepdims=True) / totals[...]
    offset[...] = jnp.transpose(sums)[:8, :]
    query_acc[...] = jnp.zeros_like(query_acc)

    def visit(number, carry):
        start = pl.multiple_of(number * tile, tile)
        window = pl.ds(start, tile)
        key_acc[...] = jnp.zeros_like(key_acc)
        value_acc[...] = jnp.zeros_like(value_acc)
        for step in range(steps):
            span = slice(step * tile, (step + 1) * tile)

            @pl.when(live[step, number] > 0)
            def unused():
                scores = lax.dot_general(
                    key[window, :],
                    query[span, :],
                    (((1,), (1,)), ((), ())),
                    preferred_element_type=jnp.float32,
                )
                marks = twice(key_col[window, :], copies)
                allowed = (marks <= at_row[:, span]) & (marks >= opening_row[:, span])
                expo = jnp.where(allowed, jnp.exp2(scores * (factor * LOG2E)), 0.0)
                inner = lax.dot_general(
                    value[window, :],
                    scaled[span, :],
                    (((1,), (1,)), ((), ())),
                    preferred_element_type=jnp.float32,
                )
                back = (expo * (inner - offset[0:1, span])).astype(jnp.bfloat16)
                key_acc[...] += jnp.dot(back, query[span, :], preferred_element_type=jnp.float32)
                value_acc[...] += jnp.dot(
                    expo.astype(jnp.bfloat16), scaled[span, :], preferred_element_type=jnp.float32
                )
                query_acc[span, :] += lax.dot_general(
                    back,
                    key[window, :],
                    (((0,), (0,)), ((), ())),
                    preferred_element_type=jnp.float32,
                )

        key_out[window, :] = (key_acc[...] * factor).astype(jnp.bfloat16)
        value_out[window, :] = value_acc[...].astype(jnp.bfloat16)
        return carry

    lax.fori_loop(0, key.shape[0] // tile, visit, 0)
    query_out[...] = (query_acc[...] * factor).astype(jnp.bfloat16)


def attend_backward(queries, keys, values, grads, attended, totals, marks, tables, tile):
    group, columns = queries.shape
    total_rows = keys.shape[0]
    live = tables[2]
    at_row, opening_row, key_col = marks[3], marks[4], marks[5]
    heads = columns // HDIM
    lane = lambda rows: pl.BlockSpec((rows, HDIM), lambda h, *refs: (0, h))
    fixed = lambda array: pl.BlockSpec(array.shape, lambda h, *refs: (0, 0))
    return pl.pallas_call(
        partial(backward_kernel, tile=tile),
        grid_spec=pltpu.PrefetchScalarGridSpec(
            num_scalar_prefetch=1,
            grid=(heads,),
            in_specs=[
                lane(group),
                lane(total_rows),
                lane(total_rows),
                lane(group),
                lane(group),
                lane(group),
                fixed(at_row),
                fixed(opening_row),
                fixed(key_col),
            ],
            out_specs=[lane(group), lane(total_rows), lane(total_rows)],
            scratch_shapes=[
                pltpu.VMEM((group, HDIM), jnp.bfloat16),
                pltpu.VMEM((8, group), jnp.float32),
                pltpu.VMEM((group, HDIM), jnp.float32),
                pltpu.VMEM((tile, HDIM), jnp.float32),
                pltpu.VMEM((tile, HDIM), jnp.float32),
            ],
        ),
        out_shape=[
            jax.ShapeDtypeStruct((group, columns), jnp.bfloat16),
            jax.ShapeDtypeStruct((total_rows, columns), jnp.bfloat16),
            jax.ShapeDtypeStruct((total_rows, columns), jnp.bfloat16),
        ],
        name="attend_backward",
    )(live, queries, keys, values, grads, attended, totals, at_row, opening_row, key_col)


def attend_marks(query_index, query_start, key_index, tile):
    return (
        spread(query_index),
        spread(query_start),
        key_index.reshape(-1, tile),
        query_index[None, :],
        query_start[None, :],
        spread(key_index),
    )


def exchange(array, bit):
    count = lax.axis_size("head")
    return lax.ppermute(array, "head", [(at, at ^ bit) for at in range(count)])


def head_sum(array):
    total = array
    for other in range(1, lax.axis_size("head")):
        total = total + exchange(array, other)
    return total


def bit_order(turn):
    count = lax.axis_size("head").bit_length() - 1
    return [1 << ((turn + step) % count) for step in range(count)]


def gather_pieces(array, turn):
    pieces = {0: array}
    for bit in bit_order(turn):
        for offset in list(pieces):
            pieces[offset ^ bit] = exchange(pieces[offset], bit)
    return [pieces[offset] for offset in range(len(pieces))]


def scatter_pieces(pieces, turn):
    held = {offset: piece.astype(jnp.float32) for offset, piece in enumerate(pieces)}
    for bit in bit_order(turn):
        for offset in [item for item in held if item & bit]:
            arrived = exchange(held.pop(offset).astype(jnp.bfloat16), bit)
            held[offset ^ bit] = held[offset ^ bit] + arrived.astype(jnp.float32)
    return held[0]


def xor_chunks(array, axis):
    count = lax.axis_size("head")
    at = lax.axis_index("head")
    size = array.shape[axis] // count
    chunks = [
        lax.dynamic_slice_in_dim(array, (at ^ offset) * size, size, axis) for offset in range(count)
    ]
    return jnp.concatenate(chunks, axis=axis)


def on_device(
    tokens,
    query_weight,
    key_weight,
    value_weight,
    output_weight,
    mixing_gain,
    query_gain,
    key_gain,
    routing_gain,
    router_weight,
    gate_weight,
    up_weight,
    down_weight,
    seq_lengths,
    dealt_order,
    expert_routes,
    slot_order,
    cotangent,
):
    heads_axis = lax.axis_size("head")
    blocks = lax.axis_size("blk")
    head_at = lax.axis_index("head")
    block_at = lax.axis_index("blk")
    rows, width = tokens.shape
    picks = expert_routes.shape[1]
    total_rows = dealt_order.shape[0]
    group = rows * heads_axis
    columns = width // heads_axis
    part = query_weight.shape[0]
    head_size = HDIM
    heads_here = columns // head_size
    f32 = jnp.float32
    bf16 = jnp.bfloat16
    experts = router_weight.shape[1]
    local_experts = gate_weight.shape[0]
    capacity = 5 * rows * picks // (4 * experts)

    small = jnp.concatenate(
        [
            mixing_gain[:, None],
            query_gain[:, None],
            key_gain[:, None],
            routing_gain[:, None],
            router_weight,
        ],
        axis=1,
    ).reshape(1, -1)
    small_all = lax.all_gather(small, "blk", axis=0, tiled=True)
    small_all = lax.all_gather(small_all, "head", axis=0, tiled=True).reshape(width, 4 + experts)
    mixing_scale = small_all[:, 0].astype(f32)
    routing_scale = small_all[:, 3].astype(f32)
    query_scale = lax.dynamic_slice_in_dim(small_all[:, 1], head_at * columns, columns).astype(f32)
    key_scale = lax.dynamic_slice_in_dim(small_all[:, 2], head_at * columns, columns).astype(f32)
    router_full = small_all[:, 4:]
    codes = slot_codes(expert_routes, slot_order, experts, capacity)
    codes_all = lax.all_gather(codes, "blk", axis=0, tiled=True).reshape(blocks, rows, experts)
    codes_here = lax.dynamic_slice_in_dim(codes_all, block_at * local_experts, local_experts, 2)

    key_index = jnp.transpose(
        dealt_order.reshape(heads_axis, blocks, rows), (1, 0, 2)
    ).reshape(total_rows)
    key_seq = stream_layout(seq_lengths, key_index)[0]
    query_index = lax.dynamic_slice_in_dim(key_index, block_at * group, group)
    query_seq, query_position = stream_layout(seq_lengths, query_index)
    cosine, sine_part = rope_tables(query_position, head_size)
    tables = tile_lists(query_index, query_seq, key_index, key_seq, TILE)
    marks = attend_marks(query_index, query_index - query_position, key_index, TILE)

    tokens_group = lax.all_gather(tokens, "head", axis=0, tiled=True).astype(f32)
    stacked = jnp.stack([query_weight, key_weight, value_weight])
    turned = lax.all_to_all(stacked, "head", split_axis=2, concat_axis=1, tiled=True)
    gathered = lax.all_gather(turned, "blk", axis=1, tiled=False)
    gathered = jnp.transpose(
        gathered.reshape(3, blocks, heads_axis, part, columns), (0, 2, 1, 3, 4)
    ).reshape(3, width, columns)
    output_rows = lax.all_gather(output_weight, "blk", axis=0, tiled=True)
    cot_all = lax.all_gather(cotangent, "blk", axis=0, tiled=True).reshape(blocks, rows, width)
    token_factor = rms_factor(jnp.sum(tokens_group * tokens_group, axis=-1, keepdims=True), width)
    normed = (tokens_group * token_factor * mixing_scale).astype(bf16)
    query_raw = jnp.dot(normed, gathered[0], preferred_element_type=f32)
    key_raw = jnp.dot(normed, gathered[1], preferred_element_type=f32)
    value_heads = jnp.dot(normed, gathered[2], preferred_element_type=f32).astype(bf16)
    squares = head_sum(
        jnp.stack([jnp.sum(query_raw * query_raw, axis=-1), jnp.sum(key_raw * key_raw, axis=-1)])
    )
    query_factor = rms_factor(squares[0][:, None], width)
    key_factor = rms_factor(squares[1][:, None], width)
    query_heads = rotate(query_raw * query_factor * query_scale, cosine, sine_part).astype(bf16)
    key_heads = rotate(key_raw * key_factor * key_scale, cosine, sine_part).astype(bf16)
    keys_all = lax.all_gather(key_heads, "blk", axis=0, tiled=True)
    values_all = lax.all_gather(value_heads, "blk", axis=0, tiled=True)
    attended, context, totals = attend_forward(
        query_heads, keys_all, values_all, marks, tables, TILE
    )
    branch = jnp.dot(context, output_rows, preferred_element_type=f32).astype(bf16)
    branch_parts = lax.all_to_all(
        branch.reshape(heads_axis, rows, width), "head", split_axis=0, concat_axis=0, tiled=True
    )
    own_tokens = tokens.astype(f32)
    middle = own_tokens + jnp.sum(branch_parts.astype(f32), axis=0)
    middle_factor = rms_factor(jnp.sum(middle * middle, axis=-1, keepdims=True), width)
    routed = (middle * middle_factor * routing_scale).astype(bf16)
    probs = jax.nn.softmax(jnp.dot(routed, router_full, preferred_element_type=f32), axis=-1)

    gates, ups, downs = (
        [gather_pieces(weight[item], item) for item in range(local_experts)]
        for weight in (gate_weight, up_weight, down_weight)
    )
    routed_all = lax.all_gather(xor_chunks(routed, 1), "blk", axis=0, tiled=True)
    probs_all = jax.nn.softmax(
        jnp.dot(routed_all, xor_chunks(router_full, 0), preferred_element_type=f32), axis=-1
    )
    weight_here = lax.dynamic_slice_in_dim(
        probs_all, block_at * local_experts, local_experts, 1
    ).reshape(blocks, rows, local_experts)
    routed_all = routed_all.reshape(blocks, rows, width)
    slot_ids = jnp.arange(capacity, dtype=jnp.int32)
    slots = blocks * capacity
    combined = 0.0
    incoming = 0.0
    weight_grads = []
    stores = []
    for item in range(local_experts):
        placed = codes_here[:, None, :, item] == slot_ids[None, :, None]
        place = placed.astype(bf16)
        slot_weight = jnp.sum(
            jnp.where(placed, weight_here[:, None, :, item], 0.0), axis=-1
        ).reshape(slots, 1)
        arrived = jnp.einsum("srt,std->srd", place, routed_all).reshape(slots, width)
        arrived_cot = jnp.einsum("srt,std->srd", place, cot_all).reshape(slots, width)
        gate_all = jnp.concatenate(gates[item], axis=0)
        up_all = jnp.concatenate(ups[item], axis=0)
        down_all = jnp.concatenate(downs[item], axis=0)
        gate = jnp.dot(arrived, gate_all, preferred_element_type=f32)
        upward = jnp.dot(arrived, up_all, preferred_element_type=f32)
        sigmoid = jax.nn.sigmoid(gate)
        active = xor_chunks((gate * sigmoid * upward).astype(bf16), 1)
        produced = jnp.dot(active, down_all, preferred_element_type=f32).astype(bf16)
        cot_float = arrived_cot.astype(f32)
        produced_float = produced.astype(f32)
        weighted = (slot_weight * produced_float).astype(bf16).reshape(blocks, capacity, width)
        combined = combined + jnp.einsum(
            "srt,srd->std", place, weighted, preferred_element_type=f32
        )
        slot_grad = jnp.sum(cot_float * produced_float, axis=-1).reshape(blocks, capacity, 1)
        weight_grads.append(jnp.sum(jnp.where(placed, slot_grad, 0.0), axis=1))
        produced_grad = (slot_weight * cot_float).astype(bf16)
        active_grad = xor_chunks(
            jnp.dot(produced_grad, down_all.T, preferred_element_type=f32), 1
        )
        gate_grad = (active_grad * upward * sigmoid * (1.0 + gate * (1.0 - sigmoid))).astype(bf16)
        up_grad = (active_grad * (gate * sigmoid)).astype(bf16)
        coming = jnp.dot(gate_grad, gate_all.T, preferred_element_type=f32)
        coming = coming + jnp.dot(up_grad, up_all.T, preferred_element_type=f32)
        coming = coming.astype(bf16).reshape(blocks, capacity, width)
        incoming = incoming + jnp.einsum(
            "srt,srd->std", place, coming, preferred_element_type=f32
        )
        stores.append((arrived, produced_grad, active, gate_grad, up_grad))
    combined = lax.psum_scatter(
        combined.astype(bf16).reshape(blocks * rows, width), "blk", scatter_dimension=0, tiled=True
    )
    block_output = (middle + combined.astype(f32)).astype(bf16)
    prob_grad = lax.all_to_all(
        jnp.stack(weight_grads, axis=2), "blk", split_axis=0, concat_axis=2, tiled=True
    ).reshape(rows, experts)
    routed_grad = lax.psum_scatter(
        incoming.astype(bf16).reshape(blocks * rows, width), "blk", scatter_dimension=0, tiled=True
    )
    routed_grad = xor_chunks(routed_grad, 1).astype(f32)

    def pieces_of(left, right):
        size = left.shape[1] // heads_axis
        return [
            jnp.dot(
                left[:, offset * size : (offset + 1) * size].T, right, preferred_element_type=f32
            ).astype(bf16)
            for offset in range(heads_axis)
        ]

    down_out = jnp.stack(
        [scatter_pieces(pieces_of(store[2], store[1]), item) for item, store in enumerate(stores)]
    )
    gate_out = jnp.stack(
        [scatter_pieces(pieces_of(store[0], store[3]), item) for item, store in enumerate(stores)]
    )
    up_out = jnp.stack(
        [scatter_pieces(pieces_of(store[0], store[4]), item) for item, store in enumerate(stores)]
    )

    logit_grad = (
        probs * (prob_grad - jnp.sum(probs * prob_grad, axis=1, keepdims=True))
    ).astype(bf16)
    router_sum = jnp.dot(routed.T, logit_grad, preferred_element_type=f32)
    routed_grad = routed_grad + jnp.dot(logit_grad, router_full.T, preferred_element_type=f32)
    scaled = routed_grad * routing_scale
    inner = jnp.mean(scaled * middle, axis=-1, keepdims=True)
    middle_grad = (
        cotangent.astype(f32) + middle_factor * scaled - middle * (middle_factor**3 * inner)
    )
    routing_sum = jnp.sum(routed_grad * middle * middle_factor, axis=0)

    branch_grad = lax.all_gather(middle_grad.astype(bf16), "head", axis=0, tiled=True)
    context_grad = jnp.dot(branch_grad, output_rows.T, preferred_element_type=f32).astype(bf16)
    output_sum = jnp.dot(context.T, branch_grad, preferred_element_type=f32).astype(bf16)
    output_out = lax.psum_scatter(output_sum, "blk", scatter_dimension=0, tiled=True).astype(f32)
    query_grad_heads, key_grad_all, value_grad_all = attend_backward(
        query_heads, keys_all, values_all, context_grad, attended, totals, marks, tables, TILE
    )
    key_back = lax.psum_scatter(key_grad_all, "blk", scatter_dimension=0, tiled=True)
    value_back = lax.psum_scatter(value_grad_all, "blk", scatter_dimension=0, tiled=True)
    query_turn = rotate(query_grad_heads.astype(f32), cosine, -sine_part)
    key_turn = rotate(key_back.astype(f32), cosine, -sine_part)
    query_scaled = query_turn * query_scale
    key_scaled = key_turn * key_scale
    inners = (
        head_sum(
            jnp.stack(
                [jnp.sum(query_scaled * query_raw, axis=-1), jnp.sum(key_scaled * key_raw, axis=-1)]
            )
        )
        / width
    )
    query_raw_grad = (
        query_factor * query_scaled - query_raw * (query_factor**3 * inners[0][:, None])
    ).astype(bf16)
    key_raw_grad = (
        key_factor * key_scaled - key_raw * (key_factor**3 * inners[1][:, None])
    ).astype(bf16)
    querynorm_sum = jnp.sum(query_turn * query_raw * query_factor, axis=0)
    keynorm_sum = jnp.sum(key_turn * key_raw * key_factor, axis=0)
    normed_part = jnp.dot(query_raw_grad, gathered[0].T, preferred_element_type=f32)
    normed_part = normed_part + jnp.dot(key_raw_grad, gathered[1].T, preferred_element_type=f32)
    normed_part = normed_part + jnp.dot(value_back, gathered[2].T, preferred_element_type=f32)
    normed_parts = lax.all_to_all(
        normed_part.astype(bf16).reshape(heads_axis, rows, width),
        "head",
        split_axis=0,
        concat_axis=0,
        tiled=True,
    )
    normed_grad = jnp.sum(normed_parts.astype(f32), axis=0)
    own_factor = rms_factor(jnp.sum(own_tokens * own_tokens, axis=-1, keepdims=True), width)
    scaled = normed_grad * mixing_scale
    inner = jnp.mean(scaled * own_tokens, axis=-1, keepdims=True)
    tokens_grad = middle_grad + own_factor * scaled - own_tokens * (own_factor**3 * inner)
    mixing_sum = jnp.sum(normed_grad * own_tokens * own_factor, axis=0)
    raw_grads = jnp.stack([query_raw_grad, key_raw_grad, value_back])
    weight_sums = jnp.einsum("td,ntc->ndc", normed, raw_grads, preferred_element_type=f32).astype(
        bf16
    )
    weight_sums = jnp.transpose(
        weight_sums.reshape(3, heads_axis, blocks, part, columns), (2, 0, 1, 3, 4)
    ).reshape(blocks * 3 * heads_axis * part, columns)
    weight_sums = lax.psum_scatter(weight_sums, "blk", scatter_dimension=0, tiled=True)
    weight_sums = lax.all_to_all(
        weight_sums.reshape(3, heads_axis * part, columns),
        "head",
        split_axis=1,
        concat_axis=2,
        tiled=True,
    ).astype(f32)
    blank = jnp.zeros((heads_axis, columns), f32)
    query_line = lax.dynamic_update_slice(blank, querynorm_sum[None], (head_at, 0)).reshape(width)
    key_line = lax.dynamic_update_slice(blank, keynorm_sum[None], (head_at, 0)).reshape(width)
    lines = jnp.concatenate(
        [
            mixing_sum[:, None],
            query_line[:, None],
            key_line[:, None],
            routing_sum[:, None],
            router_sum,
        ],
        axis=1,
    )
    lines = lines.reshape(heads_axis, blocks, -1)
    lines = jnp.sum(lax.all_to_all(lines, "head", 0, 0, tiled=True), axis=0)
    lines = jnp.sum(lax.all_to_all(lines, "blk", 0, 0, tiled=True), axis=0)
    lines = lines.reshape(part, 4 + experts)
    return (
        block_output,
        tokens_grad,
        weight_sums[0],
        weight_sums[1],
        weight_sums[2],
        output_out,
        lines[:, 0],
        lines[:, 1],
        lines[:, 2],
        lines[:, 3],
        lines[:, 4:],
        gate_out,
        up_out,
        down_out,
    )


def solution(mesh):
    in_specs = (
        P(("head", "blk"), None),
        P(("head", "blk"), None),
        P(("head", "blk"), None),
        P(("head", "blk"), None),
        P(("head", "blk"), None),
        P(("head", "blk")),
        P(("head", "blk")),
        P(("head", "blk")),
        P(("head", "blk")),
        P(("head", "blk"), None),
        P("blk", "head", None),
        P("blk", "head", None),
        P("blk", "head", None),
        P(),
        P(),
        P(("head", "blk"), None),
        P(("head", "blk"), None),
        P(("head", "blk"), None),
    )
    out_specs = (
        P(("head", "blk"), None),
        P(("head", "blk"), None),
        P(("head", "blk"), None),
        P(("head", "blk"), None),
        P(("head", "blk"), None),
        P(("head", "blk"), None),
        P(("head", "blk")),
        P(("head", "blk")),
        P(("head", "blk")),
        P(("head", "blk")),
        P(("head", "blk"), None),
        P("blk", "head", None),
        P("blk", "head", None),
        P("blk", "head", None),
    )
    return jax.shard_map(
        on_device, mesh=mesh, in_specs=in_specs, out_specs=out_specs, check_vma=False
    )
```

```python
from functools import partial
import math

import jax
import jax.numpy as jnp
import numpy as np
from jax import lax
from jax.experimental import pallas as pl
from jax.experimental.pallas import tpu as pltpu
from jax.sharding import PartitionSpec as P


HDIM = 128
TILE = 256
LOG2E = 1.4426950408889634
norm_eps = 1e-05
rope_base = 10000.0
f32 = jnp.float32
bf16 = jnp.bfloat16


def rms_factor(square_sum, width):
    return lax.rsqrt(square_sum / width + norm_eps)


def rope_tables(position, head_size):
    half = head_size // 2
    freqs = rope_base ** (-(np.arange(half, dtype=np.float64) * 2.0) / head_size)
    angles = position.astype(f32)[:, None] * jnp.asarray(freqs.astype(np.float32))[None, :]
    cosine = jnp.cos(angles)
    sine_part = jnp.sin(angles)
    return (
        jnp.concatenate([cosine, cosine], axis=1),
        jnp.concatenate([-sine_part, sine_part], axis=1),
    )


def column_of(pieces):
    count = len(pieces)
    rows = pieces[0].shape[1] // count
    total = pieces[0][...]
    for offset in range(1, count):
        parts = [
            pieces[offset][:, (at ^ offset) * rows : ((at ^ offset) + 1) * rows]
            for at in range(count)
        ]
        total = total + jnp.concatenate(parts, axis=1)
    return jnp.transpose(jnp.broadcast_to(total, (8, total.shape[1])))[:, :1]


def turned(value, cosine, sine_part):
    return value * cosine + pltpu.roll(value, HDIM // 2, 1) * sine_part


def rope_kernel(*refs, count, width, paired):
    squares = refs[:count]
    raw, scale, cosine, sine_part = refs[count : count + 4]
    out, factors = refs[-2:]
    factor = lax.rsqrt(column_of(squares) / width + norm_eps)
    factors[...] = jnp.broadcast_to(factor, factors.shape)
    for head in range(raw.shape[1] // HDIM):
        span = slice(head * HDIM, (head + 1) * HDIM)
        value = turned(raw[:, span] * factor * scale[:, span], cosine[...], sine_part[...])
        if paired:
            start = 2 * head * HDIM
            out[:, start : start + HDIM] = value.astype(jnp.bfloat16)
            out[:, start + HDIM : start + 2 * HDIM] = refs[count + 4][:, span]
        else:
            out[:, span] = value.astype(jnp.bfloat16)


def rope_forward(squares, raw, scale, cosine, sine_part, values, width):
    group, columns = raw.shape
    paired = values is not None
    extra = (values,) if paired else ()
    return pl.pallas_call(
        partial(rope_kernel, count=len(squares), width=width, paired=paired),
        out_shape=[
            jax.ShapeDtypeStruct((group, columns * (2 if paired else 1)), jnp.bfloat16),
            jax.ShapeDtypeStruct((group, HDIM), jnp.float32),
        ],
    )(*squares, raw, scale[None], cosine, sine_part, *extra)


def unrope_kernel(back, raw, factors, scale, cosine, sine_part, scaled, inner, gain, *, stride):
    group = raw.shape[0]
    total = jnp.zeros((group, HDIM), jnp.float32)
    for head in range(raw.shape[1] // HDIM):
        span = slice(head * HDIM, (head + 1) * HDIM)
        start = stride * head * HDIM
        grad = back[:, start : start + HDIM].astype(jnp.float32)
        turn = turned(grad, cosine[...], -sine_part[...])
        product = turn * raw[:, span]
        gain[:, span] = jnp.sum(product * factors[...], axis=0, keepdims=True)
        scaled[:, span] = turn * scale[:, span]
        total = total + product * scale[:, span]
    sums = jnp.broadcast_to(jnp.sum(total, axis=1, keepdims=True), (group, HDIM))
    inner[...] = jnp.transpose(sums)[:1, :]


def rope_backward(back, raw, factors, scale, cosine, sine_part, stride):
    group, columns = raw.shape
    return pl.pallas_call(
        partial(unrope_kernel, stride=stride),
        out_shape=[
            jax.ShapeDtypeStruct((group, columns), jnp.float32),
            jax.ShapeDtypeStruct((1, group), jnp.float32),
            jax.ShapeDtypeStruct((1, columns), jnp.float32),
        ],
    )(back, raw, factors, scale[None], cosine, sine_part)


def raw_kernel(*refs, count, width, paired):
    scaled, raw, factors = refs[count : count + 3]
    out = refs[-1]
    inner = column_of(refs[:count]) / width
    factor = factors[:, :1]
    columns = raw.shape[1]
    slope = factor * factor * factor * inner
    for head in range(columns // HDIM):
        span = slice(head * HDIM, (head + 1) * HDIM)
        out[:, span] = (factor * scaled[:, span] - raw[:, span] * slope).astype(jnp.bfloat16)
        if paired:
            start = (2 * head + 1) * HDIM
            out[:, columns + head * HDIM : columns + (head + 1) * HDIM] = refs[count + 3][
                :, start : start + HDIM
            ]


def raw_backward(inner, scaled, raw, factors, pairs_back, width):
    group, columns = raw.shape
    paired = pairs_back is not None
    extra = (pairs_back,) if paired else ()
    return pl.pallas_call(
        partial(raw_kernel, count=len(inner), width=width, paired=paired),
        out_shape=jax.ShapeDtypeStruct((group, columns * (2 if paired else 1)), jnp.bfloat16),
    )(*inner, scaled, raw, factors, *extra)


def slot_codes(routes, ordering, experts, capacity):
    expert_ids = jnp.arange(experts, dtype=jnp.int32)
    absent = jnp.int32(1 << 30)
    chosen = routes[:, :, None] == expert_ids[None, None, :]
    order = jnp.min(jnp.where(chosen, ordering[:, :, None], absent), axis=1)
    rank = jnp.sum((order[None, :, :] < order[:, None, :]).astype(jnp.int32), axis=1)
    return jnp.where((order < absent) & (rank < capacity), rank, -1)


def stream_layout(seq_lengths, stream_index):
    ends = jnp.cumsum(seq_lengths)
    starts = ends - seq_lengths
    passed = (stream_index[:, None] >= ends[None, :]).astype(jnp.int32)
    sequence = jnp.sum(passed, axis=1)
    owner = sequence[:, None] == jnp.arange(seq_lengths.shape[0], dtype=jnp.int32)[None, :]
    opening = jnp.sum(jnp.where(owner, starts[None, :], 0), axis=1)
    return (sequence, stream_index - opening)


def tile_lists(query_index, query_seq, key_index, key_seq, tile):
    query_tiles = query_index.shape[0] // tile
    key_tiles = key_index.shape[0] // tile
    query_marks = query_index.reshape(query_tiles, tile)
    query_seqs = query_seq.reshape(query_tiles, tile)
    key_marks = key_index.reshape(key_tiles, tile)
    key_seqs = key_seq.reshape(key_tiles, tile)
    early = jnp.min(key_marks, axis=1)[None, :] <= jnp.max(query_marks, axis=1)[:, None]
    above = jnp.max(key_seqs, axis=1)[None, :] >= jnp.min(query_seqs, axis=1)[:, None]
    below = jnp.min(key_seqs, axis=1)[None, :] <= jnp.max(query_seqs, axis=1)[:, None]
    live = (early & above & below).astype(jnp.int32)
    order = jnp.cumsum(live, axis=1) - 1
    numbers = jnp.arange(key_tiles, dtype=jnp.int32)
    hits = (order[:, :, None] == numbers[None, None, :]) & (live[:, :, None] > 0)
    listed = jnp.sum(jnp.where(hits, numbers[None, :, None], 0), axis=1)
    return (listed.astype(jnp.int32), jnp.sum(live, axis=1).astype(jnp.int32), live)


def spread(vector):
    return jnp.broadcast_to(vector[:, None], (vector.shape[0], 128))


def twice(value, count):
    return value if count == 1 else jnp.concatenate([value] * count, axis=1)


def forward_kernel(
    listed, counts, query, pairs, at, opening, key_at, attended, context, totals, total, acc, *, tile
):
    lanes = 128
    copies = tile // lanes
    factor = LOG2E / math.sqrt(HDIM)
    for step in range(query.shape[0] // tile):
        span = slice(step * tile, (step + 1) * tile)
        acc[...] = jnp.zeros_like(acc)
        total[...] = jnp.zeros_like(total)

        def visit(turn, carry):
            number = listed[step, turn]
            start = pl.multiple_of(number * tile, tile)
            scores = lax.dot_general(
                query[span, :],
                pairs[pl.ds(start, tile), :HDIM],
                (((1,), (1,)), ((), ())),
                preferred_element_type=jnp.float32,
            )
            marks = key_at[pl.ds(number, 1), :]
            allowed = (marks <= twice(at[span, :], copies)) & (
                marks >= twice(opening[span, :], copies)
            )
            expo = jnp.where(allowed, jnp.exp2(scores * factor), 0.0)
            partial_sum = expo[:, :lanes]
            for copy in range(1, copies):
                partial_sum = partial_sum + expo[:, copy * lanes : (copy + 1) * lanes]
            total[...] += partial_sum
            acc[...] += jnp.dot(
                expo.astype(jnp.bfloat16),
                pairs[pl.ds(start, tile), HDIM:],
                preferred_element_type=jnp.float32,
            )
            return carry

        lax.fori_loop(0, counts[step], visit, 0)
        full = jnp.sum(total[...], axis=1, keepdims=True)
        result = acc[...] / full
        attended[span, :] = result
        context[span, :] = result.astype(jnp.bfloat16)
        totals[span, :] = jnp.broadcast_to(full, (tile, lanes))


def attend_forward(queries, pairs, marks, tables, tile):
    group, columns = queries.shape
    total_rows = pairs.shape[0]
    listed, counts, _ = tables
    at, opening, key_at = marks[0], marks[1], marks[2]
    heads = columns // HDIM
    lane = lambda rows: pl.BlockSpec((rows, HDIM), lambda h, *refs: (0, h))
    wide = pl.BlockSpec((total_rows, 2 * HDIM), lambda h, *refs: (0, h))
    fixed = lambda array: pl.BlockSpec(array.shape, lambda h, *refs: (0, 0))
    return pl.pallas_call(
        partial(forward_kernel, tile=tile),
        grid_spec=pltpu.PrefetchScalarGridSpec(
            num_scalar_prefetch=2,
            grid=(heads,),
            in_specs=[
                lane(group),
                wide,
                fixed(at),
                fixed(opening),
                fixed(key_at),
            ],
            out_specs=[lane(group), lane(group), lane(group)],
            scratch_shapes=[
                pltpu.VMEM((tile, HDIM), jnp.float32),
                pltpu.VMEM((tile, HDIM), jnp.float32),
            ],
        ),
        out_shape=[
            jax.ShapeDtypeStruct((group, columns), jnp.float32),
            jax.ShapeDtypeStruct((group, columns), jnp.bfloat16),
            jax.ShapeDtypeStruct((group, columns), jnp.float32),
        ],
        name="attend_forward",
    )(listed, counts, queries, pairs, at, opening, key_at)


def backward_kernel(
    live,
    query,
    pairs,
    grad,
    attended,
    totals,
    at_row,
    opening_row,
    key_col,
    query_out,
    pairs_out,
    scaled,
    offset,
    query_acc,
    key_acc,
    value_acc,
    *,
    tile,
):
    copies = tile // 128
    steps = query.shape[0] // tile
    factor = 1.0 / math.sqrt(HDIM)
    grads = grad[...].astype(jnp.float32)
    scaled[...] = (grads / totals[...]).astype(jnp.bfloat16)
    sums = jnp.sum(grads * attended[...], axis=1, keepdims=True) / totals[...]
    offset[...] = jnp.transpose(sums)[:8, :]
    query_acc[...] = jnp.zeros_like(query_acc)

    def visit(number, carry):
        start = pl.multiple_of(number * tile, tile)
        window = pl.ds(start, tile)
        key_acc[...] = jnp.zeros_like(key_acc)
        value_acc[...] = jnp.zeros_like(value_acc)
        for step in range(steps):
            span = slice(step * tile, (step + 1) * tile)

            @pl.when(live[step, number] > 0)
            def unused():
                scores = lax.dot_general(
                    pairs[window, :HDIM],
                    query[span, :],
                    (((1,), (1,)), ((), ())),
                    preferred_element_type=jnp.float32,
                )
                marks = twice(key_col[window, :], copies)
                allowed = (marks <= at_row[:, span]) & (marks >= opening_row[:, span])
                expo = jnp.where(allowed, jnp.exp2(scores * (factor * LOG2E)), 0.0)
                inner = lax.dot_general(
                    pairs[window, HDIM:],
                    scaled[span, :],
                    (((1,), (1,)), ((), ())),
                    preferred_element_type=jnp.float32,
                )
                back = (expo * (inner - offset[0:1, span])).astype(jnp.bfloat16)
                key_acc[...] += jnp.dot(back, query[span, :], preferred_element_type=jnp.float32)
                value_acc[...] += jnp.dot(
                    expo.astype(jnp.bfloat16), scaled[span, :], preferred_element_type=jnp.float32
                )
                query_acc[span, :] += lax.dot_general(
                    back,
                    pairs[window, :HDIM],
                    (((0,), (0,)), ((), ())),
                    preferred_element_type=jnp.float32,
                )

        pairs_out[window, :HDIM] = (key_acc[...] * factor).astype(jnp.bfloat16)
        pairs_out[window, HDIM:] = value_acc[...].astype(jnp.bfloat16)
        return carry

    lax.fori_loop(0, pairs.shape[0] // tile, visit, 0)
    query_out[...] = (query_acc[...] * factor).astype(jnp.bfloat16)


def attend_backward(queries, pairs, grads, attended, totals, marks, tables, tile):
    group, columns = queries.shape
    total_rows = pairs.shape[0]
    live = tables[2]
    at_row, opening_row, key_col = marks[3], marks[4], marks[5]
    heads = columns // HDIM
    lane = lambda rows: pl.BlockSpec((rows, HDIM), lambda h, *refs: (0, h))
    wide = pl.BlockSpec((total_rows, 2 * HDIM), lambda h, *refs: (0, h))
    fixed = lambda array: pl.BlockSpec(array.shape, lambda h, *refs: (0, 0))
    return pl.pallas_call(
        partial(backward_kernel, tile=tile),
        grid_spec=pltpu.PrefetchScalarGridSpec(
            num_scalar_prefetch=1,
            grid=(heads,),
            in_specs=[
                lane(group),
                wide,
                lane(group),
                lane(group),
                lane(group),
                fixed(at_row),
                fixed(opening_row),
                fixed(key_col),
            ],
            out_specs=[lane(group), wide],
            scratch_shapes=[
                pltpu.VMEM((group, HDIM), jnp.bfloat16),
                pltpu.VMEM((8, group), jnp.float32),
                pltpu.VMEM((group, HDIM), jnp.float32),
                pltpu.VMEM((tile, HDIM), jnp.float32),
                pltpu.VMEM((tile, HDIM), jnp.float32),
            ],
        ),
        out_shape=[
            jax.ShapeDtypeStruct((group, columns), jnp.bfloat16),
            jax.ShapeDtypeStruct((total_rows, 2 * columns), jnp.bfloat16),
        ],
        name="attend_backward",
    )(live, queries, pairs, grads, attended, totals, at_row, opening_row, key_col)


def attend_marks(query_index, query_start, key_index, tile):
    return (
        spread(query_index),
        spread(query_start),
        key_index.reshape(-1, tile),
        query_index[None, :],
        query_start[None, :],
        spread(key_index),
    )


def exchange(array, offset):
    count = lax.axis_size("head")
    return lax.ppermute(array, "head", [(at, at ^ offset) for at in range(count)])


def head_pieces(array):
    return [array] + [exchange(array, offset) for offset in range(1, lax.axis_size("head"))]


def head_turn(pieces):
    return [pieces[0]] + [exchange(piece, at + 1) for at, piece in enumerate(pieces[1:])]


def add_all(pieces):
    total = pieces[0].astype(f32)
    for piece in pieces[1:]:
        total = total + piece.astype(f32)
    return total


def bit_order(turn):
    count = lax.axis_size("head").bit_length() - 1
    return [1 << ((turn + step) % count) for step in range(count)]


def gather_pieces(array, turn):
    pieces = {0: array}
    for bit in bit_order(turn):
        for offset in list(pieces):
            pieces[offset ^ bit] = exchange(pieces[offset], bit)
    return [pieces[offset] for offset in range(len(pieces))]


def scatter_pieces(pieces, turn):
    held = dict(enumerate(pieces))
    for bit in bit_order(turn):
        for offset in [item for item in held if item & bit]:
            piece = held.pop(offset).astype(bf16)
            arrived = exchange(piece, bit)
            held[offset ^ bit] = held[offset ^ bit].astype(f32) + arrived.astype(f32)
    return held[0]


def xor_order(array, axis):
    count = lax.axis_size("head")
    at = lax.axis_index("head")
    size = array.shape[axis] // count
    chunks = [
        lax.dynamic_slice_in_dim(array, (at ^ offset) * size, size, axis) for offset in range(count)
    ]
    return chunks


def xor_chunks(array, axis):
    return jnp.concatenate(xor_order(array, axis), axis=axis)


def absolute(pieces):
    at = lax.axis_index("head")
    result = []
    for place in range(len(pieces)):
        value = pieces[0]
        for offset in range(1, len(pieces)):
            value = jnp.where(at == place ^ offset, pieces[offset], value)
        result.append(value)
    return result


def move_rows(array, outer, inner, part):
    shaped = array.reshape(outer, inner, part, array.shape[1])
    return jnp.transpose(shaped, (1, 0, 2, 3)).reshape(array.shape)


def move_columns(array, outer, inner, part):
    shaped = array.reshape(array.shape[0], outer, inner, part)
    return jnp.transpose(shaped, (0, 2, 1, 3)).reshape(array.shape)


def layer(
    tokens,
    query_weight,
    key_weight,
    value_weight,
    output_weight,
    mixing_gain,
    query_gain,
    key_gain,
    routing_gain,
    router_weight,
    gate_weight,
    up_weight,
    down_weight,
    seq_lengths,
    dealt_order,
    expert_routes,
    slot_order,
    cotangent,
):
    heads_axis = lax.axis_size("head")
    blocks = lax.axis_size("blk")
    head_at = lax.axis_index("head")
    block_at = lax.axis_index("blk")
    rows, width = tokens.shape
    picks = expert_routes.shape[1]
    total_rows = dealt_order.shape[0]
    group = rows * heads_axis
    columns = width // heads_axis
    part = query_weight.shape[0]
    head_size = HDIM
    experts = router_weight.shape[1]
    local_experts = gate_weight.shape[0]
    capacity = 5 * rows * picks // (4 * experts)
    slots = blocks * capacity

    slices = [
        jnp.concatenate(chunks, axis=1)
        for chunks in zip(
            xor_order(key_weight, 1), xor_order(value_weight, 1), xor_order(query_weight, 1)
        )
    ]
    slices = head_turn(slices)
    output_rows = lax.all_gather(output_weight, "blk", axis=0, tiled=True)
    token_pieces = head_pieces(tokens)
    rows_here = jnp.stack(absolute(slices)).reshape(heads_axis * part, 3 * columns)
    pair_full = lax.all_gather(rows_here[:, : 2 * columns], "blk", axis=0, tiled=True)
    pair_full = move_rows(pair_full, blocks, heads_axis, part)
    query_full = lax.all_gather(rows_here[:, 2 * columns :], "blk", axis=0, tiled=True)
    query_full = move_rows(query_full, blocks, heads_axis, part)
    cot_all = lax.all_gather(cotangent, "blk", axis=0, tiled=True).reshape(blocks, rows, width)

    small = jnp.concatenate(
        [
            mixing_gain[:, None],
            query_gain[:, None],
            key_gain[:, None],
            routing_gain[:, None],
            router_weight,
        ],
        axis=1,
    ).reshape(1, -1)
    small = lax.all_gather(small, "blk", axis=0, tiled=True)
    small = jnp.stack(absolute(head_pieces(small))).reshape(width, 4 + experts)
    mixing_scale = small[:, 0].astype(f32)
    routing_scale = small[:, 3].astype(f32)
    query_scale = lax.dynamic_slice_in_dim(small[:, 1], head_at * columns, columns).astype(f32)
    key_scale = lax.dynamic_slice_in_dim(small[:, 2], head_at * columns, columns).astype(f32)
    router_full = small[:, 4:]
    codes = slot_codes(expert_routes, slot_order, experts, capacity)
    codes = lax.all_gather(codes, "blk", axis=0, tiled=True).reshape(blocks, rows, experts)
    codes_here = lax.dynamic_slice_in_dim(codes, block_at * local_experts, local_experts, 2)

    key_index = jnp.transpose(
        xor_chunks(dealt_order.reshape(heads_axis, blocks, rows), 0), (1, 0, 2)
    ).reshape(total_rows)
    key_seq = stream_layout(seq_lengths, key_index)[0]
    query_index = lax.dynamic_slice_in_dim(key_index, block_at * group, group)
    query_seq, query_position = stream_layout(seq_lengths, query_index)
    cosine, sine_part = rope_tables(query_position, head_size)
    tables = tile_lists(query_index, query_seq, key_index, key_seq, TILE)
    marks = attend_marks(query_index, query_index - query_position, key_index, TILE)

    gates, ups, downs = (
        [gather_pieces(weight[item], item) for item in range(local_experts)]
        for weight in (gate_weight, up_weight, down_weight)
    )

    token_group = jnp.concatenate(token_pieces, axis=0).astype(f32)
    token_factor = rms_factor(jnp.sum(token_group * token_group, axis=-1, keepdims=True), width)
    normed = (token_group * token_factor * mixing_scale).astype(bf16)
    normed_moved = move_columns(normed, heads_axis, blocks, part)
    key_raw = jnp.dot(normed, pair_full[:, :columns], preferred_element_type=f32)
    value_heads = jnp.dot(normed, pair_full[:, columns:], preferred_element_type=f32)
    value_heads = value_heads.astype(bf16)
    key_squares = head_pieces(jnp.sum(key_raw * key_raw, axis=-1)[None])
    pairs, key_factor = rope_forward(
        key_squares, key_raw, key_scale, cosine, sine_part, value_heads, width
    )
    query_raw = jnp.dot(normed, query_full, preferred_element_type=f32)
    query_squares = head_pieces(jnp.sum(query_raw * query_raw, axis=-1)[None])
    query_heads, query_factor = rope_forward(
        query_squares, query_raw, query_scale, cosine, sine_part, None, width
    )
    pairs_all = lax.all_gather(pairs, "blk", axis=0, tiled=True)
    attended, context, totals = attend_forward(query_heads, pairs_all, marks, tables, TILE)
    branch = jnp.dot(context, output_rows, preferred_element_type=f32).astype(bf16)
    branch = head_turn([branch[piece * rows : (piece + 1) * rows] for piece in range(heads_axis)])
    own_tokens = tokens.astype(f32)
    middle = own_tokens + add_all(branch)
    middle_factor = rms_factor(jnp.sum(middle * middle, axis=-1, keepdims=True), width)
    routed = (middle * middle_factor * routing_scale).astype(bf16)

    routed_all = lax.all_gather(xor_chunks(routed, 1), "blk", axis=0, tiled=True)
    probs = jax.nn.softmax(jnp.dot(routed, router_full, preferred_element_type=f32), axis=-1)
    probs_all = jax.nn.softmax(
        jnp.dot(routed_all, xor_chunks(router_full, 0), preferred_element_type=f32), axis=-1
    )
    weight_here = lax.dynamic_slice_in_dim(
        probs_all, block_at * local_experts, local_experts, 1
    ).reshape(blocks, rows, local_experts)
    routed_all = routed_all.reshape(blocks, rows, width)
    slot_ids = jnp.arange(capacity, dtype=jnp.int32)
    combined = 0.0
    incoming = 0.0
    weight_grads = []
    stores = []
    for item in range(local_experts):
        placed = codes_here[:, None, :, item] == slot_ids[None, :, None]
        place = placed.astype(bf16)
        slot_weight = jnp.sum(
            jnp.where(placed, weight_here[:, None, :, item], 0.0), axis=-1
        ).reshape(slots, 1)
        arrived = jnp.einsum("srt,std->srd", place, routed_all).reshape(slots, width)
        arrived_cot = jnp.einsum("srt,std->srd", place, cot_all).reshape(slots, width)
        gate_all = jnp.concatenate(gates[item], axis=0)
        up_all = jnp.concatenate(ups[item], axis=0)
        down_all = jnp.concatenate(downs[item], axis=0)
        gate = jnp.dot(arrived, gate_all, preferred_element_type=f32)
        upward = jnp.dot(arrived, up_all, preferred_element_type=f32)
        sigmoid = jax.nn.sigmoid(gate)
        active = xor_chunks((gate * sigmoid * upward).astype(bf16), 1)
        produced = jnp.dot(active, down_all, preferred_element_type=f32).astype(bf16)
        cot_float = arrived_cot.astype(f32)
        produced_float = produced.astype(f32)
        weighted = (slot_weight * produced_float).astype(bf16).reshape(blocks, capacity, width)
        combined = combined + jnp.einsum(
            "srt,srd->std", place, weighted, preferred_element_type=f32
        )
        slot_grad = jnp.sum(cot_float * produced_float, axis=-1).reshape(blocks, capacity, 1)
        weight_grads.append(jnp.sum(jnp.where(placed, slot_grad, 0.0), axis=1))
        produced_grad = (slot_weight * cot_float).astype(bf16)
        active_grad = xor_chunks(
            jnp.dot(produced_grad, down_all.T, preferred_element_type=f32), 1
        )
        gate_grad = (active_grad * upward * sigmoid * (1.0 + gate * (1.0 - sigmoid))).astype(bf16)
        up_grad = (active_grad * (gate * sigmoid)).astype(bf16)
        coming = jnp.dot(gate_grad, gate_all.T, preferred_element_type=f32)
        coming = coming + jnp.dot(up_grad, up_all.T, preferred_element_type=f32)
        coming = coming.astype(bf16).reshape(blocks, capacity, width)
        incoming = incoming + jnp.einsum(
            "srt,srd->std", place, coming, preferred_element_type=f32
        )
        stores.append((arrived, produced_grad, active, gate_grad, up_grad))
    routed_grad = lax.psum_scatter(
        incoming.astype(bf16).reshape(blocks * rows, width),
        "blk",
        scatter_dimension=0,
        tiled=True,
    )
    combined = lax.psum_scatter(
        combined.astype(bf16).reshape(blocks * rows, width),
        "blk",
        scatter_dimension=0,
        tiled=True,
    )
    block_output = (middle + combined.astype(f32)).astype(bf16)
    prob_grad = lax.all_to_all(
        jnp.stack(weight_grads, axis=2), "blk", split_axis=0, concat_axis=2, tiled=True
    ).reshape(rows, experts)

    def pieces_of(left, right):
        size = left.shape[1] // heads_axis
        return [
            lax.optimization_barrier(
                jnp.dot(
                    left[:, offset * size : (offset + 1) * size].T,
                    right,
                    preferred_element_type=f32,
                ).astype(bf16)
            )
            for offset in range(heads_axis)
        ]

    down_out, gate_out, up_out = (
        jnp.stack(
            [
                scatter_pieces(pieces_of(store[left], store[right]), item)
                for item, store in enumerate(stores)
            ]
        ).astype(f32)
        for left, right in ((2, 1), (0, 3), (0, 4))
    )

    logit_grad = (
        probs * (prob_grad - jnp.sum(probs * prob_grad, axis=1, keepdims=True))
    ).astype(bf16)
    router_sum = jnp.dot(routed.T, logit_grad, preferred_element_type=f32)
    routed_grad = xor_chunks(routed_grad, 1).astype(f32) + jnp.dot(
        logit_grad, router_full.T, preferred_element_type=f32
    )
    scaled = routed_grad * routing_scale
    inner = jnp.mean(scaled * middle, axis=-1, keepdims=True)
    middle_grad = (
        cotangent.astype(f32) + middle_factor * scaled - middle * (middle_factor**3 * inner)
    )
    routing_sum = jnp.sum(routed_grad * middle * middle_factor, axis=0)

    branch_grad = head_pieces(middle_grad.astype(bf16))
    branch_grad = jnp.concatenate(branch_grad, axis=0)
    context_grad = jnp.dot(branch_grad, output_rows.T, preferred_element_type=f32).astype(bf16)
    output_sum = jnp.dot(context.T, branch_grad, preferred_element_type=f32).astype(bf16)
    output_out = lax.psum_scatter(output_sum, "blk", scatter_dimension=0, tiled=True)
    query_back, pairs_back = attend_backward(
        query_heads, pairs_all, context_grad, attended, totals, marks, tables, TILE
    )
    pairs_back = lax.psum_scatter(pairs_back, "blk", scatter_dimension=0, tiled=True)
    query_scaled, query_inner, querynorm_sum = rope_backward(
        query_back, query_raw, query_factor, query_scale, cosine, sine_part, 1
    )
    query_inner = head_pieces(query_inner)
    query_raw_grad = raw_backward(query_inner, query_scaled, query_raw, query_factor, None, width)
    query_sum = jnp.dot(normed_moved.T, query_raw_grad, preferred_element_type=f32).astype(bf16)
    query_sum = lax.psum_scatter(query_sum, "blk", scatter_dimension=0, tiled=True)
    normed_part = jnp.dot(query_raw_grad, query_full.T, preferred_element_type=f32)
    key_scaled, key_inner, keynorm_sum = rope_backward(
        pairs_back, key_raw, key_factor, key_scale, cosine, sine_part, 2
    )
    key_inner = head_pieces(key_inner)
    pair_grad = raw_backward(key_inner, key_scaled, key_raw, key_factor, pairs_back, width)
    pair_sum = jnp.dot(normed_moved.T, pair_grad, preferred_element_type=f32).astype(bf16)
    pair_sum = lax.psum_scatter(pair_sum, "blk", scatter_dimension=0, tiled=True)
    normed_part = normed_part + jnp.dot(pair_grad, pair_full.T, preferred_element_type=f32)
    normed_part = normed_part.astype(bf16)
    normed_part = head_turn(
        [normed_part[piece * rows : (piece + 1) * rows] for piece in range(heads_axis)]
    )
    normed_grad = add_all(normed_part)
    own_factor = rms_factor(jnp.sum(own_tokens * own_tokens, axis=-1, keepdims=True), width)
    scaled = normed_grad * mixing_scale
    inner = jnp.mean(scaled * own_tokens, axis=-1, keepdims=True)
    tokens_grad = middle_grad + own_factor * scaled - own_tokens * (own_factor**3 * inner)
    mixing_sum = jnp.sum(normed_grad * own_tokens * own_factor, axis=0)

    def turned_back(array):
        return jnp.stack(
            [
                jnp.concatenate(absolute(list(pieces)), axis=1).astype(f32)
                for pieces in zip(
                    *(
                        [piece[:, at : at + columns] for at in range(0, piece.shape[1], columns)]
                        for piece in head_turn(xor_order(array, 0))
                    )
                )
            ]
        )

    query_out = turned_back(query_sum)[0]
    pair_out = turned_back(pair_sum)

    blank = jnp.zeros((heads_axis, columns), f32)
    query_line = lax.dynamic_update_slice(blank, querynorm_sum, (head_at, 0)).reshape(width)
    key_line = lax.dynamic_update_slice(blank, keynorm_sum, (head_at, 0)).reshape(width)
    lines = jnp.concatenate(
        [
            mixing_sum[:, None],
            query_line[:, None],
            key_line[:, None],
            routing_sum[:, None],
            router_sum,
        ],
        axis=1,
    ).reshape(heads_axis, -1)
    lines = add_all(head_turn(xor_order(lines, 0)))
    lines = lax.all_to_all(lines.reshape(blocks, -1), "blk", 0, 0, tiled=True)
    lines = jnp.sum(lines, axis=0).reshape(part, 4 + experts)
    return (
        block_output,
        tokens_grad,
        query_out,
        pair_out[0],
        pair_out[1],
        output_out.astype(f32),
        lines[:, 0],
        lines[:, 1],
        lines[:, 2],
        lines[:, 3],
        lines[:, 4:],
        gate_out,
        up_out,
        down_out,
    )


def solution(mesh):
    in_specs = (
        P(("head", "blk"), None),
        P(("head", "blk"), None),
        P(("head", "blk"), None),
        P(("head", "blk"), None),
        P(("head", "blk"), None),
        P(("head", "blk")),
        P(("head", "blk")),
        P(("head", "blk")),
        P(("head", "blk")),
        P(("head", "blk"), None),
        P("blk", "head", None),
        P("blk", "head", None),
        P("blk", "head", None),
        P(),
        P(),
        P(("head", "blk"), None),
        P(("head", "blk"), None),
        P(("head", "blk"), None),
    )
    out_specs = (
        P(("head", "blk"), None),
        P(("head", "blk"), None),
        P(("head", "blk"), None),
        P(("head", "blk"), None),
        P(("head", "blk"), None),
        P(("head", "blk"), None),
        P(("head", "blk")),
        P(("head", "blk")),
        P(("head", "blk")),
        P(("head", "blk")),
        P(("head", "blk"), None),
        P("blk", "head", None),
        P("blk", "head", None),
        P("blk", "head", None),
    )
    return jax.shard_map(layer, mesh=mesh, in_specs=in_specs, out_specs=out_specs, check_vma=False)
```

```python
from functools import partial
import math

import jax
import jax.numpy as jnp
import numpy as np
from jax import lax
from jax.experimental import pallas as pl
from jax.experimental.pallas import tpu as pltpu
from jax.sharding import PartitionSpec as P


HDIM = 128
TILE = 256
LOG2E = 1.4426950408889634
norm_eps = 1e-05
rope_base = 10000.0
f32 = jnp.float32
bf16 = jnp.bfloat16


def rms_factor(square_sum, width):
    return lax.rsqrt(square_sum / width + norm_eps)


def rope_tables(position, head_size):
    half = head_size // 2
    freqs = rope_base ** (-(np.arange(half, dtype=np.float64) * 2.0) / head_size)
    angles = position.astype(f32)[:, None] * jnp.asarray(freqs.astype(np.float32))[None, :]
    cosine = jnp.cos(angles)
    sine_part = jnp.sin(angles)
    return (
        jnp.concatenate([cosine, cosine], axis=1),
        jnp.concatenate([-sine_part, sine_part], axis=1),
    )


def column_of(pieces):
    count = len(pieces)
    rows = pieces[0].shape[1] // count
    total = pieces[0][...]
    for offset in range(1, count):
        parts = [
            pieces[offset][:, (at ^ offset) * rows : ((at ^ offset) + 1) * rows]
            for at in range(count)
        ]
        total = total + jnp.concatenate(parts, axis=1)
    return jnp.transpose(jnp.broadcast_to(total, (8, total.shape[1])))[:, :1]


def turned(value, cosine, sine_part):
    return value * cosine + pltpu.roll(value, HDIM // 2, 1) * sine_part


def rope_kernel(*refs, count, width, paired):
    squares = refs[:count]
    raw, scale, cosine, sine_part = refs[count : count + 4]
    out, factors = refs[-2:]
    factor = lax.rsqrt(column_of(squares) / width + norm_eps)
    factors[...] = jnp.broadcast_to(factor, factors.shape)
    for head in range(raw.shape[1] // HDIM):
        span = slice(head * HDIM, (head + 1) * HDIM)
        value = turned(raw[:, span] * factor * scale[:, span], cosine[...], sine_part[...])
        if paired:
            start = 2 * head * HDIM
            out[:, start : start + HDIM] = value.astype(jnp.bfloat16)
            out[:, start + HDIM : start + 2 * HDIM] = refs[count + 4][:, span]
        else:
            out[:, span] = value.astype(jnp.bfloat16)


def rope_forward(squares, raw, scale, cosine, sine_part, values, width):
    group, columns = raw.shape
    paired = values is not None
    extra = (values,) if paired else ()
    return pl.pallas_call(
        partial(rope_kernel, count=len(squares), width=width, paired=paired),
        out_shape=[
            jax.ShapeDtypeStruct((group, columns * (2 if paired else 1)), jnp.bfloat16),
            jax.ShapeDtypeStruct((group, HDIM), jnp.float32),
        ],
    )(*squares, raw, scale[None], cosine, sine_part, *extra)


def unrope_kernel(back, raw, factors, scale, cosine, sine_part, scaled, inner, gain, *, stride):
    group = raw.shape[0]
    total = jnp.zeros((group, HDIM), jnp.float32)
    for head in range(raw.shape[1] // HDIM):
        span = slice(head * HDIM, (head + 1) * HDIM)
        start = stride * head * HDIM
        grad = back[:, start : start + HDIM].astype(jnp.float32)
        turn = turned(grad, cosine[...], -sine_part[...])
        product = turn * raw[:, span]
        gain[:, span] = jnp.sum(product * factors[...], axis=0, keepdims=True)
        scaled[:, span] = turn * scale[:, span]
        total = total + product * scale[:, span]
    sums = jnp.broadcast_to(jnp.sum(total, axis=1, keepdims=True), (group, HDIM))
    inner[...] = jnp.transpose(sums)[:1, :]


def rope_backward(back, raw, factors, scale, cosine, sine_part, stride):
    group, columns = raw.shape
    return pl.pallas_call(
        partial(unrope_kernel, stride=stride),
        out_shape=[
            jax.ShapeDtypeStruct((group, columns), jnp.float32),
            jax.ShapeDtypeStruct((1, group), jnp.float32),
            jax.ShapeDtypeStruct((1, columns), jnp.float32),
        ],
    )(back, raw, factors, scale[None], cosine, sine_part)


def raw_kernel(*refs, count, width, paired):
    scaled, raw, factors = refs[count : count + 3]
    out = refs[-1]
    inner = column_of(refs[:count]) / width
    factor = factors[:, :1]
    columns = raw.shape[1]
    slope = factor * factor * factor * inner
    for head in range(columns // HDIM):
        span = slice(head * HDIM, (head + 1) * HDIM)
        out[:, span] = (factor * scaled[:, span] - raw[:, span] * slope).astype(jnp.bfloat16)
        if paired:
            start = (2 * head + 1) * HDIM
            out[:, columns + head * HDIM : columns + (head + 1) * HDIM] = refs[count + 3][
                :, start : start + HDIM
            ]


def raw_backward(inner, scaled, raw, factors, pairs_back, width):
    group, columns = raw.shape
    paired = pairs_back is not None
    extra = (pairs_back,) if paired else ()
    return pl.pallas_call(
        partial(raw_kernel, count=len(inner), width=width, paired=paired),
        out_shape=jax.ShapeDtypeStruct((group, columns * (2 if paired else 1)), jnp.bfloat16),
    )(*inner, scaled, raw, factors, *extra)


def norm_kernel(*refs, count):
    scale, out = refs[count], refs[count + 1]
    rows, width = refs[0].shape
    for place in range(count):
        value = refs[place][...].astype(jnp.float32)
        square = jnp.sum(value * value, axis=1, keepdims=True)
        factor = lax.rsqrt(square / width + norm_eps)
        out[place * rows : (place + 1) * rows, :] = (value * factor * scale[...]).astype(
            jnp.bfloat16
        )


def norm_rows(pieces, scale):
    rows, width = pieces[0].shape
    return pl.pallas_call(
        partial(norm_kernel, count=len(pieces)),
        out_shape=jax.ShapeDtypeStruct((rows * len(pieces), width), jnp.bfloat16),
        name="norm_rows",
    )(*pieces, scale[None])


def project_kernel(normed, weight, raw, square, total):
    step = pl.program_id(0)

    @pl.when(step == 0)
    def start():
        total[...] = jnp.zeros_like(total)

    value = jnp.dot(normed[...], weight[...], preferred_element_type=jnp.float32)
    raw[...] = value
    for at in range(0, value.shape[1], HDIM):
        total[...] += value[:, at : at + HDIM] * value[:, at : at + HDIM]

    @pl.when(step == pl.num_programs(0) - 1)
    def finish():
        sums = jnp.sum(total[...], axis=1, keepdims=True)
        square[...] = jnp.transpose(jnp.broadcast_to(sums, total.shape))[:1, :]


def project(normed, weight, columns):
    group, width = normed.shape
    block = min(columns, 256)
    return pl.pallas_call(
        project_kernel,
        grid=(columns // block,),
        in_specs=[
            pl.BlockSpec((group, width), lambda step: (0, 0)),
            pl.BlockSpec((width, block), lambda step: (0, step)),
        ],
        out_specs=[
            pl.BlockSpec((group, block), lambda step: (0, step)),
            pl.BlockSpec((1, group), lambda step: (0, 0)),
        ],
        out_shape=[
            jax.ShapeDtypeStruct((group, columns), jnp.float32),
            jax.ShapeDtypeStruct((1, group), jnp.float32),
        ],
        scratch_shapes=[pltpu.VMEM((group, HDIM), jnp.float32)],
    )(normed, weight)


def slot_codes(routes, ordering, experts, capacity):
    expert_ids = jnp.arange(experts, dtype=jnp.int32)
    absent = jnp.int32(1 << 30)
    chosen = routes[:, :, None] == expert_ids[None, None, :]
    order = jnp.min(jnp.where(chosen, ordering[:, :, None], absent), axis=1)
    rank = jnp.sum((order[None, :, :] < order[:, None, :]).astype(jnp.int32), axis=1)
    return jnp.where((order < absent) & (rank < capacity), rank, -1)


def stream_layout(seq_lengths, stream_index):
    ends = jnp.cumsum(seq_lengths)
    starts = ends - seq_lengths
    passed = (stream_index[:, None] >= ends[None, :]).astype(jnp.int32)
    sequence = jnp.sum(passed, axis=1)
    owner = sequence[:, None] == jnp.arange(seq_lengths.shape[0], dtype=jnp.int32)[None, :]
    opening = jnp.sum(jnp.where(owner, starts[None, :], 0), axis=1)
    return (sequence, stream_index - opening)


def tile_lists(query_index, query_seq, key_index, key_seq, tile):
    query_tiles = query_index.shape[0] // tile
    key_tiles = key_index.shape[0] // tile
    query_marks = query_index.reshape(query_tiles, tile)
    query_seqs = query_seq.reshape(query_tiles, tile)
    key_marks = key_index.reshape(key_tiles, tile)
    key_seqs = key_seq.reshape(key_tiles, tile)
    early = jnp.min(key_marks, axis=1)[None, :] <= jnp.max(query_marks, axis=1)[:, None]
    above = jnp.max(key_seqs, axis=1)[None, :] >= jnp.min(query_seqs, axis=1)[:, None]
    below = jnp.min(key_seqs, axis=1)[None, :] <= jnp.max(query_seqs, axis=1)[:, None]
    live = (early & above & below).astype(jnp.int32)
    order = jnp.cumsum(live, axis=1) - 1
    numbers = jnp.arange(key_tiles, dtype=jnp.int32)
    hits = (order[:, :, None] == numbers[None, None, :]) & (live[:, :, None] > 0)
    listed = jnp.sum(jnp.where(hits, numbers[None, :, None], 0), axis=1)
    return (listed.astype(jnp.int32), jnp.sum(live, axis=1).astype(jnp.int32), live)


def spread(vector):
    return jnp.broadcast_to(vector[:, None], (vector.shape[0], 128))


def twice(value, count):
    return value if count == 1 else jnp.concatenate([value] * count, axis=1)


def forward_kernel(
    listed, counts, query, pairs, at, opening, key_at, attended, context, totals, total, acc, *, tile
):
    lanes = 128
    copies = tile // lanes
    factor = LOG2E / math.sqrt(HDIM)
    for step in range(query.shape[0] // tile):
        span = slice(step * tile, (step + 1) * tile)
        acc[...] = jnp.zeros_like(acc)
        total[...] = jnp.zeros_like(total)

        def visit(turn, carry):
            number = listed[step, turn]
            start = pl.multiple_of(number * tile, tile)
            scores = lax.dot_general(
                query[span, :],
                pairs[pl.ds(start, tile), :HDIM],
                (((1,), (1,)), ((), ())),
                preferred_element_type=jnp.float32,
            )
            marks = key_at[pl.ds(number, 1), :]
            allowed = (marks <= twice(at[span, :], copies)) & (
                marks >= twice(opening[span, :], copies)
            )
            expo = jnp.where(allowed, jnp.exp2(scores * factor), 0.0)
            partial_sum = expo[:, :lanes]
            for copy in range(1, copies):
                partial_sum = partial_sum + expo[:, copy * lanes : (copy + 1) * lanes]
            total[...] += partial_sum
            acc[...] += jnp.dot(
                expo.astype(jnp.bfloat16),
                pairs[pl.ds(start, tile), HDIM:],
                preferred_element_type=jnp.float32,
            )
            return carry

        lax.fori_loop(0, counts[step], visit, 0)
        full = jnp.sum(total[...], axis=1, keepdims=True)
        result = acc[...] / full
        attended[span, :] = result
        context[span, :] = result.astype(jnp.bfloat16)
        totals[span, :] = jnp.broadcast_to(full, (tile, lanes))


def attend_forward(queries, pairs, marks, tables, tile):
    group, columns = queries.shape
    total_rows = pairs.shape[0]
    listed, counts, _ = tables
    at, opening, key_at = marks[0], marks[1], marks[2]
    heads = columns // HDIM
    lane = lambda rows: pl.BlockSpec((rows, HDIM), lambda h, *refs: (0, h))
    wide = pl.BlockSpec((total_rows, 2 * HDIM), lambda h, *refs: (0, h))
    fixed = lambda array: pl.BlockSpec(array.shape, lambda h, *refs: (0, 0))
    return pl.pallas_call(
        partial(forward_kernel, tile=tile),
        grid_spec=pltpu.PrefetchScalarGridSpec(
            num_scalar_prefetch=2,
            grid=(heads,),
            in_specs=[
                lane(group),
                wide,
                fixed(at),
                fixed(opening),
                fixed(key_at),
            ],
            out_specs=[lane(group), lane(group), lane(group)],
            scratch_shapes=[
                pltpu.VMEM((tile, HDIM), jnp.float32),
                pltpu.VMEM((tile, HDIM), jnp.float32),
            ],
        ),
        out_shape=[
            jax.ShapeDtypeStruct((group, columns), jnp.float32),
            jax.ShapeDtypeStruct((group, columns), jnp.bfloat16),
            jax.ShapeDtypeStruct((group, columns), jnp.float32),
        ],
        name="attend_forward",
    )(listed, counts, queries, pairs, at, opening, key_at)


def backward_kernel(
    live,
    query,
    pairs,
    grad,
    attended,
    totals,
    at_row,
    opening_row,
    key_col,
    query_out,
    pairs_out,
    scaled,
    offset,
    query_acc,
    key_acc,
    value_acc,
    *,
    tile,
):
    copies = tile // 128
    steps = query.shape[0] // tile
    factor = 1.0 / math.sqrt(HDIM)
    grads = grad[...].astype(jnp.float32)
    scaled[...] = (grads / totals[...]).astype(jnp.bfloat16)
    sums = jnp.sum(grads * attended[...], axis=1, keepdims=True) / totals[...]
    offset[...] = jnp.transpose(sums)[:8, :]
    query_acc[...] = jnp.zeros_like(query_acc)

    def visit(number, carry):
        start = pl.multiple_of(number * tile, tile)
        window = pl.ds(start, tile)
        key_acc[...] = jnp.zeros_like(key_acc)
        value_acc[...] = jnp.zeros_like(value_acc)
        for step in range(steps):
            span = slice(step * tile, (step + 1) * tile)

            @pl.when(live[step, number] > 0)
            def unused():
                scores = lax.dot_general(
                    pairs[window, :HDIM],
                    query[span, :],
                    (((1,), (1,)), ((), ())),
                    preferred_element_type=jnp.float32,
                )
                marks = twice(key_col[window, :], copies)
                allowed = (marks <= at_row[:, span]) & (marks >= opening_row[:, span])
                expo = jnp.where(allowed, jnp.exp2(scores * (factor * LOG2E)), 0.0)
                inner = lax.dot_general(
                    pairs[window, HDIM:],
                    scaled[span, :],
                    (((1,), (1,)), ((), ())),
                    preferred_element_type=jnp.float32,
                )
                back = (expo * (inner - offset[0:1, span])).astype(jnp.bfloat16)
                key_acc[...] += jnp.dot(back, query[span, :], preferred_element_type=jnp.float32)
                value_acc[...] += jnp.dot(
                    expo.astype(jnp.bfloat16), scaled[span, :], preferred_element_type=jnp.float32
                )
                query_acc[span, :] += lax.dot_general(
                    back,
                    pairs[window, :HDIM],
                    (((0,), (0,)), ((), ())),
                    preferred_element_type=jnp.float32,
                )

        pairs_out[window, :HDIM] = (key_acc[...] * factor).astype(jnp.bfloat16)
        pairs_out[window, HDIM:] = value_acc[...].astype(jnp.bfloat16)
        return carry

    lax.fori_loop(0, pairs.shape[0] // tile, visit, 0)
    query_out[...] = (query_acc[...] * factor).astype(jnp.bfloat16)


def attend_backward(queries, pairs, grads, attended, totals, marks, tables, tile):
    group, columns = queries.shape
    total_rows = pairs.shape[0]
    live = tables[2]
    at_row, opening_row, key_col = marks[3], marks[4], marks[5]
    heads = columns // HDIM
    lane = lambda rows: pl.BlockSpec((rows, HDIM), lambda h, *refs: (0, h))
    wide = pl.BlockSpec((total_rows, 2 * HDIM), lambda h, *refs: (0, h))
    fixed = lambda array: pl.BlockSpec(array.shape, lambda h, *refs: (0, 0))
    return pl.pallas_call(
        partial(backward_kernel, tile=tile),
        grid_spec=pltpu.PrefetchScalarGridSpec(
            num_scalar_prefetch=1,
            grid=(heads,),
            in_specs=[
                lane(group),
                wide,
                lane(group),
                lane(group),
                lane(group),
                fixed(at_row),
                fixed(opening_row),
                fixed(key_col),
            ],
            out_specs=[lane(group), wide],
            scratch_shapes=[
                pltpu.VMEM((group, HDIM), jnp.bfloat16),
                pltpu.VMEM((8, group), jnp.float32),
                pltpu.VMEM((group, HDIM), jnp.float32),
                pltpu.VMEM((tile, HDIM), jnp.float32),
                pltpu.VMEM((tile, HDIM), jnp.float32),
            ],
        ),
        out_shape=[
            jax.ShapeDtypeStruct((group, columns), jnp.bfloat16),
            jax.ShapeDtypeStruct((total_rows, 2 * columns), jnp.bfloat16),
        ],
        name="attend_backward",
    )(live, queries, pairs, grads, attended, totals, at_row, opening_row, key_col)


def attend_marks(query_index, query_start, key_index, tile):
    return (
        spread(query_index),
        spread(query_start),
        key_index.reshape(-1, tile),
        query_index[None, :],
        query_start[None, :],
        spread(key_index),
    )


def exchange(array, offset):
    count = lax.axis_size("head")
    return lax.ppermute(array, "head", [(at, at ^ offset) for at in range(count)])


def head_pieces(array):
    return [array] + [exchange(array, offset) for offset in range(1, lax.axis_size("head"))]


def head_turn(pieces):
    return [pieces[0]] + [exchange(piece, at + 1) for at, piece in enumerate(pieces[1:])]


def add_all(pieces):
    total = pieces[0].astype(f32)
    for piece in pieces[1:]:
        total = total + piece.astype(f32)
    return total


def bit_order(turn):
    count = lax.axis_size("head").bit_length() - 1
    return [1 << ((turn + step) % count) for step in range(count)]


def gather_pieces(array, turn):
    pieces = {0: array}
    for bit in bit_order(turn):
        for offset in list(pieces):
            pieces[offset ^ bit] = exchange(pieces[offset], bit)
    return [pieces[offset] for offset in range(len(pieces))]


def scatter_pieces(pieces, turn):
    held = dict(enumerate(pieces))
    for bit in bit_order(turn):
        for offset in [item for item in held if item & bit]:
            piece = held.pop(offset).astype(bf16)
            arrived = exchange(piece, bit)
            held[offset ^ bit] = held[offset ^ bit].astype(f32) + arrived.astype(f32)
    return held[0]


def xor_order(array, axis):
    count = lax.axis_size("head")
    at = lax.axis_index("head")
    size = array.shape[axis] // count
    chunks = [
        lax.dynamic_slice_in_dim(array, (at ^ offset) * size, size, axis) for offset in range(count)
    ]
    return chunks


def xor_chunks(array, axis):
    return jnp.concatenate(xor_order(array, axis), axis=axis)


def absolute(pieces):
    at = lax.axis_index("head")
    result = []
    for place in range(len(pieces)):
        value = pieces[0]
        for offset in range(1, len(pieces)):
            value = jnp.where(at == place ^ offset, pieces[offset], value)
        result.append(value)
    return result


def move_rows(array, outer, inner, part):
    shaped = array.reshape(outer, inner, part, array.shape[1])
    return jnp.transpose(shaped, (1, 0, 2, 3)).reshape(array.shape)


def move_columns(array, outer, inner, part):
    shaped = array.reshape(array.shape[0], outer, inner, part)
    return jnp.transpose(shaped, (0, 2, 1, 3)).reshape(array.shape)


def layer(
    tokens,
    query_weight,
    key_weight,
    value_weight,
    output_weight,
    mixing_gain,
    query_gain,
    key_gain,
    routing_gain,
    router_weight,
    gate_weight,
    up_weight,
    down_weight,
    seq_lengths,
    dealt_order,
    expert_routes,
    slot_order,
    cotangent,
):
    heads_axis = lax.axis_size("head")
    blocks = lax.axis_size("blk")
    head_at = lax.axis_index("head")
    block_at = lax.axis_index("blk")
    rows, width = tokens.shape
    picks = expert_routes.shape[1]
    total_rows = dealt_order.shape[0]
    group = rows * heads_axis
    columns = width // heads_axis
    part = query_weight.shape[0]
    head_size = HDIM
    experts = router_weight.shape[1]
    local_experts = gate_weight.shape[0]
    capacity = 5 * rows * picks // (4 * experts)
    slots = blocks * capacity

    slices = [
        jnp.concatenate(chunks, axis=1)
        for chunks in zip(
            xor_order(key_weight, 1), xor_order(value_weight, 1), xor_order(query_weight, 1)
        )
    ]
    slices = head_turn(slices)
    output_rows = lax.all_gather(output_weight, "blk", axis=0, tiled=True)
    token_pieces = head_pieces(tokens)
    rows_here = jnp.stack(absolute(slices)).reshape(heads_axis * part, 3 * columns)
    pair_full = lax.all_gather(rows_here[:, : 2 * columns], "blk", axis=0, tiled=True)
    pair_full = move_rows(pair_full, blocks, heads_axis, part)
    query_full = lax.all_gather(rows_here[:, 2 * columns :], "blk", axis=0, tiled=True)
    query_full = move_rows(query_full, blocks, heads_axis, part)
    cot_all = lax.all_gather(cotangent, "blk", axis=0, tiled=True).reshape(blocks, rows, width)

    small = jnp.concatenate(
        [
            mixing_gain[:, None],
            query_gain[:, None],
            key_gain[:, None],
            routing_gain[:, None],
            router_weight,
        ],
        axis=1,
    ).reshape(1, -1)
    codes = slot_codes(expert_routes, slot_order, experts, capacity).astype(bf16)
    sizes = small.shape[1]
    small = lax.all_gather(
        jnp.concatenate([small, codes.reshape(1, -1)], axis=1), "blk", axis=0, tiled=True
    )
    codes = small[:, sizes:].reshape(blocks, rows, experts).astype(jnp.int32)
    small = small[:, :sizes]
    small = jnp.stack(absolute(head_pieces(small))).reshape(width, 4 + experts)
    mixing_scale = small[:, 0].astype(f32)
    routing_scale = small[:, 3].astype(f32)
    query_scale = lax.dynamic_slice_in_dim(small[:, 1], head_at * columns, columns).astype(f32)
    key_scale = lax.dynamic_slice_in_dim(small[:, 2], head_at * columns, columns).astype(f32)
    router_full = small[:, 4:]
    codes_here = lax.dynamic_slice_in_dim(codes, block_at * local_experts, local_experts, 2)

    key_index = jnp.transpose(
        xor_chunks(dealt_order.reshape(heads_axis, blocks, rows), 0), (1, 0, 2)
    ).reshape(total_rows)
    key_seq = stream_layout(seq_lengths, key_index)[0]
    query_index = lax.dynamic_slice_in_dim(key_index, block_at * group, group)
    query_seq, query_position = stream_layout(seq_lengths, query_index)
    cosine, sine_part = rope_tables(query_position, head_size)
    tables = tile_lists(query_index, query_seq, key_index, key_seq, TILE)
    marks = attend_marks(query_index, query_index - query_position, key_index, TILE)

    gates, ups, downs = (
        [gather_pieces(weight[item], item) for item in range(local_experts)]
        for weight in (gate_weight, up_weight, down_weight)
    )

    normed = norm_rows(token_pieces, mixing_scale)
    normed_moved = move_columns(normed, heads_axis, blocks, part)
    key_raw, key_square = project(normed, pair_full, columns)
    value_heads = jnp.dot(normed, pair_full[:, columns:], preferred_element_type=f32)
    value_heads = value_heads.astype(bf16)
    key_squares = head_pieces(key_square)
    pairs, key_factor = rope_forward(
        key_squares, key_raw, key_scale, cosine, sine_part, value_heads, width
    )
    query_raw, query_square = project(normed, query_full, columns)
    query_squares = head_pieces(query_square)
    query_heads, query_factor = rope_forward(
        query_squares, query_raw, query_scale, cosine, sine_part, None, width
    )
    pairs_all = lax.all_gather(pairs, "blk", axis=0, tiled=True)
    attended, context, totals = attend_forward(query_heads, pairs_all, marks, tables, TILE)
    branch = jnp.dot(context, output_rows, preferred_element_type=f32).astype(bf16)
    branch = head_turn([branch[piece * rows : (piece + 1) * rows] for piece in range(heads_axis)])
    own_tokens = tokens.astype(f32)
    middle = own_tokens + add_all(branch)
    middle_factor = rms_factor(jnp.sum(middle * middle, axis=-1, keepdims=True), width)
    routed = (middle * middle_factor * routing_scale).astype(bf16)

    routed_all = lax.all_gather(xor_chunks(routed, 1), "blk", axis=0, tiled=True)
    probs = jax.nn.softmax(jnp.dot(routed, router_full, preferred_element_type=f32), axis=-1)
    probs_all = jax.nn.softmax(
        jnp.dot(routed_all, xor_chunks(router_full, 0), preferred_element_type=f32), axis=-1
    )
    weight_here = lax.dynamic_slice_in_dim(
        probs_all, block_at * local_experts, local_experts, 1
    ).reshape(blocks, rows, local_experts)
    routed_all = routed_all.reshape(blocks, rows, width)
    slot_ids = jnp.arange(capacity, dtype=jnp.int32)
    combined = 0.0
    incoming = 0.0
    weight_grads = []
    stores = []
    for item in range(local_experts):
        placed = codes_here[:, None, :, item] == slot_ids[None, :, None]
        place = placed.astype(bf16)
        slot_weight = jnp.sum(
            jnp.where(placed, weight_here[:, None, :, item], 0.0), axis=-1
        ).reshape(slots, 1)
        arrived = jnp.einsum("srt,std->srd", place, routed_all).reshape(slots, width)
        arrived_cot = jnp.einsum("srt,std->srd", place, cot_all).reshape(slots, width)
        gate_all = jnp.concatenate(gates[item], axis=0)
        up_all = jnp.concatenate(ups[item], axis=0)
        down_all = jnp.concatenate(downs[item], axis=0)
        gate = jnp.dot(arrived, gate_all, preferred_element_type=f32)
        upward = jnp.dot(arrived, up_all, preferred_element_type=f32)
        sigmoid = jax.nn.sigmoid(gate)
        active = xor_chunks((gate * sigmoid * upward).astype(bf16), 1)
        produced = jnp.dot(active, down_all, preferred_element_type=f32).astype(bf16)
        cot_float = arrived_cot.astype(f32)
        produced_float = produced.astype(f32)
        weighted = (slot_weight * produced_float).astype(bf16).reshape(blocks, capacity, width)
        combined = combined + jnp.einsum(
            "srt,srd->std", place, weighted, preferred_element_type=f32
        )
        slot_grad = jnp.sum(cot_float * produced_float, axis=-1).reshape(blocks, capacity, 1)
        weight_grads.append(jnp.sum(jnp.where(placed, slot_grad, 0.0), axis=1))
        produced_grad = (slot_weight * cot_float).astype(bf16)
        active_grad = xor_chunks(
            jnp.dot(produced_grad, down_all.T, preferred_element_type=f32), 1
        )
        gate_grad = (active_grad * upward * sigmoid * (1.0 + gate * (1.0 - sigmoid))).astype(bf16)
        up_grad = (active_grad * (gate * sigmoid)).astype(bf16)
        coming = jnp.dot(gate_grad, gate_all.T, preferred_element_type=f32)
        coming = coming + jnp.dot(up_grad, up_all.T, preferred_element_type=f32)
        coming = coming.astype(bf16).reshape(blocks, capacity, width)
        incoming = incoming + jnp.einsum(
            "srt,srd->std", place, coming, preferred_element_type=f32
        )
        stores.append((arrived, produced_grad, active, gate_grad, up_grad))
    routed_grad = lax.psum_scatter(
        incoming.astype(bf16).reshape(blocks * rows, width),
        "blk",
        scatter_dimension=0,
        tiled=True,
    )
    combined = lax.psum_scatter(
        combined.astype(bf16).reshape(blocks * rows, width),
        "blk",
        scatter_dimension=0,
        tiled=True,
    )
    block_output = (middle + combined.astype(f32)).astype(bf16)
    prob_grad = lax.all_to_all(
        jnp.stack(weight_grads, axis=2), "blk", split_axis=0, concat_axis=2, tiled=True
    ).reshape(rows, experts)

    def pieces_of(left, right):
        size = left.shape[1] // heads_axis
        return [
            lax.optimization_barrier(
                jnp.dot(
                    left[:, offset * size : (offset + 1) * size].T,
                    right,
                    preferred_element_type=f32,
                ).astype(bf16)
            )
            for offset in range(heads_axis)
        ]

    down_out, gate_out, up_out = (
        jnp.stack(
            [
                scatter_pieces(pieces_of(store[left], store[right]), item)
                for item, store in enumerate(stores)
            ]
        ).astype(f32)
        for left, right in ((2, 1), (0, 3), (0, 4))
    )

    logit_grad = (
        probs * (prob_grad - jnp.sum(probs * prob_grad, axis=1, keepdims=True))
    ).astype(bf16)
    router_sum = jnp.dot(routed.T, logit_grad, preferred_element_type=f32)
    routed_grad = xor_chunks(routed_grad, 1).astype(f32) + jnp.dot(
        logit_grad, router_full.T, preferred_element_type=f32
    )
    scaled = routed_grad * routing_scale
    inner = jnp.mean(scaled * middle, axis=-1, keepdims=True)
    middle_grad = (
        cotangent.astype(f32) + middle_factor * scaled - middle * (middle_factor**3 * inner)
    )
    routing_sum = jnp.sum(routed_grad * middle * middle_factor, axis=0)

    branch_grad = head_pieces(middle_grad.astype(bf16))
    branch_grad = jnp.concatenate(branch_grad, axis=0)
    context_grad = jnp.dot(branch_grad, output_rows.T, preferred_element_type=f32).astype(bf16)
    output_sum = jnp.dot(context.T, branch_grad, preferred_element_type=f32).astype(bf16)
    output_out = lax.psum_scatter(output_sum, "blk", scatter_dimension=0, tiled=True)
    query_back, pairs_back = attend_backward(
        query_heads, pairs_all, context_grad, attended, totals, marks, tables, TILE
    )
    pairs_back = lax.psum_scatter(pairs_back, "blk", scatter_dimension=0, tiled=True)
    query_scaled, query_inner, querynorm_sum = rope_backward(
        query_back, query_raw, query_factor, query_scale, cosine, sine_part, 1
    )
    query_inner = head_pieces(query_inner)
    query_raw_grad = raw_backward(query_inner, query_scaled, query_raw, query_factor, None, width)
    query_sum = jnp.dot(normed_moved.T, query_raw_grad, preferred_element_type=f32).astype(bf16)
    query_sum = lax.psum_scatter(query_sum, "blk", scatter_dimension=0, tiled=True)
    normed_part = jnp.dot(query_raw_grad, query_full.T, preferred_element_type=f32)
    key_scaled, key_inner, keynorm_sum = rope_backward(
        pairs_back, key_raw, key_factor, key_scale, cosine, sine_part, 2
    )
    key_inner = head_pieces(key_inner)
    pair_grad = raw_backward(key_inner, key_scaled, key_raw, key_factor, pairs_back, width)
    pair_sum = jnp.dot(normed_moved.T, pair_grad, preferred_element_type=f32).astype(bf16)
    pair_sum = lax.psum_scatter(pair_sum, "blk", scatter_dimension=0, tiled=True)
    normed_part = normed_part + jnp.dot(pair_grad, pair_full.T, preferred_element_type=f32)
    normed_part = normed_part.astype(bf16)
    normed_part = head_turn(
        [normed_part[piece * rows : (piece + 1) * rows] for piece in range(heads_axis)]
    )
    normed_grad = add_all(normed_part)
    own_factor = rms_factor(jnp.sum(own_tokens * own_tokens, axis=-1, keepdims=True), width)
    scaled = normed_grad * mixing_scale
    inner = jnp.mean(scaled * own_tokens, axis=-1, keepdims=True)
    tokens_grad = middle_grad + own_factor * scaled - own_tokens * (own_factor**3 * inner)
    mixing_sum = jnp.sum(normed_grad * own_tokens * own_factor, axis=0)

    def turned_back(array):
        return jnp.stack(
            [
                jnp.concatenate(absolute(list(pieces)), axis=1).astype(f32)
                for pieces in zip(
                    *(
                        [piece[:, at : at + columns] for at in range(0, piece.shape[1], columns)]
                        for piece in head_turn(xor_order(array, 0))
                    )
                )
            ]
        )

    query_out = turned_back(query_sum)[0]
    pair_out = turned_back(pair_sum)

    blank = jnp.zeros((heads_axis, columns), f32)
    query_line = lax.dynamic_update_slice(blank, querynorm_sum, (head_at, 0)).reshape(width)
    key_line = lax.dynamic_update_slice(blank, keynorm_sum, (head_at, 0)).reshape(width)
    lines = jnp.concatenate(
        [
            mixing_sum[:, None],
            query_line[:, None],
            key_line[:, None],
            routing_sum[:, None],
            router_sum,
        ],
        axis=1,
    ).reshape(heads_axis, -1)
    lines = add_all(head_turn(xor_order(lines, 0)))
    lines = lax.all_to_all(lines.reshape(blocks, -1), "blk", 0, 0, tiled=True)
    lines = jnp.sum(lines, axis=0).reshape(part, 4 + experts)
    return (
        block_output,
        tokens_grad,
        query_out,
        pair_out[0],
        pair_out[1],
        output_out.astype(f32),
        lines[:, 0],
        lines[:, 1],
        lines[:, 2],
        lines[:, 3],
        lines[:, 4:],
        gate_out,
        up_out,
        down_out,
    )


def solution(mesh):
    in_specs = (
        P(("head", "blk"), None),
        P(("head", "blk"), None),
        P(("head", "blk"), None),
        P(("head", "blk"), None),
        P(("head", "blk"), None),
        P(("head", "blk")),
        P(("head", "blk")),
        P(("head", "blk")),
        P(("head", "blk")),
        P(("head", "blk"), None),
        P("blk", "head", None),
        P("blk", "head", None),
        P("blk", "head", None),
        P(),
        P(),
        P(("head", "blk"), None),
        P(("head", "blk"), None),
        P(("head", "blk"), None),
    )
    out_specs = (
        P(("head", "blk"), None),
        P(("head", "blk"), None),
        P(("head", "blk"), None),
        P(("head", "blk"), None),
        P(("head", "blk"), None),
        P(("head", "blk"), None),
        P(("head", "blk")),
        P(("head", "blk")),
        P(("head", "blk")),
        P(("head", "blk")),
        P(("head", "blk"), None),
        P("blk", "head", None),
        P("blk", "head", None),
        P("blk", "head", None),
    )
    return jax.shard_map(layer, mesh=mesh, in_specs=in_specs, out_specs=out_specs, check_vma=False)
```

```python
from functools import partial
import math

import jax
import jax.numpy as jnp
import numpy as np
from jax import lax
from jax.experimental import pallas as pl
from jax.experimental.pallas import tpu as pltpu
from jax.sharding import PartitionSpec as P


HDIM = 128
TILE = 256
LOG2E = 1.4426950408889634
norm_eps = 1e-05
rope_base = 10000.0
f32 = jnp.float32
bf16 = jnp.bfloat16


def rms_factor(square_sum, width):
    return lax.rsqrt(square_sum / width + norm_eps)


def rope_tables(position, head_size):
    half = head_size // 2
    freqs = rope_base ** (-(np.arange(half, dtype=np.float64) * 2.0) / head_size)
    angles = position.astype(f32)[:, None] * jnp.asarray(freqs.astype(np.float32))[None, :]
    cosine = jnp.cos(angles)
    sine_part = jnp.sin(angles)
    return (
        jnp.concatenate([cosine, cosine], axis=1),
        jnp.concatenate([-sine_part, sine_part], axis=1),
    )


def column_of(pieces):
    count = len(pieces)
    rows = pieces[0].shape[1] // count
    total = pieces[0][...]
    for offset in range(1, count):
        parts = [
            pieces[offset][:, (at ^ offset) * rows : ((at ^ offset) + 1) * rows]
            for at in range(count)
        ]
        total = total + jnp.concatenate(parts, axis=1)
    return jnp.transpose(jnp.broadcast_to(total, (8, total.shape[1])))[:, :1]


def turned(value, cosine, sine_part):
    return value * cosine + pltpu.roll(value, HDIM // 2, 1) * sine_part


def rope_kernel(*refs, count, width, paired):
    squares = refs[:count]
    raw, scale, cosine, sine_part = refs[count : count + 4]
    out, factors = refs[-2:]
    factor = lax.rsqrt(column_of(squares) / width + norm_eps)
    factors[...] = jnp.broadcast_to(factor, factors.shape)
    for head in range(raw.shape[1] // HDIM):
        span = slice(head * HDIM, (head + 1) * HDIM)
        value = turned(raw[:, span] * factor * scale[:, span], cosine[...], sine_part[...])
        if paired:
            start = 2 * head * HDIM
            out[:, start : start + HDIM] = value.astype(jnp.bfloat16)
            out[:, start + HDIM : start + 2 * HDIM] = refs[count + 4][:, span]
        else:
            out[:, span] = value.astype(jnp.bfloat16)


def rope_forward(squares, raw, scale, cosine, sine_part, values, width):
    group, columns = raw.shape
    paired = values is not None
    extra = (values,) if paired else ()
    return pl.pallas_call(
        partial(rope_kernel, count=len(squares), width=width, paired=paired),
        out_shape=[
            jax.ShapeDtypeStruct((group, columns * (2 if paired else 1)), jnp.bfloat16),
            jax.ShapeDtypeStruct((group, HDIM), jnp.float32),
        ],
    )(*squares, raw, scale[None], cosine, sine_part, *extra)


def unrope_kernel(back, raw, factors, scale, cosine, sine_part, scaled, inner, gain, *, stride):
    group = raw.shape[0]
    total = jnp.zeros((group, HDIM), jnp.float32)
    for head in range(raw.shape[1] // HDIM):
        span = slice(head * HDIM, (head + 1) * HDIM)
        start = stride * head * HDIM
        grad = back[:, start : start + HDIM].astype(jnp.float32)
        turn = turned(grad, cosine[...], -sine_part[...])
        product = turn * raw[:, span]
        gain[:, span] = jnp.sum(product * factors[...], axis=0, keepdims=True)
        scaled[:, span] = turn * scale[:, span]
        total = total + product * scale[:, span]
    sums = jnp.broadcast_to(jnp.sum(total, axis=1, keepdims=True), (group, HDIM))
    inner[...] = jnp.transpose(sums)[:1, :]


def rope_backward(back, raw, factors, scale, cosine, sine_part, stride):
    group, columns = raw.shape
    return pl.pallas_call(
        partial(unrope_kernel, stride=stride),
        out_shape=[
            jax.ShapeDtypeStruct((group, columns), jnp.float32),
            jax.ShapeDtypeStruct((1, group), jnp.float32),
            jax.ShapeDtypeStruct((1, columns), jnp.float32),
        ],
    )(back, raw, factors, scale[None], cosine, sine_part)


def raw_kernel(*refs, count, width, paired):
    scaled, raw, factors = refs[count : count + 3]
    out = refs[-1]
    inner = column_of(refs[:count]) / width
    factor = factors[:, :1]
    columns = raw.shape[1]
    slope = factor * factor * factor * inner
    for head in range(columns // HDIM):
        span = slice(head * HDIM, (head + 1) * HDIM)
        out[:, span] = (factor * scaled[:, span] - raw[:, span] * slope).astype(jnp.bfloat16)
        if paired:
            start = (2 * head + 1) * HDIM
            out[:, columns + head * HDIM : columns + (head + 1) * HDIM] = refs[count + 3][
                :, start : start + HDIM
            ]


def raw_backward(inner, scaled, raw, factors, pairs_back, width):
    group, columns = raw.shape
    paired = pairs_back is not None
    extra = (pairs_back,) if paired else ()
    return pl.pallas_call(
        partial(raw_kernel, count=len(inner), width=width, paired=paired),
        out_shape=jax.ShapeDtypeStruct((group, columns * (2 if paired else 1)), jnp.bfloat16),
    )(*inner, scaled, raw, factors, *extra)


def norm_kernel(*refs, count):
    scale, out = refs[count], refs[count + 1]
    rows, width = refs[0].shape
    for place in range(count):
        value = refs[place][...].astype(jnp.float32)
        square = jnp.sum(value * value, axis=1, keepdims=True)
        factor = lax.rsqrt(square / width + norm_eps)
        out[place * rows : (place + 1) * rows, :] = (value * factor * scale[...]).astype(
            jnp.bfloat16
        )


def norm_rows(pieces, scale):
    rows, width = pieces[0].shape
    return pl.pallas_call(
        partial(norm_kernel, count=len(pieces)),
        out_shape=jax.ShapeDtypeStruct((rows * len(pieces), width), jnp.bfloat16),
        name="norm_rows",
    )(*pieces, scale[None])


def project_kernel(normed, weight, raw, square, total):
    step = pl.program_id(0)

    @pl.when(step == 0)
    def start():
        total[...] = jnp.zeros_like(total)

    value = jnp.dot(normed[...], weight[...], preferred_element_type=jnp.float32)
    raw[...] = value
    for at in range(0, value.shape[1], HDIM):
        total[...] += value[:, at : at + HDIM] * value[:, at : at + HDIM]

    @pl.when(step == pl.num_programs(0) - 1)
    def finish():
        sums = jnp.sum(total[...], axis=1, keepdims=True)
        square[...] = jnp.transpose(jnp.broadcast_to(sums, total.shape))[:1, :]


def project(normed, weight, columns):
    group, width = normed.shape
    block = min(columns, 256)
    return pl.pallas_call(
        project_kernel,
        grid=(columns // block,),
        in_specs=[
            pl.BlockSpec((group, width), lambda step: (0, 0)),
            pl.BlockSpec((width, block), lambda step: (0, step)),
        ],
        out_specs=[
            pl.BlockSpec((group, block), lambda step: (0, step)),
            pl.BlockSpec((1, group), lambda step: (0, 0)),
        ],
        out_shape=[
            jax.ShapeDtypeStruct((group, columns), jnp.float32),
            jax.ShapeDtypeStruct((1, group), jnp.float32),
        ],
        scratch_shapes=[pltpu.VMEM((group, HDIM), jnp.float32)],
    )(normed, weight)


def slot_codes(routes, ordering, experts, capacity):
    expert_ids = jnp.arange(experts, dtype=jnp.int32)
    absent = jnp.int32(1 << 30)
    chosen = routes[:, :, None] == expert_ids[None, None, :]
    order = jnp.min(jnp.where(chosen, ordering[:, :, None], absent), axis=1)
    rank = jnp.sum((order[None, :, :] < order[:, None, :]).astype(jnp.int32), axis=1)
    return jnp.where((order < absent) & (rank < capacity), rank, -1)


def stream_layout(seq_lengths, stream_index):
    ends = jnp.cumsum(seq_lengths)
    starts = ends - seq_lengths
    passed = (stream_index[:, None] >= ends[None, :]).astype(jnp.int32)
    sequence = jnp.sum(passed, axis=1)
    owner = sequence[:, None] == jnp.arange(seq_lengths.shape[0], dtype=jnp.int32)[None, :]
    opening = jnp.sum(jnp.where(owner, starts[None, :], 0), axis=1)
    return (sequence, stream_index - opening)


def tile_lists(query_index, query_seq, key_index, key_seq, tile):
    query_tiles = query_index.shape[0] // tile
    key_tiles = key_index.shape[0] // tile
    query_marks = query_index.reshape(query_tiles, tile)
    query_seqs = query_seq.reshape(query_tiles, tile)
    key_marks = key_index.reshape(key_tiles, tile)
    key_seqs = key_seq.reshape(key_tiles, tile)
    early = jnp.min(key_marks, axis=1)[None, :] <= jnp.max(query_marks, axis=1)[:, None]
    above = jnp.max(key_seqs, axis=1)[None, :] >= jnp.min(query_seqs, axis=1)[:, None]
    below = jnp.min(key_seqs, axis=1)[None, :] <= jnp.max(query_seqs, axis=1)[:, None]
    live = (early & above & below).astype(jnp.int32)
    order = jnp.cumsum(live, axis=1) - 1
    numbers = jnp.arange(key_tiles, dtype=jnp.int32)
    hits = (order[:, :, None] == numbers[None, None, :]) & (live[:, :, None] > 0)
    listed = jnp.sum(jnp.where(hits, numbers[None, :, None], 0), axis=1)
    return (listed.astype(jnp.int32), jnp.sum(live, axis=1).astype(jnp.int32), live)


def spread(vector):
    return jnp.broadcast_to(vector[:, None], (vector.shape[0], 128))


def twice(value, count):
    return value if count == 1 else jnp.concatenate([value] * count, axis=1)


def forward_kernel(
    listed, counts, query, pairs, at, opening, key_at, attended, context, totals, total, acc, *, tile
):
    lanes = 128
    copies = tile // lanes
    factor = LOG2E / math.sqrt(HDIM)
    for step in range(query.shape[0] // tile):
        span = slice(step * tile, (step + 1) * tile)
        acc[...] = jnp.zeros_like(acc)
        total[...] = jnp.zeros_like(total)

        def visit(turn, carry):
            number = listed[step, turn]
            start = pl.multiple_of(number * tile, tile)
            scores = lax.dot_general(
                query[span, :],
                pairs[pl.ds(start, tile), :HDIM],
                (((1,), (1,)), ((), ())),
                preferred_element_type=jnp.float32,
            )
            marks = key_at[pl.ds(number, 1), :]
            allowed = (marks <= twice(at[span, :], copies)) & (
                marks >= twice(opening[span, :], copies)
            )
            expo = jnp.where(allowed, jnp.exp2(scores * factor), 0.0)
            partial_sum = expo[:, :lanes]
            for copy in range(1, copies):
                partial_sum = partial_sum + expo[:, copy * lanes : (copy + 1) * lanes]
            total[...] += partial_sum
            acc[...] += jnp.dot(
                expo.astype(jnp.bfloat16),
                pairs[pl.ds(start, tile), HDIM:],
                preferred_element_type=jnp.float32,
            )
            return carry

        lax.fori_loop(0, counts[step], visit, 0)
        full = jnp.sum(total[...], axis=1, keepdims=True)
        result = acc[...] / full
        attended[span, :] = result
        context[span, :] = result.astype(jnp.bfloat16)
        totals[span, :] = jnp.broadcast_to(full, (tile, lanes))


def attend_forward(queries, pairs, marks, tables, tile):
    group, columns = queries.shape
    total_rows = pairs.shape[0]
    listed, counts, _ = tables
    at, opening, key_at = marks[0], marks[1], marks[2]
    heads = columns // HDIM
    lane = lambda rows: pl.BlockSpec((rows, HDIM), lambda h, *refs: (0, h))
    wide = pl.BlockSpec((total_rows, 2 * HDIM), lambda h, *refs: (0, h))
    fixed = lambda array: pl.BlockSpec(array.shape, lambda h, *refs: (0, 0))
    return pl.pallas_call(
        partial(forward_kernel, tile=tile),
        grid_spec=pltpu.PrefetchScalarGridSpec(
            num_scalar_prefetch=2,
            grid=(heads,),
            in_specs=[
                lane(group),
                wide,
                fixed(at),
                fixed(opening),
                fixed(key_at),
            ],
            out_specs=[lane(group), lane(group), lane(group)],
            scratch_shapes=[
                pltpu.VMEM((tile, HDIM), jnp.float32),
                pltpu.VMEM((tile, HDIM), jnp.float32),
            ],
        ),
        out_shape=[
            jax.ShapeDtypeStruct((group, columns), jnp.float32),
            jax.ShapeDtypeStruct((group, columns), jnp.bfloat16),
            jax.ShapeDtypeStruct((group, columns), jnp.float32),
        ],
        name="attend_forward",
    )(listed, counts, queries, pairs, at, opening, key_at)


def backward_kernel(
    live,
    query,
    pairs,
    grad,
    attended,
    totals,
    at_row,
    opening_row,
    key_col,
    query_out,
    pairs_out,
    scaled,
    offset,
    query_acc,
    key_acc,
    value_acc,
    *,
    tile,
):
    copies = tile // 128
    steps = query.shape[0] // tile
    factor = 1.0 / math.sqrt(HDIM)
    grads = grad[...].astype(jnp.float32)
    scaled[...] = (grads / totals[...]).astype(jnp.bfloat16)
    sums = jnp.sum(grads * attended[...], axis=1, keepdims=True) / totals[...]
    offset[...] = jnp.transpose(sums)[:8, :]
    query_acc[...] = jnp.zeros_like(query_acc)

    def visit(number, carry):
        start = pl.multiple_of(number * tile, tile)
        window = pl.ds(start, tile)
        key_acc[...] = jnp.zeros_like(key_acc)
        value_acc[...] = jnp.zeros_like(value_acc)
        for step in range(steps):
            span = slice(step * tile, (step + 1) * tile)

            @pl.when(live[step, number] > 0)
            def unused():
                scores = lax.dot_general(
                    pairs[window, :HDIM],
                    query[span, :],
                    (((1,), (1,)), ((), ())),
                    preferred_element_type=jnp.float32,
                )
                marks = twice(key_col[window, :], copies)
                allowed = (marks <= at_row[:, span]) & (marks >= opening_row[:, span])
                expo = jnp.where(allowed, jnp.exp2(scores * (factor * LOG2E)), 0.0)
                inner = lax.dot_general(
                    pairs[window, HDIM:],
                    scaled[span, :],
                    (((1,), (1,)), ((), ())),
                    preferred_element_type=jnp.float32,
                )
                back = (expo * (inner - offset[0:1, span])).astype(jnp.bfloat16)
                key_acc[...] += jnp.dot(back, query[span, :], preferred_element_type=jnp.float32)
                value_acc[...] += jnp.dot(
                    expo.astype(jnp.bfloat16), scaled[span, :], preferred_element_type=jnp.float32
                )
                query_acc[span, :] += lax.dot_general(
                    back,
                    pairs[window, :HDIM],
                    (((0,), (0,)), ((), ())),
                    preferred_element_type=jnp.float32,
                )

        pairs_out[window, :HDIM] = (key_acc[...] * factor).astype(jnp.bfloat16)
        pairs_out[window, HDIM:] = value_acc[...].astype(jnp.bfloat16)
        return carry

    lax.fori_loop(0, pairs.shape[0] // tile, visit, 0)
    query_out[...] = (query_acc[...] * factor).astype(jnp.bfloat16)


def attend_backward(queries, pairs, grads, attended, totals, marks, tables, tile):
    group, columns = queries.shape
    total_rows = pairs.shape[0]
    live = tables[2]
    at_row, opening_row, key_col = marks[3], marks[4], marks[5]
    heads = columns // HDIM
    lane = lambda rows: pl.BlockSpec((rows, HDIM), lambda h, *refs: (0, h))
    wide = pl.BlockSpec((total_rows, 2 * HDIM), lambda h, *refs: (0, h))
    fixed = lambda array: pl.BlockSpec(array.shape, lambda h, *refs: (0, 0))
    return pl.pallas_call(
        partial(backward_kernel, tile=tile),
        grid_spec=pltpu.PrefetchScalarGridSpec(
            num_scalar_prefetch=1,
            grid=(heads,),
            in_specs=[
                lane(group),
                wide,
                lane(group),
                lane(group),
                lane(group),
                fixed(at_row),
                fixed(opening_row),
                fixed(key_col),
            ],
            out_specs=[lane(group), wide],
            scratch_shapes=[
                pltpu.VMEM((group, HDIM), jnp.bfloat16),
                pltpu.VMEM((8, group), jnp.float32),
                pltpu.VMEM((group, HDIM), jnp.float32),
                pltpu.VMEM((tile, HDIM), jnp.float32),
                pltpu.VMEM((tile, HDIM), jnp.float32),
            ],
        ),
        out_shape=[
            jax.ShapeDtypeStruct((group, columns), jnp.bfloat16),
            jax.ShapeDtypeStruct((total_rows, 2 * columns), jnp.bfloat16),
        ],
        name="attend_backward",
    )(live, queries, pairs, grads, attended, totals, at_row, opening_row, key_col)


def attend_marks(query_index, query_start, key_index, tile):
    return (
        spread(query_index),
        spread(query_start),
        key_index.reshape(-1, tile),
        query_index[None, :],
        query_start[None, :],
        spread(key_index),
    )


def expert_kernel(
    perm,
    arrived,
    cot,
    weight,
    gate_weight,
    up_weight,
    down_weight,
    active,
    gate_grad,
    up_grad,
    weighted,
    inner,
    incoming,
    produced_grad,
    out_acc,
    in_acc,
):
    step = pl.program_id(0)

    @pl.when(step == 0)
    def start():
        produced_grad[...] = (weight[...] * cot[...].astype(jnp.float32)).astype(jnp.bfloat16)

    gate = jnp.dot(arrived[...], gate_weight[...], preferred_element_type=jnp.float32)
    upward = jnp.dot(arrived[...], up_weight[...], preferred_element_type=jnp.float32)
    active_grad = lax.dot_general(
        produced_grad[...],
        down_weight[...],
        (((1,), (1,)), ((), ())),
        preferred_element_type=jnp.float32,
    )
    sigmoid = 1.0 / (1.0 + jnp.exp(-gate))
    silu = gate * sigmoid
    hidden = (silu * upward).astype(jnp.bfloat16)
    active[...] = hidden
    gate_back = (active_grad * upward * sigmoid * (1.0 + gate * (1.0 - sigmoid))).astype(
        jnp.bfloat16
    )
    up_back = (active_grad * silu).astype(jnp.bfloat16)
    gate_grad[...] = gate_back
    up_grad[...] = up_back
    out_part = jnp.dot(hidden, down_weight[...], preferred_element_type=jnp.float32)
    in_part = lax.dot_general(
        jnp.concatenate([gate_back, up_back], axis=1),
        jnp.concatenate([gate_weight[...], up_weight[...]], axis=1),
        (((1,), (1,)), ((), ())),
        preferred_element_type=jnp.float32,
    )

    @pl.when(step == 0)
    def first():
        out_acc[...] = out_part
        in_acc[...] = in_part

    @pl.when(step > 0)
    def later():
        out_acc[...] += out_part
        in_acc[...] += in_part

    @pl.when(step == pl.num_programs(0) - 1)
    def finish():
        produced = out_acc[...].astype(jnp.bfloat16).astype(jnp.float32)
        weighted[...] = (weight[...] * produced).astype(jnp.bfloat16)
        sums = jnp.sum(cot[...].astype(jnp.float32) * produced, axis=1, keepdims=True)
        inner[...] = jnp.transpose(jnp.broadcast_to(sums, (sums.shape[0], 128)))[:8, :]
        incoming[...] = in_acc[...].astype(jnp.bfloat16)


def run_expert(perm, arrived, cot, weight, gate_all, up_all, down_all):
    slots, width = arrived.shape
    hidden = gate_all.shape[1]
    steps = perm.shape[0]
    chunk = hidden // steps
    rows = pl.BlockSpec((slots, width), lambda c, perm: (0, 0))
    natural = pl.BlockSpec((slots, chunk), lambda c, perm: (0, perm[c]))
    turned_in = pl.BlockSpec((width, chunk), lambda c, perm: (0, perm[c]))
    wide = jax.ShapeDtypeStruct((slots, width), jnp.bfloat16)
    thin = jax.ShapeDtypeStruct((slots, hidden), jnp.bfloat16)
    return pl.pallas_call(
        expert_kernel,
        grid_spec=pltpu.PrefetchScalarGridSpec(
            num_scalar_prefetch=1,
            grid=(steps,),
            in_specs=[
                rows,
                rows,
                pl.BlockSpec((slots, 1), lambda c, perm: (0, 0)),
                turned_in,
                turned_in,
                pl.BlockSpec((chunk, width), lambda c, perm: (c, 0)),
            ],
            out_specs=[
                pl.BlockSpec((slots, chunk), lambda c, perm: (0, c)),
                natural,
                natural,
                rows,
                pl.BlockSpec((8, slots), lambda c, perm: (0, 0)),
                rows,
                rows,
            ],
            scratch_shapes=[
                pltpu.VMEM((slots, width), jnp.float32),
                pltpu.VMEM((slots, width), jnp.float32),
            ],
        ),
        out_shape=[
            thin,
            thin,
            thin,
            wide,
            jax.ShapeDtypeStruct((8, slots), jnp.float32),
            wide,
            wide,
        ],
        name="run_expert",
    )(perm, arrived, cot, weight, gate_all, up_all, down_all)


def dispatch_kernel(codes, chosen_weights, rows, *outs, capacity, experts):
    blocks, tokens = codes.shape[1:]
    numbers = lax.broadcasted_iota(jnp.int32, (capacity, tokens), 0)
    for item in range(experts):
        for block in range(blocks):
            placed = numbers == codes[item, block : block + 1, :]
            span = slice(block * capacity, (block + 1) * capacity)
            outs[item][span, :] = jnp.dot(
                placed.astype(jnp.bfloat16),
                rows[block * tokens : (block + 1) * tokens, :],
                preferred_element_type=jnp.float32,
            ).astype(jnp.bfloat16)

    @pl.when(pl.program_id(0) == 0)
    def weigh():
        for item in range(experts):
            for block in range(blocks):
                placed = numbers == codes[item, block : block + 1, :]
                span = slice(block * capacity, (block + 1) * capacity)
                row = chosen_weights[item, block : block + 1, :]
                outs[experts + item][span, :] = jnp.sum(
                    jnp.where(placed, row, 0.0), axis=1, keepdims=True
                )


def dispatch(codes, chosen_weights, rows, capacity):
    experts, blocks, _ = codes.shape
    slots = blocks * capacity
    width = rows.shape[1]
    block = min(width, 512)
    whole = pl.BlockSpec(codes.shape, lambda step: (0, 0, 0))
    results = pl.pallas_call(
        partial(dispatch_kernel, capacity=capacity, experts=experts),
        grid=(width // block,),
        in_specs=[whole, whole, pl.BlockSpec((rows.shape[0], block), lambda step: (0, step))],
        out_specs=[pl.BlockSpec((slots, block), lambda step: (0, step))] * experts
        + [pl.BlockSpec((slots, 1), lambda step: (0, 0))] * experts,
        out_shape=[jax.ShapeDtypeStruct((slots, width), jnp.bfloat16)] * experts
        + [jax.ShapeDtypeStruct((slots, 1), jnp.float32)] * experts,
    )(codes, chosen_weights, rows)
    return results[:experts], results[experts:]


def exchange(array, offset):
    count = lax.axis_size("head")
    return lax.ppermute(array, "head", [(at, at ^ offset) for at in range(count)])


def head_pieces(array):
    return [array] + [exchange(array, offset) for offset in range(1, lax.axis_size("head"))]


def head_turn(pieces):
    return [pieces[0]] + [exchange(piece, at + 1) for at, piece in enumerate(pieces[1:])]


def add_all(pieces):
    total = pieces[0].astype(f32)
    for piece in pieces[1:]:
        total = total + piece.astype(f32)
    return total


def bit_order(turn):
    count = lax.axis_size("head").bit_length() - 1
    return [1 << ((turn + step) % count) for step in range(count)]


def gather_pieces(array, turn):
    pieces = {0: array}
    for bit in bit_order(turn):
        for offset in list(pieces):
            pieces[offset ^ bit] = exchange(pieces[offset], bit)
    return [pieces[offset] for offset in range(len(pieces))]


def scatter_pieces(pieces, turn):
    held = dict(enumerate(pieces))
    for bit in bit_order(turn):
        for offset in [item for item in held if item & bit]:
            piece = held.pop(offset).astype(bf16)
            arrived = exchange(piece, bit)
            held[offset ^ bit] = held[offset ^ bit].astype(f32) + arrived.astype(f32)
    return held[0]


def xor_order(array, axis):
    count = lax.axis_size("head")
    at = lax.axis_index("head")
    size = array.shape[axis] // count
    chunks = [
        lax.dynamic_slice_in_dim(array, (at ^ offset) * size, size, axis) for offset in range(count)
    ]
    return chunks


def xor_chunks(array, axis):
    return jnp.concatenate(xor_order(array, axis), axis=axis)


def absolute(pieces):
    at = lax.axis_index("head")
    result = []
    for place in range(len(pieces)):
        value = pieces[0]
        for offset in range(1, len(pieces)):
            value = jnp.where(at == place ^ offset, pieces[offset], value)
        result.append(value)
    return result


def move_rows(array, outer, inner, part):
    shaped = array.reshape(outer, inner, part, array.shape[1])
    return jnp.transpose(shaped, (1, 0, 2, 3)).reshape(array.shape)


def move_columns(array, outer, inner, part):
    shaped = array.reshape(array.shape[0], outer, inner, part)
    return jnp.transpose(shaped, (0, 2, 1, 3)).reshape(array.shape)


def layer(
    tokens,
    query_weight,
    key_weight,
    value_weight,
    output_weight,
    mixing_gain,
    query_gain,
    key_gain,
    routing_gain,
    router_weight,
    gate_weight,
    up_weight,
    down_weight,
    seq_lengths,
    dealt_order,
    expert_routes,
    slot_order,
    cotangent,
):
    heads_axis = lax.axis_size("head")
    blocks = lax.axis_size("blk")
    head_at = lax.axis_index("head")
    block_at = lax.axis_index("blk")
    rows, width = tokens.shape
    picks = expert_routes.shape[1]
    total_rows = dealt_order.shape[0]
    group = rows * heads_axis
    columns = width // heads_axis
    part = query_weight.shape[0]
    head_size = HDIM
    experts = router_weight.shape[1]
    local_experts = gate_weight.shape[0]
    capacity = 5 * rows * picks // (4 * experts)
    slots = blocks * capacity

    slices = [
        jnp.concatenate(chunks, axis=1)
        for chunks in zip(
            xor_order(key_weight, 1), xor_order(value_weight, 1), xor_order(query_weight, 1)
        )
    ]
    slices = head_turn(slices)
    output_rows = lax.all_gather(output_weight, "blk", axis=0, tiled=True)
    token_pieces = head_pieces(tokens)
    rows_here = jnp.stack(absolute(slices)).reshape(heads_axis * part, 3 * columns)
    pair_full = lax.all_gather(rows_here[:, : 2 * columns], "blk", axis=0, tiled=True)
    pair_full = move_rows(pair_full, blocks, heads_axis, part)
    query_full = lax.all_gather(rows_here[:, 2 * columns :], "blk", axis=0, tiled=True)
    query_full = move_rows(query_full, blocks, heads_axis, part)
    cot_all = lax.all_gather(cotangent, "blk", axis=0, tiled=True)

    small = jnp.concatenate(
        [
            mixing_gain[:, None],
            query_gain[:, None],
            key_gain[:, None],
            routing_gain[:, None],
            router_weight,
        ],
        axis=1,
    ).reshape(1, -1)
    codes = slot_codes(expert_routes, slot_order, experts, capacity).astype(bf16)
    sizes = small.shape[1]
    small = lax.all_gather(
        jnp.concatenate([small, codes.reshape(1, -1)], axis=1), "blk", axis=0, tiled=True
    )
    codes = small[:, sizes:].reshape(blocks, rows, experts).astype(jnp.int32)
    small = small[:, :sizes]
    small = jnp.stack(absolute(head_pieces(small))).reshape(width, 4 + experts)
    mixing_scale = small[:, 0].astype(f32)
    routing_scale = small[:, 3].astype(f32)
    query_scale = lax.dynamic_slice_in_dim(small[:, 1], head_at * columns, columns).astype(f32)
    key_scale = lax.dynamic_slice_in_dim(small[:, 2], head_at * columns, columns).astype(f32)
    router_full = small[:, 4:]
    codes_here = lax.dynamic_slice_in_dim(codes, block_at * local_experts, local_experts, 2)

    key_index = jnp.transpose(
        xor_chunks(dealt_order.reshape(heads_axis, blocks, rows), 0), (1, 0, 2)
    ).reshape(total_rows)
    key_seq = stream_layout(seq_lengths, key_index)[0]
    query_index = lax.dynamic_slice_in_dim(key_index, block_at * group, group)
    query_seq, query_position = stream_layout(seq_lengths, query_index)
    cosine, sine_part = rope_tables(query_position, head_size)
    tables = tile_lists(query_index, query_seq, key_index, key_seq, TILE)
    marks = attend_marks(query_index, query_index - query_position, key_index, TILE)

    gates, ups, downs = (
        [gather_pieces(weight[item], item) for item in range(local_experts)]
        for weight in (gate_weight, up_weight, down_weight)
    )

    normed = norm_rows(token_pieces, mixing_scale)
    normed_moved = move_columns(normed, heads_axis, blocks, part)
    key_raw, key_square = project(normed, pair_full, columns)
    value_heads = jnp.dot(normed, pair_full[:, columns:], preferred_element_type=f32)
    value_heads = value_heads.astype(bf16)
    key_squares = head_pieces(key_square)
    pairs, key_factor = rope_forward(
        key_squares, key_raw, key_scale, cosine, sine_part, value_heads, width
    )
    query_raw, query_square = project(normed, query_full, columns)
    query_squares = head_pieces(query_square)
    query_heads, query_factor = rope_forward(
        query_squares, query_raw, query_scale, cosine, sine_part, None, width
    )
    pairs_all = lax.all_gather(pairs, "blk", axis=0, tiled=True)
    attended, context, totals = attend_forward(query_heads, pairs_all, marks, tables, TILE)
    branch = jnp.dot(context, output_rows, preferred_element_type=f32).astype(bf16)
    branch = head_turn([branch[piece * rows : (piece + 1) * rows] for piece in range(heads_axis)])
    own_tokens = tokens.astype(f32)
    middle = own_tokens + add_all(branch)
    middle_factor = rms_factor(jnp.sum(middle * middle, axis=-1, keepdims=True), width)
    routed = (middle * middle_factor * routing_scale).astype(bf16)

    routed_all = lax.all_gather(xor_chunks(routed, 1), "blk", axis=0, tiled=True)
    probs = jax.nn.softmax(jnp.dot(routed, router_full, preferred_element_type=f32), axis=-1)
    probs_all = jax.nn.softmax(
        jnp.dot(routed_all, xor_chunks(router_full, 0), preferred_element_type=f32), axis=-1
    )
    weight_here = lax.dynamic_slice_in_dim(
        probs_all, block_at * local_experts, local_experts, 1
    ).reshape(blocks, rows, local_experts)
    slot_ids = jnp.arange(capacity, dtype=jnp.int32)
    codes_here = jnp.transpose(codes_here, (2, 0, 1))
    weight_here = jnp.transpose(weight_here, (2, 0, 1))
    placed = codes_here[:, :, None, :] == slot_ids[None, None, :, None]
    place = placed.astype(bf16)

    def arrange(flat, weighed=True):
        lots_here = weight_here if weighed else jnp.zeros(codes_here.shape, f32)
        if capacity % 16 == 0:
            return dispatch(codes_here, lots_here, flat, capacity)
        shaped = flat.reshape(blocks, rows, width)
        lots = jnp.sum(jnp.where(placed, lots_here[:, :, None, :], 0.0), axis=-1)
        return (
            [
                jnp.einsum("srt,std->srd", item, shaped).reshape(slots, width)
                for item in place
            ],
            [item.reshape(slots, 1) for item in lots],
        )

    arrived_cot = arrange(cot_all, False)[0]
    gate_all, up_all, down_all = (
        [jnp.concatenate(pieces, axis=0) for pieces in group_pieces]
        for group_pieces in (gates, ups, downs)
    )
    arrived, slot_weight = arrange(routed_all)
    offsets = jnp.bitwise_xor(head_at, jnp.arange(heads_axis, dtype=jnp.int32))
    results = [
        run_expert(
            offsets,
            arrived[item],
            arrived_cot[item],
            slot_weight[item],
            gate_all[item],
            up_all[item],
            down_all[item],
        )
        for item in range(local_experts)
    ]

    def back_to_rows(which):
        return sum(
            jnp.einsum(
                "srt,srd->std",
                place[item],
                results[item][which].reshape(blocks, capacity, width),
                preferred_element_type=f32,
            )
            for item in range(local_experts)
        )

    incoming = back_to_rows(5)
    combined = back_to_rows(3)
    slot_grad = jnp.stack([result[4][0] for result in results])
    slot_grad = slot_grad.reshape(local_experts, blocks, capacity, 1)
    weight_grads = jnp.sum(jnp.where(placed, slot_grad, 0.0), axis=2)
    weight_grads = jnp.transpose(weight_grads, (1, 2, 0))
    stores = [
        (arrived[item], results[item][6], results[item][0], results[item][1], results[item][2])
        for item in range(local_experts)
    ]
    routed_grad = lax.psum_scatter(
        incoming.astype(bf16).reshape(blocks * rows, width),
        "blk",
        scatter_dimension=0,
        tiled=True,
    )
    combined = lax.psum_scatter(
        combined.astype(bf16).reshape(blocks * rows, width),
        "blk",
        scatter_dimension=0,
        tiled=True,
    )
    block_output = (middle + combined.astype(f32)).astype(bf16)
    prob_grad = lax.all_to_all(
        weight_grads, "blk", split_axis=0, concat_axis=2, tiled=True
    ).reshape(rows, experts)

    def pieces_of(left, right):
        size = left.shape[1] // heads_axis
        return [
            lax.optimization_barrier(
                jnp.dot(
                    left[:, offset * size : (offset + 1) * size].T,
                    right,
                    preferred_element_type=f32,
                ).astype(bf16)
            )
            for offset in range(heads_axis)
        ]

    down_out, gate_out, up_out = (
        jnp.stack(
            [
                scatter_pieces(pieces_of(store[left], store[right]), item)
                for item, store in enumerate(stores)
            ]
        ).astype(f32)
        for left, right in ((2, 1), (0, 3), (0, 4))
    )

    logit_grad = (
        probs * (prob_grad - jnp.sum(probs * prob_grad, axis=1, keepdims=True))
    ).astype(bf16)
    router_sum = jnp.dot(routed.T, logit_grad, preferred_element_type=f32)
    routed_grad = xor_chunks(routed_grad, 1).astype(f32) + jnp.dot(
        logit_grad, router_full.T, preferred_element_type=f32
    )
    scaled = routed_grad * routing_scale
    inner = jnp.mean(scaled * middle, axis=-1, keepdims=True)
    middle_grad = (
        cotangent.astype(f32) + middle_factor * scaled - middle * (middle_factor**3 * inner)
    )
    routing_sum = jnp.sum(routed_grad * middle * middle_factor, axis=0)

    branch_grad = head_pieces(middle_grad.astype(bf16))
    branch_grad = jnp.concatenate(branch_grad, axis=0)
    context_grad = jnp.dot(branch_grad, output_rows.T, preferred_element_type=f32).astype(bf16)
    output_sum = jnp.dot(context.T, branch_grad, preferred_element_type=f32).astype(bf16)
    output_out = lax.psum_scatter(output_sum, "blk", scatter_dimension=0, tiled=True)
    query_back, pairs_back = attend_backward(
        query_heads, pairs_all, context_grad, attended, totals, marks, tables, TILE
    )
    pairs_back = lax.psum_scatter(pairs_back, "blk", scatter_dimension=0, tiled=True)
    query_scaled, query_inner, querynorm_sum = rope_backward(
        query_back, query_raw, query_factor, query_scale, cosine, sine_part, 1
    )
    query_inner = head_pieces(query_inner)
    query_raw_grad = raw_backward(query_inner, query_scaled, query_raw, query_factor, None, width)
    query_sum = jnp.dot(normed_moved.T, query_raw_grad, preferred_element_type=f32).astype(bf16)
    query_sum = lax.psum_scatter(query_sum, "blk", scatter_dimension=0, tiled=True)
    normed_part = jnp.dot(query_raw_grad, query_full.T, preferred_element_type=f32)
    key_scaled, key_inner, keynorm_sum = rope_backward(
        pairs_back, key_raw, key_factor, key_scale, cosine, sine_part, 2
    )
    key_inner = head_pieces(key_inner)
    pair_grad = raw_backward(key_inner, key_scaled, key_raw, key_factor, pairs_back, width)
    pair_sum = jnp.dot(normed_moved.T, pair_grad, preferred_element_type=f32).astype(bf16)
    pair_sum = lax.psum_scatter(pair_sum, "blk", scatter_dimension=0, tiled=True)
    normed_part = normed_part + jnp.dot(pair_grad, pair_full.T, preferred_element_type=f32)
    normed_part = normed_part.astype(bf16)
    normed_part = head_turn(
        [normed_part[piece * rows : (piece + 1) * rows] for piece in range(heads_axis)]
    )
    normed_grad = add_all(normed_part)
    own_factor = rms_factor(jnp.sum(own_tokens * own_tokens, axis=-1, keepdims=True), width)
    scaled = normed_grad * mixing_scale
    inner = jnp.mean(scaled * own_tokens, axis=-1, keepdims=True)
    tokens_grad = middle_grad + own_factor * scaled - own_tokens * (own_factor**3 * inner)
    mixing_sum = jnp.sum(normed_grad * own_tokens * own_factor, axis=0)

    def turned_back(array):
        return jnp.stack(
            [
                jnp.concatenate(absolute(list(pieces)), axis=1).astype(f32)
                for pieces in zip(
                    *(
                        [piece[:, at : at + columns] for at in range(0, piece.shape[1], columns)]
                        for piece in head_turn(xor_order(array, 0))
                    )
                )
            ]
        )

    query_out = turned_back(query_sum)[0]
    pair_out = turned_back(pair_sum)

    blank = jnp.zeros((heads_axis, columns), f32)
    query_line = lax.dynamic_update_slice(blank, querynorm_sum, (head_at, 0)).reshape(width)
    key_line = lax.dynamic_update_slice(blank, keynorm_sum, (head_at, 0)).reshape(width)
    lines = jnp.concatenate(
        [
            mixing_sum[:, None],
            query_line[:, None],
            key_line[:, None],
            routing_sum[:, None],
            router_sum,
        ],
        axis=1,
    ).reshape(heads_axis, -1)
    lines = add_all(head_turn(xor_order(lines, 0)))
    lines = lax.all_to_all(lines.reshape(blocks, -1), "blk", 0, 0, tiled=True)
    lines = jnp.sum(lines, axis=0).reshape(part, 4 + experts)
    return (
        block_output,
        tokens_grad,
        query_out,
        pair_out[0],
        pair_out[1],
        output_out.astype(f32),
        lines[:, 0],
        lines[:, 1],
        lines[:, 2],
        lines[:, 3],
        lines[:, 4:],
        gate_out,
        up_out,
        down_out,
    )


def solution(mesh):
    in_specs = (
        P(("head", "blk"), None),
        P(("head", "blk"), None),
        P(("head", "blk"), None),
        P(("head", "blk"), None),
        P(("head", "blk"), None),
        P(("head", "blk")),
        P(("head", "blk")),
        P(("head", "blk")),
        P(("head", "blk")),
        P(("head", "blk"), None),
        P("blk", "head", None),
        P("blk", "head", None),
        P("blk", "head", None),
        P(),
        P(),
        P(("head", "blk"), None),
        P(("head", "blk"), None),
        P(("head", "blk"), None),
    )
    out_specs = (
        P(("head", "blk"), None),
        P(("head", "blk"), None),
        P(("head", "blk"), None),
        P(("head", "blk"), None),
        P(("head", "blk"), None),
        P(("head", "blk"), None),
        P(("head", "blk")),
        P(("head", "blk")),
        P(("head", "blk")),
        P(("head", "blk")),
        P(("head", "blk"), None),
        P("blk", "head", None),
        P("blk", "head", None),
        P("blk", "head", None),
    )
    return jax.shard_map(layer, mesh=mesh, in_specs=in_specs, out_specs=out_specs, check_vma=False)
```

```python
from functools import partial
import math

import jax
import jax.numpy as jnp
import numpy as np
from jax import lax
from jax.experimental import pallas as pl
from jax.experimental.pallas import tpu as pltpu
from jax.sharding import PartitionSpec as P


HDIM = 128
TILE = 256
LOG2E = 1.4426950408889634
norm_eps = 1e-05
rope_base = 10000.0
f32 = jnp.float32
bf16 = jnp.bfloat16


def rms_factor(square_sum, width):
    return lax.rsqrt(square_sum / width + norm_eps)


def rope_tables(position, head_size):
    half = head_size // 2
    freqs = rope_base ** (-(np.arange(half, dtype=np.float64) * 2.0) / head_size)
    angles = position.astype(f32)[:, None] * jnp.asarray(freqs.astype(np.float32))[None, :]
    cosine = jnp.cos(angles)
    sine_part = jnp.sin(angles)
    return (
        jnp.concatenate([cosine, cosine], axis=1),
        jnp.concatenate([-sine_part, sine_part], axis=1),
    )


def column_of(pieces):
    count = len(pieces)
    rows = pieces[0].shape[1] // count
    total = pieces[0][...]
    for offset in range(1, count):
        parts = [
            pieces[offset][:, (at ^ offset) * rows : ((at ^ offset) + 1) * rows]
            for at in range(count)
        ]
        total = total + jnp.concatenate(parts, axis=1)
    return jnp.transpose(jnp.broadcast_to(total, (8, total.shape[1])))[:, :1]


def turned(value, cosine, sine_part):
    return value * cosine + pltpu.roll(value, HDIM // 2, 1) * sine_part


def rope_kernel(*refs, count, width, paired):
    squares = refs[:count]
    raw, scale, cosine, sine_part = refs[count : count + 4]
    out, factors = refs[-2:]
    factor = lax.rsqrt(column_of(squares) / width + norm_eps)
    factors[...] = jnp.broadcast_to(factor, factors.shape)
    for head in range(raw.shape[1] // HDIM):
        span = slice(head * HDIM, (head + 1) * HDIM)
        value = turned(raw[:, span] * factor * scale[:, span], cosine[...], sine_part[...])
        if paired:
            start = 2 * head * HDIM
            out[:, start : start + HDIM] = value.astype(jnp.bfloat16)
            out[:, start + HDIM : start + 2 * HDIM] = refs[count + 4][:, span]
        else:
            out[:, span] = value.astype(jnp.bfloat16)


def rope_forward(squares, raw, scale, cosine, sine_part, values, width):
    group, columns = raw.shape
    paired = values is not None
    extra = (values,) if paired else ()
    return pl.pallas_call(
        partial(rope_kernel, count=len(squares), width=width, paired=paired),
        out_shape=[
            jax.ShapeDtypeStruct((group, columns * (2 if paired else 1)), jnp.bfloat16),
            jax.ShapeDtypeStruct((group, HDIM), jnp.float32),
        ],
    )(*squares, raw, scale[None], cosine, sine_part, *extra)


def unrope_kernel(back, raw, factors, scale, cosine, sine_part, scaled, inner, gain, *, stride):
    group = raw.shape[0]
    total = jnp.zeros((group, HDIM), jnp.float32)
    for head in range(raw.shape[1] // HDIM):
        span = slice(head * HDIM, (head + 1) * HDIM)
        start = stride * head * HDIM
        grad = back[:, start : start + HDIM].astype(jnp.float32)
        turn = turned(grad, cosine[...], -sine_part[...])
        product = turn * raw[:, span]
        gain[:, span] = jnp.sum(product * factors[...], axis=0, keepdims=True)
        scaled[:, span] = turn * scale[:, span]
        total = total + product * scale[:, span]
    sums = jnp.broadcast_to(jnp.sum(total, axis=1, keepdims=True), (group, HDIM))
    inner[...] = jnp.transpose(sums)[:1, :]


def rope_backward(back, raw, factors, scale, cosine, sine_part, stride):
    group, columns = raw.shape
    return pl.pallas_call(
        partial(unrope_kernel, stride=stride),
        out_shape=[
            jax.ShapeDtypeStruct((group, columns), jnp.float32),
            jax.ShapeDtypeStruct((1, group), jnp.float32),
            jax.ShapeDtypeStruct((1, columns), jnp.float32),
        ],
    )(back, raw, factors, scale[None], cosine, sine_part)


def raw_kernel(*refs, count, width, paired):
    scaled, raw, factors = refs[count : count + 3]
    out = refs[-1]
    inner = column_of(refs[:count]) / width
    factor = factors[:, :1]
    columns = raw.shape[1]
    slope = factor * factor * factor * inner
    for head in range(columns // HDIM):
        span = slice(head * HDIM, (head + 1) * HDIM)
        out[:, span] = (factor * scaled[:, span] - raw[:, span] * slope).astype(jnp.bfloat16)
        if paired:
            start = (2 * head + 1) * HDIM
            out[:, columns + head * HDIM : columns + (head + 1) * HDIM] = refs[count + 3][
                :, start : start + HDIM
            ]


def raw_backward(inner, scaled, raw, factors, pairs_back, width):
    group, columns = raw.shape
    paired = pairs_back is not None
    extra = (pairs_back,) if paired else ()
    return pl.pallas_call(
        partial(raw_kernel, count=len(inner), width=width, paired=paired),
        out_shape=jax.ShapeDtypeStruct((group, columns * (2 if paired else 1)), jnp.bfloat16),
    )(*inner, scaled, raw, factors, *extra)


def norm_kernel(*refs, count):
    scale, out = refs[count], refs[count + 1]
    rows, width = refs[0].shape
    for place in range(count):
        value = refs[place][...].astype(jnp.float32)
        square = jnp.sum(value * value, axis=1, keepdims=True)
        factor = lax.rsqrt(square / width + norm_eps)
        out[place * rows : (place + 1) * rows, :] = (value * factor * scale[...]).astype(
            jnp.bfloat16
        )


def norm_rows(pieces, scale):
    rows, width = pieces[0].shape
    return pl.pallas_call(
        partial(norm_kernel, count=len(pieces)),
        out_shape=jax.ShapeDtypeStruct((rows * len(pieces), width), jnp.bfloat16),
        name="norm_rows",
    )(*pieces, scale[None])


def project_kernel(normed, weight, raw, square, total):
    step = pl.program_id(0)

    @pl.when(step == 0)
    def start():
        total[...] = jnp.zeros_like(total)

    value = jnp.dot(normed[...], weight[...], preferred_element_type=jnp.float32)
    raw[...] = value
    for at in range(0, value.shape[1], HDIM):
        total[...] += value[:, at : at + HDIM] * value[:, at : at + HDIM]

    @pl.when(step == pl.num_programs(0) - 1)
    def finish():
        sums = jnp.sum(total[...], axis=1, keepdims=True)
        square[...] = jnp.transpose(jnp.broadcast_to(sums, total.shape))[:1, :]


def project(normed, weight, columns):
    group, width = normed.shape
    block = min(columns, 256)
    return pl.pallas_call(
        project_kernel,
        grid=(columns // block,),
        in_specs=[
            pl.BlockSpec((group, width), lambda step: (0, 0)),
            pl.BlockSpec((width, block), lambda step: (0, step)),
        ],
        out_specs=[
            pl.BlockSpec((group, block), lambda step: (0, step)),
            pl.BlockSpec((1, group), lambda step: (0, 0)),
        ],
        out_shape=[
            jax.ShapeDtypeStruct((group, columns), jnp.float32),
            jax.ShapeDtypeStruct((1, group), jnp.float32),
        ],
        scratch_shapes=[pltpu.VMEM((group, HDIM), jnp.float32)],
    )(normed, weight)


def slot_codes(routes, ordering, experts, capacity):
    expert_ids = jnp.arange(experts, dtype=jnp.int32)
    absent = jnp.int32(1 << 30)
    chosen = routes[:, :, None] == expert_ids[None, None, :]
    order = jnp.min(jnp.where(chosen, ordering[:, :, None], absent), axis=1)
    rank = jnp.sum((order[None, :, :] < order[:, None, :]).astype(jnp.int32), axis=1)
    return jnp.where((order < absent) & (rank < capacity), rank, -1)


def stream_layout(seq_lengths, stream_index):
    ends = jnp.cumsum(seq_lengths)
    starts = ends - seq_lengths
    passed = (stream_index[:, None] >= ends[None, :]).astype(jnp.int32)
    sequence = jnp.sum(passed, axis=1)
    owner = sequence[:, None] == jnp.arange(seq_lengths.shape[0], dtype=jnp.int32)[None, :]
    opening = jnp.sum(jnp.where(owner, starts[None, :], 0), axis=1)
    return (sequence, stream_index - opening)


def tile_lists(query_index, query_seq, key_index, key_seq, tile):
    query_tiles = query_index.shape[0] // tile
    key_tiles = key_index.shape[0] // tile
    query_marks = query_index.reshape(query_tiles, tile)
    query_seqs = query_seq.reshape(query_tiles, tile)
    key_marks = key_index.reshape(key_tiles, tile)
    key_seqs = key_seq.reshape(key_tiles, tile)
    early = jnp.min(key_marks, axis=1)[None, :] <= jnp.max(query_marks, axis=1)[:, None]
    above = jnp.max(key_seqs, axis=1)[None, :] >= jnp.min(query_seqs, axis=1)[:, None]
    below = jnp.min(key_seqs, axis=1)[None, :] <= jnp.max(query_seqs, axis=1)[:, None]
    live = (early & above & below).astype(jnp.int32)
    order = jnp.cumsum(live, axis=1) - 1
    numbers = jnp.arange(key_tiles, dtype=jnp.int32)
    hits = (order[:, :, None] == numbers[None, None, :]) & (live[:, :, None] > 0)
    listed = jnp.sum(jnp.where(hits, numbers[None, :, None], 0), axis=1)
    return (listed.astype(jnp.int32), jnp.sum(live, axis=1).astype(jnp.int32), live)


def spread(vector):
    return jnp.broadcast_to(vector[:, None], (vector.shape[0], 128))


def twice(value, count):
    return value if count == 1 else jnp.concatenate([value] * count, axis=1)


def forward_kernel(
    listed, counts, query, pairs, at, opening, key_at, attended, context, totals, total, acc, *, tile
):
    lanes = 128
    copies = tile // lanes
    factor = LOG2E / math.sqrt(HDIM)
    for step in range(query.shape[0] // tile):
        span = slice(step * tile, (step + 1) * tile)
        acc[...] = jnp.zeros_like(acc)
        total[...] = jnp.zeros_like(total)

        def visit(turn, carry):
            number = listed[step, turn]
            start = pl.multiple_of(number * tile, tile)
            scores = lax.dot_general(
                query[span, :],
                pairs[pl.ds(start, tile), :HDIM],
                (((1,), (1,)), ((), ())),
                preferred_element_type=jnp.float32,
            )
            marks = key_at[pl.ds(number, 1), :]
            allowed = (marks <= twice(at[span, :], copies)) & (
                marks >= twice(opening[span, :], copies)
            )
            expo = jnp.where(allowed, jnp.exp2(scores * factor), 0.0)
            partial_sum = expo[:, :lanes]
            for copy in range(1, copies):
                partial_sum = partial_sum + expo[:, copy * lanes : (copy + 1) * lanes]
            total[...] += partial_sum
            acc[...] += jnp.dot(
                expo.astype(jnp.bfloat16),
                pairs[pl.ds(start, tile), HDIM:],
                preferred_element_type=jnp.float32,
            )
            return carry

        lax.fori_loop(0, counts[step], visit, 0)
        full = jnp.sum(total[...], axis=1, keepdims=True)
        result = acc[...] / full
        attended[span, :] = result
        context[span, :] = result.astype(jnp.bfloat16)
        totals[span, :] = jnp.broadcast_to(full, (tile, lanes))


def attend_forward(queries, pairs, marks, tables, tile):
    group, columns = queries.shape
    total_rows = pairs.shape[0]
    listed, counts, _ = tables
    at, opening, key_at = marks[0], marks[1], marks[2]
    heads = columns // HDIM
    lane = lambda rows: pl.BlockSpec((rows, HDIM), lambda h, *refs: (0, h))
    wide = pl.BlockSpec((total_rows, 2 * HDIM), lambda h, *refs: (0, h))
    fixed = lambda array: pl.BlockSpec(array.shape, lambda h, *refs: (0, 0))
    return pl.pallas_call(
        partial(forward_kernel, tile=tile),
        grid_spec=pltpu.PrefetchScalarGridSpec(
            num_scalar_prefetch=2,
            grid=(heads,),
            in_specs=[
                lane(group),
                wide,
                fixed(at),
                fixed(opening),
                fixed(key_at),
            ],
            out_specs=[lane(group), lane(group), lane(group)],
            scratch_shapes=[
                pltpu.VMEM((tile, HDIM), jnp.float32),
                pltpu.VMEM((tile, HDIM), jnp.float32),
            ],
        ),
        out_shape=[
            jax.ShapeDtypeStruct((group, columns), jnp.float32),
            jax.ShapeDtypeStruct((group, columns), jnp.bfloat16),
            jax.ShapeDtypeStruct((group, columns), jnp.float32),
        ],
        name="attend_forward",
    )(listed, counts, queries, pairs, at, opening, key_at)


def backward_kernel(
    live,
    query,
    pairs,
    grad,
    attended,
    totals,
    at_row,
    opening_row,
    key_col,
    query_out,
    pairs_out,
    scaled,
    offset,
    query_acc,
    key_acc,
    value_acc,
    *,
    tile,
):
    copies = tile // 128
    steps = query.shape[0] // tile
    factor = 1.0 / math.sqrt(HDIM)
    grads = grad[...].astype(jnp.float32)
    scaled[...] = (grads / totals[...]).astype(jnp.bfloat16)
    sums = jnp.sum(grads * attended[...], axis=1, keepdims=True) / totals[...]
    offset[...] = jnp.transpose(sums)[:8, :]
    query_acc[...] = jnp.zeros_like(query_acc)

    def visit(number, carry):
        start = pl.multiple_of(number * tile, tile)
        window = pl.ds(start, tile)
        key_acc[...] = jnp.zeros_like(key_acc)
        value_acc[...] = jnp.zeros_like(value_acc)
        for step in range(steps):
            span = slice(step * tile, (step + 1) * tile)

            @pl.when(live[step, number] > 0)
            def unused():
                scores = lax.dot_general(
                    pairs[window, :HDIM],
                    query[span, :],
                    (((1,), (1,)), ((), ())),
                    preferred_element_type=jnp.float32,
                )
                marks = twice(key_col[window, :], copies)
                allowed = (marks <= at_row[:, span]) & (marks >= opening_row[:, span])
                expo = jnp.where(allowed, jnp.exp2(scores * (factor * LOG2E)), 0.0)
                inner = lax.dot_general(
                    pairs[window, HDIM:],
                    scaled[span, :],
                    (((1,), (1,)), ((), ())),
                    preferred_element_type=jnp.float32,
                )
                back = (expo * (inner - offset[0:1, span])).astype(jnp.bfloat16)
                key_acc[...] += jnp.dot(back, query[span, :], preferred_element_type=jnp.float32)
                value_acc[...] += jnp.dot(
                    expo.astype(jnp.bfloat16), scaled[span, :], preferred_element_type=jnp.float32
                )
                query_acc[span, :] += lax.dot_general(
                    back,
                    pairs[window, :HDIM],
                    (((0,), (0,)), ((), ())),
                    preferred_element_type=jnp.float32,
                )

        pairs_out[window, :HDIM] = (key_acc[...] * factor).astype(jnp.bfloat16)
        pairs_out[window, HDIM:] = value_acc[...].astype(jnp.bfloat16)
        return carry

    lax.fori_loop(0, pairs.shape[0] // tile, visit, 0)
    query_out[...] = (query_acc[...] * factor).astype(jnp.bfloat16)


def attend_backward(queries, pairs, grads, attended, totals, marks, tables, tile):
    group, columns = queries.shape
    total_rows = pairs.shape[0]
    live = tables[2]
    at_row, opening_row, key_col = marks[3], marks[4], marks[5]
    heads = columns // HDIM
    lane = lambda rows: pl.BlockSpec((rows, HDIM), lambda h, *refs: (0, h))
    wide = pl.BlockSpec((total_rows, 2 * HDIM), lambda h, *refs: (0, h))
    fixed = lambda array: pl.BlockSpec(array.shape, lambda h, *refs: (0, 0))
    return pl.pallas_call(
        partial(backward_kernel, tile=tile),
        grid_spec=pltpu.PrefetchScalarGridSpec(
            num_scalar_prefetch=1,
            grid=(heads,),
            in_specs=[
                lane(group),
                wide,
                lane(group),
                lane(group),
                lane(group),
                fixed(at_row),
                fixed(opening_row),
                fixed(key_col),
            ],
            out_specs=[lane(group), wide],
            scratch_shapes=[
                pltpu.VMEM((group, HDIM), jnp.bfloat16),
                pltpu.VMEM((8, group), jnp.float32),
                pltpu.VMEM((group, HDIM), jnp.float32),
                pltpu.VMEM((tile, HDIM), jnp.float32),
                pltpu.VMEM((tile, HDIM), jnp.float32),
            ],
        ),
        out_shape=[
            jax.ShapeDtypeStruct((group, columns), jnp.bfloat16),
            jax.ShapeDtypeStruct((total_rows, 2 * columns), jnp.bfloat16),
        ],
        name="attend_backward",
    )(live, queries, pairs, grads, attended, totals, at_row, opening_row, key_col)


def attend_marks(query_index, query_start, key_index, tile):
    return (
        spread(query_index),
        spread(query_start),
        key_index.reshape(-1, tile),
        query_index[None, :],
        query_start[None, :],
        spread(key_index),
    )


def expert_kernel(
    perm,
    arrived,
    cot,
    weight,
    gate_weight,
    up_weight,
    down_weight,
    active,
    gate_grad,
    up_grad,
    weighted,
    inner,
    incoming,
    produced_grad,
    out_acc,
    in_acc,
):
    step = pl.program_id(0)

    @pl.when(step == 0)
    def start():
        produced_grad[...] = (weight[...] * cot[...].astype(jnp.float32)).astype(jnp.bfloat16)

    gate = jnp.dot(arrived[...], gate_weight[...], preferred_element_type=jnp.float32)
    upward = jnp.dot(arrived[...], up_weight[...], preferred_element_type=jnp.float32)
    active_grad = lax.dot_general(
        produced_grad[...],
        down_weight[...],
        (((1,), (1,)), ((), ())),
        preferred_element_type=jnp.float32,
    )
    sigmoid = 1.0 / (1.0 + jnp.exp(-gate))
    silu = gate * sigmoid
    hidden = (silu * upward).astype(jnp.bfloat16)
    active[...] = hidden
    gate_back = (active_grad * upward * sigmoid * (1.0 + gate * (1.0 - sigmoid))).astype(
        jnp.bfloat16
    )
    up_back = (active_grad * silu).astype(jnp.bfloat16)
    gate_grad[...] = gate_back
    up_grad[...] = up_back
    out_part = jnp.dot(hidden, down_weight[...], preferred_element_type=jnp.float32)
    in_part = lax.dot_general(
        jnp.concatenate([gate_back, up_back], axis=1),
        jnp.concatenate([gate_weight[...], up_weight[...]], axis=1),
        (((1,), (1,)), ((), ())),
        preferred_element_type=jnp.float32,
    )

    @pl.when(step == 0)
    def first():
        out_acc[...] = out_part
        in_acc[...] = in_part

    @pl.when(step > 0)
    def later():
        out_acc[...] += out_part
        in_acc[...] += in_part

    @pl.when(step == pl.num_programs(0) - 1)
    def finish():
        produced = out_acc[...].astype(jnp.bfloat16).astype(jnp.float32)
        weighted[...] = (weight[...] * produced).astype(jnp.bfloat16)
        sums = jnp.sum(cot[...].astype(jnp.float32) * produced, axis=1, keepdims=True)
        inner[...] = jnp.transpose(jnp.broadcast_to(sums, (sums.shape[0], 128)))[:8, :]
        incoming[...] = in_acc[...].astype(jnp.bfloat16)


def run_expert(perm, arrived, cot, weight, gate_all, up_all, down_all):
    slots, width = arrived.shape
    hidden = gate_all.shape[1]
    steps = perm.shape[0]
    chunk = hidden // steps
    rows = pl.BlockSpec((slots, width), lambda c, perm: (0, 0))
    natural = pl.BlockSpec((slots, chunk), lambda c, perm: (0, perm[c]))
    turned_in = pl.BlockSpec((width, chunk), lambda c, perm: (0, perm[c]))
    wide = jax.ShapeDtypeStruct((slots, width), jnp.bfloat16)
    thin = jax.ShapeDtypeStruct((slots, hidden), jnp.bfloat16)
    return pl.pallas_call(
        expert_kernel,
        grid_spec=pltpu.PrefetchScalarGridSpec(
            num_scalar_prefetch=1,
            grid=(steps,),
            in_specs=[
                rows,
                rows,
                pl.BlockSpec((slots, 1), lambda c, perm: (0, 0)),
                turned_in,
                turned_in,
                pl.BlockSpec((chunk, width), lambda c, perm: (c, 0)),
            ],
            out_specs=[
                pl.BlockSpec((slots, chunk), lambda c, perm: (0, c)),
                natural,
                natural,
                rows,
                pl.BlockSpec((8, slots), lambda c, perm: (0, 0)),
                rows,
                rows,
            ],
            scratch_shapes=[
                pltpu.VMEM((slots, width), jnp.float32),
                pltpu.VMEM((slots, width), jnp.float32),
            ],
        ),
        out_shape=[
            thin,
            thin,
            thin,
            wide,
            jax.ShapeDtypeStruct((8, slots), jnp.float32),
            wide,
            wide,
        ],
        name="run_expert",
    )(perm, arrived, cot, weight, gate_all, up_all, down_all)


def dispatch_kernel(codes, chosen_weights, rows, *outs, capacity, experts):
    blocks, tokens = codes.shape[1:]
    numbers = lax.broadcasted_iota(jnp.int32, (capacity, tokens), 0)
    for block in range(blocks):
        span = slice(block * capacity, (block + 1) * capacity)
        placed = [
            (numbers == codes[item, block : block + 1, :]).astype(jnp.bfloat16)
            for item in range(experts)
        ]
        found = jnp.dot(
            jnp.concatenate(placed, axis=0),
            rows[block * tokens : (block + 1) * tokens, :],
            preferred_element_type=jnp.float32,
        ).astype(jnp.bfloat16)
        for item in range(experts):
            outs[item][span, :] = found[item * capacity : (item + 1) * capacity, :]

    @pl.when(pl.program_id(0) == 0)
    def weigh():
        for item in range(experts):
            for block in range(blocks):
                placed = numbers == codes[item, block : block + 1, :]
                span = slice(block * capacity, (block + 1) * capacity)
                row = chosen_weights[item, block : block + 1, :]
                outs[experts + item][span, :] = jnp.sum(
                    jnp.where(placed, row, 0.0), axis=1, keepdims=True
                )


def dispatch(codes, chosen_weights, rows, capacity):
    experts, blocks, _ = codes.shape
    slots = blocks * capacity
    width = rows.shape[1]
    block = min(width, 512)
    whole = pl.BlockSpec(codes.shape, lambda step: (0, 0, 0))
    results = pl.pallas_call(
        partial(dispatch_kernel, capacity=capacity, experts=experts),
        grid=(width // block,),
        in_specs=[whole, whole, pl.BlockSpec((rows.shape[0], block), lambda step: (0, step))],
        out_specs=[pl.BlockSpec((slots, block), lambda step: (0, step))] * experts
        + [pl.BlockSpec((slots, 1), lambda step: (0, 0))] * experts,
        out_shape=[jax.ShapeDtypeStruct((slots, width), jnp.bfloat16)] * experts
        + [jax.ShapeDtypeStruct((slots, 1), jnp.float32)] * experts,
    )(codes, chosen_weights, rows)
    return results[:experts], results[experts:]


def collect_kernel(codes, *refs, capacity, experts):
    out = refs[-1]
    blocks, tokens = codes.shape[1:]
    numbers = lax.broadcasted_iota(jnp.int32, (capacity, tokens), 0)
    for block in range(blocks):
        span = slice(block * capacity, (block + 1) * capacity)
        placed = [
            (numbers == codes[item, block : block + 1, :]).astype(jnp.bfloat16)
            for item in range(experts)
        ]
        total = lax.dot_general(
            jnp.concatenate(placed, axis=0),
            jnp.concatenate([refs[item][span, :] for item in range(experts)], axis=0),
            (((0,), (0,)), ((), ())),
            preferred_element_type=jnp.float32,
        )
        out[block * tokens : (block + 1) * tokens, :] = total.astype(jnp.bfloat16)


def collect(codes, arrays, capacity):
    experts, blocks, tokens = codes.shape
    slots, width = arrays[0].shape
    block = min(width, 512)
    return pl.pallas_call(
        partial(collect_kernel, capacity=capacity, experts=experts),
        grid=(width // block,),
        in_specs=[pl.BlockSpec(codes.shape, lambda step: (0, 0, 0))]
        + [pl.BlockSpec((slots, block), lambda step: (0, step))] * experts,
        out_specs=pl.BlockSpec((blocks * tokens, block), lambda step: (0, step)),
        out_shape=jax.ShapeDtypeStruct((blocks * tokens, width), jnp.bfloat16),
    )(codes, *arrays)


def exchange(array, offset):
    count = lax.axis_size("head")
    return lax.ppermute(array, "head", [(at, at ^ offset) for at in range(count)])


def head_pieces(array):
    return [array] + [exchange(array, offset) for offset in range(1, lax.axis_size("head"))]


def head_turn(pieces):
    return [pieces[0]] + [exchange(piece, at + 1) for at, piece in enumerate(pieces[1:])]


def add_all(pieces):
    total = pieces[0].astype(f32)
    for piece in pieces[1:]:
        total = total + piece.astype(f32)
    return total


def bit_order(turn):
    count = lax.axis_size("head").bit_length() - 1
    return [1 << ((turn + step) % count) for step in range(count)]


def gather_pieces(array, turn):
    pieces = {0: array}
    for bit in bit_order(turn):
        for offset in list(pieces):
            pieces[offset ^ bit] = exchange(pieces[offset], bit)
    return [pieces[offset] for offset in range(len(pieces))]


def scatter_pieces(pieces, turn):
    held = dict(enumerate(pieces))
    for bit in bit_order(turn):
        for offset in [item for item in held if item & bit]:
            piece = held.pop(offset).astype(bf16)
            arrived = exchange(piece, bit)
            held[offset ^ bit] = held[offset ^ bit].astype(f32) + arrived.astype(f32)
    return held[0]


def xor_order(array, axis):
    count = lax.axis_size("head")
    at = lax.axis_index("head")
    size = array.shape[axis] // count
    chunks = [
        lax.dynamic_slice_in_dim(array, (at ^ offset) * size, size, axis) for offset in range(count)
    ]
    return chunks


def xor_chunks(array, axis):
    return jnp.concatenate(xor_order(array, axis), axis=axis)


def absolute(pieces):
    at = lax.axis_index("head")
    result = []
    for place in range(len(pieces)):
        value = pieces[0]
        for offset in range(1, len(pieces)):
            value = jnp.where(at == place ^ offset, pieces[offset], value)
        result.append(value)
    return result


def move_rows(array, outer, inner, part):
    shaped = array.reshape(outer, inner, part, array.shape[1])
    return jnp.transpose(shaped, (1, 0, 2, 3)).reshape(array.shape)


def move_columns(array, outer, inner, part):
    shaped = array.reshape(array.shape[0], outer, inner, part)
    return jnp.transpose(shaped, (0, 2, 1, 3)).reshape(array.shape)


def layer(
    tokens,
    query_weight,
    key_weight,
    value_weight,
    output_weight,
    mixing_gain,
    query_gain,
    key_gain,
    routing_gain,
    router_weight,
    gate_weight,
    up_weight,
    down_weight,
    seq_lengths,
    dealt_order,
    expert_routes,
    slot_order,
    cotangent,
):
    heads_axis = lax.axis_size("head")
    blocks = lax.axis_size("blk")
    head_at = lax.axis_index("head")
    block_at = lax.axis_index("blk")
    rows, width = tokens.shape
    picks = expert_routes.shape[1]
    total_rows = dealt_order.shape[0]
    group = rows * heads_axis
    columns = width // heads_axis
    part = query_weight.shape[0]
    head_size = HDIM
    experts = router_weight.shape[1]
    local_experts = gate_weight.shape[0]
    capacity = 5 * rows * picks // (4 * experts)
    slots = blocks * capacity

    slices = [
        jnp.concatenate(chunks, axis=1)
        for chunks in zip(
            xor_order(key_weight, 1), xor_order(value_weight, 1), xor_order(query_weight, 1)
        )
    ]
    slices = head_turn(slices)
    output_rows = lax.all_gather(output_weight, "blk", axis=0, tiled=True)
    token_pieces = head_pieces(tokens)
    rows_here = jnp.stack(absolute(slices)).reshape(heads_axis * part, 3 * columns)
    pair_full = lax.all_gather(rows_here[:, : 2 * columns], "blk", axis=0, tiled=True)
    pair_full = move_rows(pair_full, blocks, heads_axis, part)
    query_full = lax.all_gather(rows_here[:, 2 * columns :], "blk", axis=0, tiled=True)
    query_full = move_rows(query_full, blocks, heads_axis, part)
    cot_all = lax.all_gather(cotangent, "blk", axis=0, tiled=True)

    small = jnp.concatenate(
        [
            mixing_gain[:, None],
            query_gain[:, None],
            key_gain[:, None],
            routing_gain[:, None],
            router_weight,
        ],
        axis=1,
    ).reshape(1, -1)
    codes = slot_codes(expert_routes, slot_order, experts, capacity).astype(bf16)
    sizes = small.shape[1]
    small = lax.all_gather(
        jnp.concatenate([small, codes.reshape(1, -1)], axis=1), "blk", axis=0, tiled=True
    )
    codes = small[:, sizes:].reshape(blocks, rows, experts).astype(jnp.int32)
    small = small[:, :sizes]
    small = jnp.stack(absolute(head_pieces(small))).reshape(width, 4 + experts)
    mixing_scale = small[:, 0].astype(f32)
    routing_scale = small[:, 3].astype(f32)
    query_scale = lax.dynamic_slice_in_dim(small[:, 1], head_at * columns, columns).astype(f32)
    key_scale = lax.dynamic_slice_in_dim(small[:, 2], head_at * columns, columns).astype(f32)
    router_full = small[:, 4:]
    codes_here = lax.dynamic_slice_in_dim(codes, block_at * local_experts, local_experts, 2)

    key_index = jnp.transpose(
        xor_chunks(dealt_order.reshape(heads_axis, blocks, rows), 0), (1, 0, 2)
    ).reshape(total_rows)
    key_seq = stream_layout(seq_lengths, key_index)[0]
    query_index = lax.dynamic_slice_in_dim(key_index, block_at * group, group)
    query_seq, query_position = stream_layout(seq_lengths, query_index)
    cosine, sine_part = rope_tables(query_position, head_size)
    tables = tile_lists(query_index, query_seq, key_index, key_seq, TILE)
    marks = attend_marks(query_index, query_index - query_position, key_index, TILE)

    gates, ups, downs = (
        [gather_pieces(weight[item], item) for item in range(local_experts)]
        for weight in (gate_weight, up_weight, down_weight)
    )

    normed = norm_rows(token_pieces, mixing_scale)
    normed_moved = move_columns(normed, heads_axis, blocks, part)
    key_raw, key_square = project(normed, pair_full, columns)
    value_heads = jnp.dot(normed, pair_full[:, columns:], preferred_element_type=f32)
    value_heads = value_heads.astype(bf16)
    key_squares = head_pieces(key_square)
    pairs, key_factor = rope_forward(
        key_squares, key_raw, key_scale, cosine, sine_part, value_heads, width
    )
    query_raw, query_square = project(normed, query_full, columns)
    query_squares = head_pieces(query_square)
    query_heads, query_factor = rope_forward(
        query_squares, query_raw, query_scale, cosine, sine_part, None, width
    )
    pairs_all = lax.all_gather(pairs, "blk", axis=0, tiled=True)
    attended, context, totals = attend_forward(query_heads, pairs_all, marks, tables, TILE)
    branch = jnp.dot(context, output_rows, preferred_element_type=f32).astype(bf16)
    branch = head_turn([branch[piece * rows : (piece + 1) * rows] for piece in range(heads_axis)])
    own_tokens = tokens.astype(f32)
    middle = own_tokens + add_all(branch)
    middle_factor = rms_factor(jnp.sum(middle * middle, axis=-1, keepdims=True), width)
    routed = (middle * middle_factor * routing_scale).astype(bf16)

    routed_all = lax.all_gather(xor_chunks(routed, 1), "blk", axis=0, tiled=True)
    probs = jax.nn.softmax(jnp.dot(routed, router_full, preferred_element_type=f32), axis=-1)
    probs_all = jax.nn.softmax(
        jnp.dot(routed_all, xor_chunks(router_full, 0), preferred_element_type=f32), axis=-1
    )
    weight_here = lax.dynamic_slice_in_dim(
        probs_all, block_at * local_experts, local_experts, 1
    ).reshape(blocks, rows, local_experts)
    slot_ids = jnp.arange(capacity, dtype=jnp.int32)
    codes_here = jnp.transpose(codes_here, (2, 0, 1))
    weight_here = jnp.transpose(weight_here, (2, 0, 1))
    placed = codes_here[:, :, None, :] == slot_ids[None, None, :, None]
    place = placed.astype(bf16)

    def arrange(flat, weighed=True):
        lots_here = weight_here if weighed else jnp.zeros(codes_here.shape, f32)
        if capacity % 16 == 0:
            return dispatch(codes_here, lots_here, flat, capacity)
        shaped = flat.reshape(blocks, rows, width)
        lots = jnp.sum(jnp.where(placed, lots_here[:, :, None, :], 0.0), axis=-1)
        return (
            [
                jnp.einsum("srt,std->srd", item, shaped).reshape(slots, width)
                for item in place
            ],
            [item.reshape(slots, 1) for item in lots],
        )

    arrived_cot = arrange(cot_all, False)[0]
    gate_all, up_all, down_all = (
        [jnp.concatenate(pieces, axis=0) for pieces in group_pieces]
        for group_pieces in (gates, ups, downs)
    )
    arrived, slot_weight = arrange(routed_all)
    offsets = jnp.bitwise_xor(head_at, jnp.arange(heads_axis, dtype=jnp.int32))
    results = [
        run_expert(
            offsets,
            arrived[item],
            arrived_cot[item],
            slot_weight[item],
            gate_all[item],
            up_all[item],
            down_all[item],
        )
        for item in range(local_experts)
    ]

    def back_to_rows(which):
        arrays = [result[which] for result in results]
        if capacity % 16 == 0:
            return collect(codes_here, arrays, capacity)
        return sum(
            jnp.einsum(
                "srt,srd->std",
                place[item],
                arrays[item].reshape(blocks, capacity, width),
                preferred_element_type=f32,
            )
            for item in range(local_experts)
        ).astype(bf16)

    incoming = back_to_rows(5)
    combined = back_to_rows(3)
    slot_grad = jnp.stack([result[4][0] for result in results])
    slot_grad = slot_grad.reshape(local_experts, blocks, capacity, 1)
    weight_grads = jnp.sum(jnp.where(placed, slot_grad, 0.0), axis=2)
    weight_grads = jnp.transpose(weight_grads, (1, 2, 0))
    stores = [
        (arrived[item], results[item][6], results[item][0], results[item][1], results[item][2])
        for item in range(local_experts)
    ]
    routed_grad = lax.psum_scatter(
        incoming.reshape(blocks * rows, width),
        "blk",
        scatter_dimension=0,
        tiled=True,
    )
    combined = lax.psum_scatter(
        combined.reshape(blocks * rows, width),
        "blk",
        scatter_dimension=0,
        tiled=True,
    )
    block_output = (middle + combined.astype(f32)).astype(bf16)
    prob_grad = lax.all_to_all(
        weight_grads, "blk", split_axis=0, concat_axis=2, tiled=True
    ).reshape(rows, experts)

    def pieces_of(left, right):
        size = left.shape[1] // heads_axis
        products = []
        for offset in range(heads_axis):
            product = jnp.dot(
                left[:, offset * size : (offset + 1) * size].T,
                right,
                preferred_element_type=f32,
            )
            products.append(lax.optimization_barrier(product.astype(bf16)))
        return products

    def stacked(items):
        return jnp.stack(items).astype(f32)

    down_out, gate_out, up_out = (
        stacked(
            [
                scatter_pieces(pieces_of(store[left], store[right]), item)
                for item, store in enumerate(stores)
            ]
        )
        for left, right in ((2, 1), (0, 3), (0, 4))
    )

    logit_grad = (
        probs * (prob_grad - jnp.sum(probs * prob_grad, axis=1, keepdims=True))
    ).astype(bf16)
    router_sum = jnp.dot(routed.T, logit_grad, preferred_element_type=f32)
    routed_grad = xor_chunks(routed_grad, 1).astype(f32) + jnp.dot(
        logit_grad, router_full.T, preferred_element_type=f32
    )
    scaled = routed_grad * routing_scale
    inner = jnp.mean(scaled * middle, axis=-1, keepdims=True)
    middle_grad = (
        cotangent.astype(f32) + middle_factor * scaled - middle * (middle_factor**3 * inner)
    )
    routing_sum = jnp.sum(routed_grad * middle * middle_factor, axis=0)

    branch_grad = head_pieces(middle_grad.astype(bf16))
    branch_grad = jnp.concatenate(branch_grad, axis=0)
    context_grad = jnp.dot(branch_grad, output_rows.T, preferred_element_type=f32).astype(bf16)
    output_sum = jnp.dot(context.T, branch_grad, preferred_element_type=f32).astype(bf16)
    output_out = lax.psum_scatter(output_sum, "blk", scatter_dimension=0, tiled=True)
    query_back, pairs_back = attend_backward(
        query_heads, pairs_all, context_grad, attended, totals, marks, tables, TILE
    )
    pairs_back = lax.psum_scatter(pairs_back, "blk", scatter_dimension=0, tiled=True)
    query_scaled, query_inner, querynorm_sum = rope_backward(
        query_back, query_raw, query_factor, query_scale, cosine, sine_part, 1
    )
    query_inner = head_pieces(query_inner)
    query_raw_grad = raw_backward(query_inner, query_scaled, query_raw, query_factor, None, width)
    query_sum = jnp.dot(normed_moved.T, query_raw_grad, preferred_element_type=f32).astype(bf16)
    query_sum = lax.psum_scatter(query_sum, "blk", scatter_dimension=0, tiled=True)
    normed_part = jnp.dot(query_raw_grad, query_full.T, preferred_element_type=f32)
    key_scaled, key_inner, keynorm_sum = rope_backward(
        pairs_back, key_raw, key_factor, key_scale, cosine, sine_part, 2
    )
    key_inner = head_pieces(key_inner)
    pair_grad = raw_backward(key_inner, key_scaled, key_raw, key_factor, pairs_back, width)
    pair_sum = jnp.dot(normed_moved.T, pair_grad, preferred_element_type=f32).astype(bf16)
    pair_sum = lax.psum_scatter(pair_sum, "blk", scatter_dimension=0, tiled=True)
    normed_part = normed_part + jnp.dot(pair_grad, pair_full.T, preferred_element_type=f32)
    normed_part = normed_part.astype(bf16)
    normed_part = head_turn(
        [normed_part[piece * rows : (piece + 1) * rows] for piece in range(heads_axis)]
    )
    normed_grad = add_all(normed_part)
    own_factor = rms_factor(jnp.sum(own_tokens * own_tokens, axis=-1, keepdims=True), width)
    scaled = normed_grad * mixing_scale
    inner = jnp.mean(scaled * own_tokens, axis=-1, keepdims=True)
    tokens_grad = middle_grad + own_factor * scaled - own_tokens * (own_factor**3 * inner)
    mixing_sum = jnp.sum(normed_grad * own_tokens * own_factor, axis=0)

    def turned_back(array):
        return jnp.stack(
            [
                jnp.concatenate(absolute(list(pieces)), axis=1).astype(f32)
                for pieces in zip(
                    *(
                        [piece[:, at : at + columns] for at in range(0, piece.shape[1], columns)]
                        for piece in head_turn(xor_order(array, 0))
                    )
                )
            ]
        )

    query_out = turned_back(query_sum)[0]
    pair_out = turned_back(pair_sum)

    blank = jnp.zeros((heads_axis, columns), f32)
    query_line = lax.dynamic_update_slice(blank, querynorm_sum, (head_at, 0)).reshape(width)
    key_line = lax.dynamic_update_slice(blank, keynorm_sum, (head_at, 0)).reshape(width)
    lines = jnp.concatenate(
        [
            mixing_sum[:, None],
            query_line[:, None],
            key_line[:, None],
            routing_sum[:, None],
            router_sum,
        ],
        axis=1,
    ).reshape(heads_axis, -1)
    lines = add_all(head_turn(xor_order(lines, 0)))
    lines = lax.all_to_all(lines.reshape(blocks, -1), "blk", 0, 0, tiled=True)
    lines = jnp.sum(lines, axis=0).reshape(part, 4 + experts)
    return (
        block_output,
        tokens_grad,
        query_out,
        pair_out[0],
        pair_out[1],
        output_out.astype(f32),
        lines[:, 0],
        lines[:, 1],
        lines[:, 2],
        lines[:, 3],
        lines[:, 4:],
        gate_out,
        up_out,
        down_out,
    )


def solution(mesh):
    in_specs = (
        P(("head", "blk"), None),
        P(("head", "blk"), None),
        P(("head", "blk"), None),
        P(("head", "blk"), None),
        P(("head", "blk"), None),
        P(("head", "blk")),
        P(("head", "blk")),
        P(("head", "blk")),
        P(("head", "blk")),
        P(("head", "blk"), None),
        P("blk", "head", None),
        P("blk", "head", None),
        P("blk", "head", None),
        P(),
        P(),
        P(("head", "blk"), None),
        P(("head", "blk"), None),
        P(("head", "blk"), None),
    )
    out_specs = (
        P(("head", "blk"), None),
        P(("head", "blk"), None),
        P(("head", "blk"), None),
        P(("head", "blk"), None),
        P(("head", "blk"), None),
        P(("head", "blk"), None),
        P(("head", "blk")),
        P(("head", "blk")),
        P(("head", "blk")),
        P(("head", "blk")),
        P(("head", "blk"), None),
        P("blk", "head", None),
        P("blk", "head", None),
        P("blk", "head", None),
    )
    return jax.shard_map(layer, mesh=mesh, in_specs=in_specs, out_specs=out_specs, check_vma=False)
```

```python
from functools import partial
import math

import jax
import jax.numpy as jnp
import numpy as np
from jax import lax
from jax.experimental import pallas as pl
from jax.experimental.pallas import tpu as pltpu
from jax.sharding import PartitionSpec as P


HDIM = 128
TILE = 256
LOG2E = 1.4426950408889634
norm_eps = 1e-05
rope_base = 10000.0
f32 = jnp.float32
bf16 = jnp.bfloat16


def rms_factor(square_sum, width):
    return lax.rsqrt(square_sum / width + norm_eps)


def rope_tables(position, head_size):
    half = head_size // 2
    freqs = rope_base ** (-(np.arange(half, dtype=np.float64) * 2.0) / head_size)
    angles = position.astype(f32)[:, None] * jnp.asarray(freqs.astype(np.float32))[None, :]
    cosine = jnp.cos(angles)
    sine_part = jnp.sin(angles)
    return (
        jnp.concatenate([cosine, cosine], axis=1),
        jnp.concatenate([-sine_part, sine_part], axis=1),
    )


def column_of(pieces):
    count = len(pieces)
    rows = pieces[0].shape[1] // count
    total = pieces[0][...]
    for offset in range(1, count):
        parts = [
            pieces[offset][:, (at ^ offset) * rows : ((at ^ offset) + 1) * rows]
            for at in range(count)
        ]
        total = total + jnp.concatenate(parts, axis=1)
    return jnp.transpose(jnp.broadcast_to(total, (8, total.shape[1])))[:, :1]


def turned(value, cosine, sine_part):
    return value * cosine + pltpu.roll(value, HDIM // 2, 1) * sine_part


def rope_kernel(*refs, count, width, paired):
    squares = refs[:count]
    raw, scale, cosine, sine_part = refs[count : count + 4]
    out, factors = refs[-2:]
    factor = lax.rsqrt(column_of(squares) / width + norm_eps)
    factors[...] = jnp.broadcast_to(factor, factors.shape)
    for head in range(raw.shape[1] // HDIM):
        span = slice(head * HDIM, (head + 1) * HDIM)
        value = turned(raw[:, span] * factor * scale[:, span], cosine[...], sine_part[...])
        if paired:
            start = 2 * head * HDIM
            out[:, start : start + HDIM] = value.astype(jnp.bfloat16)
            out[:, start + HDIM : start + 2 * HDIM] = refs[count + 4][:, span]
        else:
            out[:, span] = value.astype(jnp.bfloat16)


def rope_forward(squares, raw, scale, cosine, sine_part, values, width):
    group, columns = raw.shape
    paired = values is not None
    extra = (values,) if paired else ()
    return pl.pallas_call(
        partial(rope_kernel, count=len(squares), width=width, paired=paired),
        out_shape=[
            jax.ShapeDtypeStruct((group, columns * (2 if paired else 1)), jnp.bfloat16),
            jax.ShapeDtypeStruct((group, HDIM), jnp.float32),
        ],
    )(*squares, raw, scale[None], cosine, sine_part, *extra)


def unrope_kernel(back, raw, factors, scale, cosine, sine_part, scaled, inner, gain, *, stride):
    group = raw.shape[0]
    total = jnp.zeros((group, HDIM), jnp.float32)
    for head in range(raw.shape[1] // HDIM):
        span = slice(head * HDIM, (head + 1) * HDIM)
        start = stride * head * HDIM
        grad = back[:, start : start + HDIM].astype(jnp.float32)
        turn = turned(grad, cosine[...], -sine_part[...])
        product = turn * raw[:, span]
        gain[:, span] = jnp.sum(product * factors[...], axis=0, keepdims=True)
        scaled[:, span] = turn * scale[:, span]
        total = total + product * scale[:, span]
    sums = jnp.broadcast_to(jnp.sum(total, axis=1, keepdims=True), (group, HDIM))
    inner[...] = jnp.transpose(sums)[:1, :]


def rope_backward(back, raw, factors, scale, cosine, sine_part, stride):
    group, columns = raw.shape
    return pl.pallas_call(
        partial(unrope_kernel, stride=stride),
        out_shape=[
            jax.ShapeDtypeStruct((group, columns), jnp.float32),
            jax.ShapeDtypeStruct((1, group), jnp.float32),
            jax.ShapeDtypeStruct((1, columns), jnp.float32),
        ],
    )(back, raw, factors, scale[None], cosine, sine_part)


def raw_kernel(*refs, count, width, paired):
    scaled, raw, factors = refs[count : count + 3]
    out = refs[-1]
    inner = column_of(refs[:count]) / width
    factor = factors[:, :1]
    columns = raw.shape[1]
    slope = factor * factor * factor * inner
    for head in range(columns // HDIM):
        span = slice(head * HDIM, (head + 1) * HDIM)
        out[:, span] = (factor * scaled[:, span] - raw[:, span] * slope).astype(jnp.bfloat16)
        if paired:
            start = (2 * head + 1) * HDIM
            out[:, columns + head * HDIM : columns + (head + 1) * HDIM] = refs[count + 3][
                :, start : start + HDIM
            ]


def raw_backward(inner, scaled, raw, factors, pairs_back, width):
    group, columns = raw.shape
    paired = pairs_back is not None
    extra = (pairs_back,) if paired else ()
    return pl.pallas_call(
        partial(raw_kernel, count=len(inner), width=width, paired=paired),
        out_shape=jax.ShapeDtypeStruct((group, columns * (2 if paired else 1)), jnp.bfloat16),
    )(*inner, scaled, raw, factors, *extra)


def norm_kernel(*refs, count):
    scale, out = refs[count], refs[count + 1]
    rows, width = refs[0].shape
    for place in range(count):
        value = refs[place][...].astype(jnp.float32)
        square = jnp.sum(value * value, axis=1, keepdims=True)
        factor = lax.rsqrt(square / width + norm_eps)
        out[place * rows : (place + 1) * rows, :] = (value * factor * scale[...]).astype(
            jnp.bfloat16
        )


def norm_rows(pieces, scale):
    rows, width = pieces[0].shape
    return pl.pallas_call(
        partial(norm_kernel, count=len(pieces)),
        out_shape=jax.ShapeDtypeStruct((rows * len(pieces), width), jnp.bfloat16),
        name="norm_rows",
    )(*pieces, scale[None])


def project_kernel(normed, weight, raw, square, total):
    step = pl.program_id(0)

    @pl.when(step == 0)
    def start():
        total[...] = jnp.zeros_like(total)

    value = jnp.dot(normed[...], weight[...], preferred_element_type=jnp.float32)
    raw[...] = value
    for at in range(0, value.shape[1], HDIM):
        total[...] += value[:, at : at + HDIM] * value[:, at : at + HDIM]

    @pl.when(step == pl.num_programs(0) - 1)
    def finish():
        sums = jnp.sum(total[...], axis=1, keepdims=True)
        square[...] = jnp.transpose(jnp.broadcast_to(sums, total.shape))[:1, :]


def project(normed, weight, columns):
    group, width = normed.shape
    block = min(columns, 256)
    return pl.pallas_call(
        project_kernel,
        grid=(columns // block,),
        in_specs=[
            pl.BlockSpec((group, width), lambda step: (0, 0)),
            pl.BlockSpec((width, block), lambda step: (0, step)),
        ],
        out_specs=[
            pl.BlockSpec((group, block), lambda step: (0, step)),
            pl.BlockSpec((1, group), lambda step: (0, 0)),
        ],
        out_shape=[
            jax.ShapeDtypeStruct((group, columns), jnp.float32),
            jax.ShapeDtypeStruct((1, group), jnp.float32),
        ],
        scratch_shapes=[pltpu.VMEM((group, HDIM), jnp.float32)],
    )(normed, weight)


def slot_codes(routes, ordering, experts, capacity):
    expert_ids = jnp.arange(experts, dtype=jnp.int32)
    absent = jnp.int32(1 << 30)
    chosen = routes[:, :, None] == expert_ids[None, None, :]
    order = jnp.min(jnp.where(chosen, ordering[:, :, None], absent), axis=1)
    rank = jnp.sum((order[None, :, :] < order[:, None, :]).astype(jnp.int32), axis=1)
    return jnp.where((order < absent) & (rank < capacity), rank, -1)


def stream_layout(seq_lengths, stream_index):
    ends = jnp.cumsum(seq_lengths)
    starts = ends - seq_lengths
    passed = (stream_index[:, None] >= ends[None, :]).astype(jnp.int32)
    sequence = jnp.sum(passed, axis=1)
    owner = sequence[:, None] == jnp.arange(seq_lengths.shape[0], dtype=jnp.int32)[None, :]
    opening = jnp.sum(jnp.where(owner, starts[None, :], 0), axis=1)
    return (sequence, stream_index - opening)


def tile_lists(query_index, query_seq, key_index, key_seq, tile):
    query_tiles = query_index.shape[0] // tile
    key_tiles = key_index.shape[0] // tile
    query_marks = query_index.reshape(query_tiles, tile)
    query_seqs = query_seq.reshape(query_tiles, tile)
    key_marks = key_index.reshape(key_tiles, tile)
    key_seqs = key_seq.reshape(key_tiles, tile)
    early = jnp.min(key_marks, axis=1)[None, :] <= jnp.max(query_marks, axis=1)[:, None]
    above = jnp.max(key_seqs, axis=1)[None, :] >= jnp.min(query_seqs, axis=1)[:, None]
    below = jnp.min(key_seqs, axis=1)[None, :] <= jnp.max(query_seqs, axis=1)[:, None]
    live = (early & above & below).astype(jnp.int32)
    order = jnp.cumsum(live, axis=1) - 1
    numbers = jnp.arange(key_tiles, dtype=jnp.int32)
    hits = (order[:, :, None] == numbers[None, None, :]) & (live[:, :, None] > 0)
    listed = jnp.sum(jnp.where(hits, numbers[None, :, None], 0), axis=1)
    return (listed.astype(jnp.int32), jnp.sum(live, axis=1).astype(jnp.int32), live)


def spread(vector):
    return jnp.broadcast_to(vector[:, None], (vector.shape[0], 128))


def twice(value, count):
    return value if count == 1 else jnp.concatenate([value] * count, axis=1)


def forward_kernel(
    listed, counts, query, pairs, at, opening, key_at, attended, context, totals, total, acc, *, tile
):
    lanes = 128
    copies = tile // lanes
    factor = LOG2E / math.sqrt(HDIM)
    for step in range(query.shape[0] // tile):
        span = slice(step * tile, (step + 1) * tile)
        acc[...] = jnp.zeros_like(acc)
        total[...] = jnp.zeros_like(total)

        def visit(turn, carry):
            number = listed[step, turn]
            start = pl.multiple_of(number * tile, tile)
            scores = lax.dot_general(
                query[span, :],
                pairs[pl.ds(start, tile), :HDIM],
                (((1,), (1,)), ((), ())),
                preferred_element_type=jnp.float32,
            )
            marks = key_at[pl.ds(number, 1), :]
            allowed = (marks <= twice(at[span, :], copies)) & (
                marks >= twice(opening[span, :], copies)
            )
            expo = jnp.where(allowed, jnp.exp2(scores * factor), 0.0)
            partial_sum = expo[:, :lanes]
            for copy in range(1, copies):
                partial_sum = partial_sum + expo[:, copy * lanes : (copy + 1) * lanes]
            total[...] += partial_sum
            acc[...] += jnp.dot(
                expo.astype(jnp.bfloat16),
                pairs[pl.ds(start, tile), HDIM:],
                preferred_element_type=jnp.float32,
            )
            return carry

        lax.fori_loop(0, counts[step], visit, 0)
        full = jnp.sum(total[...], axis=1, keepdims=True)
        result = acc[...] / full
        attended[span, :] = result
        context[span, :] = result.astype(jnp.bfloat16)
        totals[span, :] = jnp.broadcast_to(full, (tile, lanes))


def attend_forward(queries, pairs, marks, tables, tile):
    group, columns = queries.shape
    total_rows = pairs.shape[0]
    listed, counts, _ = tables
    at, opening, key_at = marks[0], marks[1], marks[2]
    heads = columns // HDIM
    lane = lambda rows: pl.BlockSpec((rows, HDIM), lambda h, *refs: (0, h))
    wide = pl.BlockSpec((total_rows, 2 * HDIM), lambda h, *refs: (0, h))
    fixed = lambda array: pl.BlockSpec(array.shape, lambda h, *refs: (0, 0))
    return pl.pallas_call(
        partial(forward_kernel, tile=tile),
        grid_spec=pltpu.PrefetchScalarGridSpec(
            num_scalar_prefetch=2,
            grid=(heads,),
            in_specs=[
                lane(group),
                wide,
                fixed(at),
                fixed(opening),
                fixed(key_at),
            ],
            out_specs=[lane(group), lane(group), lane(group)],
            scratch_shapes=[
                pltpu.VMEM((tile, HDIM), jnp.float32),
                pltpu.VMEM((tile, HDIM), jnp.float32),
            ],
        ),
        out_shape=[
            jax.ShapeDtypeStruct((group, columns), jnp.float32),
            jax.ShapeDtypeStruct((group, columns), jnp.bfloat16),
            jax.ShapeDtypeStruct((group, columns), jnp.float32),
        ],
        name="attend_forward",
    )(listed, counts, queries, pairs, at, opening, key_at)


def backward_kernel(
    live,
    query,
    pairs,
    grad,
    attended,
    totals,
    at_row,
    opening_row,
    key_col,
    query_out,
    pairs_out,
    scaled,
    offset,
    query_acc,
    key_acc,
    value_acc,
    *,
    tile,
):
    copies = tile // 128
    steps = query.shape[0] // tile
    factor = 1.0 / math.sqrt(HDIM)
    grads = grad[...].astype(jnp.float32)
    scaled[...] = (grads / totals[...]).astype(jnp.bfloat16)
    sums = jnp.sum(grads * attended[...], axis=1, keepdims=True) / totals[...]
    offset[...] = jnp.transpose(sums)[:8, :]
    query_acc[...] = jnp.zeros_like(query_acc)

    def visit(number, carry):
        start = pl.multiple_of(number * tile, tile)
        window = pl.ds(start, tile)
        key_acc[...] = jnp.zeros_like(key_acc)
        value_acc[...] = jnp.zeros_like(value_acc)
        for step in range(steps):
            span = slice(step * tile, (step + 1) * tile)

            @pl.when(live[step, number] > 0)
            def unused():
                scores = lax.dot_general(
                    pairs[window, :HDIM],
                    query[span, :],
                    (((1,), (1,)), ((), ())),
                    preferred_element_type=jnp.float32,
                )
                marks = twice(key_col[window, :], copies)
                allowed = (marks <= at_row[:, span]) & (marks >= opening_row[:, span])
                expo = jnp.where(allowed, jnp.exp2(scores * (factor * LOG2E)), 0.0)
                inner = lax.dot_general(
                    pairs[window, HDIM:],
                    scaled[span, :],
                    (((1,), (1,)), ((), ())),
                    preferred_element_type=jnp.float32,
                )
                back = (expo * (inner - offset[0:1, span])).astype(jnp.bfloat16)
                key_acc[...] += jnp.dot(back, query[span, :], preferred_element_type=jnp.float32)
                value_acc[...] += jnp.dot(
                    expo.astype(jnp.bfloat16), scaled[span, :], preferred_element_type=jnp.float32
                )
                query_acc[span, :] += lax.dot_general(
                    back,
                    pairs[window, :HDIM],
                    (((0,), (0,)), ((), ())),
                    preferred_element_type=jnp.float32,
                )

        pairs_out[window, :HDIM] = (key_acc[...] * factor).astype(jnp.bfloat16)
        pairs_out[window, HDIM:] = value_acc[...].astype(jnp.bfloat16)
        return carry

    lax.fori_loop(0, pairs.shape[0] // tile, visit, 0)
    query_out[...] = (query_acc[...] * factor).astype(jnp.bfloat16)


def attend_backward(queries, pairs, grads, attended, totals, marks, tables, tile):
    group, columns = queries.shape
    total_rows = pairs.shape[0]
    live = tables[2]
    at_row, opening_row, key_col = marks[3], marks[4], marks[5]
    heads = columns // HDIM
    lane = lambda rows: pl.BlockSpec((rows, HDIM), lambda h, *refs: (0, h))
    wide = pl.BlockSpec((total_rows, 2 * HDIM), lambda h, *refs: (0, h))
    fixed = lambda array: pl.BlockSpec(array.shape, lambda h, *refs: (0, 0))
    return pl.pallas_call(
        partial(backward_kernel, tile=tile),
        grid_spec=pltpu.PrefetchScalarGridSpec(
            num_scalar_prefetch=1,
            grid=(heads,),
            in_specs=[
                lane(group),
                wide,
                lane(group),
                lane(group),
                lane(group),
                fixed(at_row),
                fixed(opening_row),
                fixed(key_col),
            ],
            out_specs=[lane(group), wide],
            scratch_shapes=[
                pltpu.VMEM((group, HDIM), jnp.bfloat16),
                pltpu.VMEM((8, group), jnp.float32),
                pltpu.VMEM((group, HDIM), jnp.float32),
                pltpu.VMEM((tile, HDIM), jnp.float32),
                pltpu.VMEM((tile, HDIM), jnp.float32),
            ],
        ),
        out_shape=[
            jax.ShapeDtypeStruct((group, columns), jnp.bfloat16),
            jax.ShapeDtypeStruct((total_rows, 2 * columns), jnp.bfloat16),
        ],
        name="attend_backward",
    )(live, queries, pairs, grads, attended, totals, at_row, opening_row, key_col)


def attend_marks(query_index, query_start, key_index, tile):
    return (
        spread(query_index),
        spread(query_start),
        key_index.reshape(-1, tile),
        query_index[None, :],
        query_start[None, :],
        spread(key_index),
    )


def expert_kernel(
    perm,
    arrived,
    cot,
    weight,
    gate_weight,
    up_weight,
    down_weight,
    active,
    gate_grad,
    up_grad,
    weighted,
    inner,
    incoming,
    produced_grad,
    out_acc,
    in_acc,
):
    step = pl.program_id(0)

    @pl.when(step == 0)
    def start():
        produced_grad[...] = (weight[...] * cot[...].astype(jnp.float32)).astype(jnp.bfloat16)
        out_acc[...] = jnp.zeros_like(out_acc)
        in_acc[...] = jnp.zeros_like(in_acc)

    gate = jnp.dot(arrived[...], gate_weight[...], preferred_element_type=jnp.float32)
    upward = jnp.dot(arrived[...], up_weight[...], preferred_element_type=jnp.float32)
    active_grad = lax.dot_general(
        produced_grad[...],
        down_weight[...],
        (((1,), (1,)), ((), ())),
        preferred_element_type=jnp.float32,
    )
    sigmoid = 1.0 / (1.0 + jnp.exp(-gate))
    silu = gate * sigmoid
    hidden = (silu * upward).astype(jnp.bfloat16)
    active[...] = hidden
    gate_back = (active_grad * upward * sigmoid * (1.0 + gate * (1.0 - sigmoid))).astype(
        jnp.bfloat16
    )
    up_back = (active_grad * silu).astype(jnp.bfloat16)
    gate_grad[...] = gate_back
    up_grad[...] = up_back
    out_acc[...] += jnp.dot(hidden, down_weight[...], preferred_element_type=jnp.float32)
    in_acc[...] += lax.dot_general(
        jnp.concatenate([gate_back, up_back], axis=1),
        jnp.concatenate([gate_weight[...], up_weight[...]], axis=1),
        (((1,), (1,)), ((), ())),
        preferred_element_type=jnp.float32,
    )

    @pl.when(step == pl.num_programs(0) - 1)
    def finish():
        produced = out_acc[...].astype(jnp.bfloat16).astype(jnp.float32)
        weighted[...] = (weight[...] * produced).astype(jnp.bfloat16)
        sums = jnp.sum(cot[...].astype(jnp.float32) * produced, axis=1, keepdims=True)
        inner[...] = jnp.transpose(jnp.broadcast_to(sums, (sums.shape[0], 128)))[:8, :]
        incoming[...] = in_acc[...].astype(jnp.bfloat16)


def run_expert(perm, arrived, cot, weight, gate_all, up_all, down_all):
    slots, width = arrived.shape
    hidden = gate_all.shape[1]
    steps = perm.shape[0]
    chunk = hidden // steps
    rows = pl.BlockSpec((slots, width), lambda c, perm: (0, 0))
    natural = pl.BlockSpec((slots, chunk), lambda c, perm: (0, perm[c]))
    turned_in = pl.BlockSpec((width, chunk), lambda c, perm: (0, perm[c]))
    wide = jax.ShapeDtypeStruct((slots, width), jnp.bfloat16)
    thin = jax.ShapeDtypeStruct((slots, hidden), jnp.bfloat16)
    return pl.pallas_call(
        expert_kernel,
        grid_spec=pltpu.PrefetchScalarGridSpec(
            num_scalar_prefetch=1,
            grid=(steps,),
            in_specs=[
                rows,
                rows,
                pl.BlockSpec((slots, 1), lambda c, perm: (0, 0)),
                turned_in,
                turned_in,
                pl.BlockSpec((chunk, width), lambda c, perm: (c, 0)),
            ],
            out_specs=[
                pl.BlockSpec((slots, chunk), lambda c, perm: (0, c)),
                natural,
                natural,
                rows,
                pl.BlockSpec((8, slots), lambda c, perm: (0, 0)),
                rows,
                rows,
            ],
            scratch_shapes=[
                pltpu.VMEM((slots, width), jnp.float32),
                pltpu.VMEM((slots, width), jnp.float32),
            ],
        ),
        out_shape=[
            thin,
            thin,
            thin,
            wide,
            jax.ShapeDtypeStruct((8, slots), jnp.float32),
            wide,
            wide,
        ],
        name="run_expert",
    )(perm, arrived, cot, weight, gate_all, up_all, down_all)


def dispatch_kernel(codes, chosen_weights, rows, *outs, capacity, experts):
    blocks, tokens = codes.shape[1:]
    numbers = lax.broadcasted_iota(jnp.int32, (capacity, tokens), 0)
    for block in range(blocks):
        span = slice(block * capacity, (block + 1) * capacity)
        placed = [
            (numbers == codes[item, block : block + 1, :]).astype(jnp.bfloat16)
            for item in range(experts)
        ]
        found = jnp.dot(
            jnp.concatenate(placed, axis=0),
            rows[block * tokens : (block + 1) * tokens, :],
            preferred_element_type=jnp.float32,
        ).astype(jnp.bfloat16)
        for item in range(experts):
            outs[item][span, :] = found[item * capacity : (item + 1) * capacity, :]

    @pl.when(pl.program_id(0) == 0)
    def weigh():
        for item in range(experts):
            for block in range(blocks):
                placed = numbers == codes[item, block : block + 1, :]
                span = slice(block * capacity, (block + 1) * capacity)
                row = chosen_weights[item, block : block + 1, :]
                outs[experts + item][span, :] = jnp.sum(
                    jnp.where(placed, row, 0.0), axis=1, keepdims=True
                )


def dispatch(codes, chosen_weights, rows, capacity):
    experts, blocks, _ = codes.shape
    slots = blocks * capacity
    width = rows.shape[1]
    block = min(width, 512)
    whole = pl.BlockSpec(codes.shape, lambda step: (0, 0, 0))
    results = pl.pallas_call(
        partial(dispatch_kernel, capacity=capacity, experts=experts),
        grid=(width // block,),
        in_specs=[whole, whole, pl.BlockSpec((rows.shape[0], block), lambda step: (0, step))],
        out_specs=[pl.BlockSpec((slots, block), lambda step: (0, step))] * experts
        + [pl.BlockSpec((slots, 1), lambda step: (0, 0))] * experts,
        out_shape=[jax.ShapeDtypeStruct((slots, width), jnp.bfloat16)] * experts
        + [jax.ShapeDtypeStruct((slots, 1), jnp.float32)] * experts,
    )(codes, chosen_weights, rows)
    return results[:experts], results[experts:]


def collect_kernel(codes, *refs, capacity, experts):
    out = refs[-1]
    blocks, tokens = codes.shape[1:]
    numbers = lax.broadcasted_iota(jnp.int32, (capacity, tokens), 0)
    for block in range(blocks):
        span = slice(block * capacity, (block + 1) * capacity)
        placed = [
            (numbers == codes[item, block : block + 1, :]).astype(jnp.bfloat16)
            for item in range(experts)
        ]
        total = lax.dot_general(
            jnp.concatenate(placed, axis=0),
            jnp.concatenate([refs[item][span, :] for item in range(experts)], axis=0),
            (((0,), (0,)), ((), ())),
            preferred_element_type=jnp.float32,
        )
        out[block * tokens : (block + 1) * tokens, :] = total.astype(jnp.bfloat16)


def collect(codes, arrays, capacity):
    experts, blocks, tokens = codes.shape
    slots, width = arrays[0].shape
    block = min(width, 512)
    return pl.pallas_call(
        partial(collect_kernel, capacity=capacity, experts=experts),
        grid=(width // block,),
        in_specs=[pl.BlockSpec(codes.shape, lambda step: (0, 0, 0))]
        + [pl.BlockSpec((slots, block), lambda step: (0, step))] * experts,
        out_specs=pl.BlockSpec((blocks * tokens, block), lambda step: (0, step)),
        out_shape=jax.ShapeDtypeStruct((blocks * tokens, width), jnp.bfloat16),
    )(codes, *arrays)


def exchange(array, offset):
    count = lax.axis_size("head")
    return lax.ppermute(array, "head", [(at, at ^ offset) for at in range(count)])


def head_pieces(array):
    return [array] + [exchange(array, offset) for offset in range(1, lax.axis_size("head"))]


def head_turn(pieces):
    return [pieces[0]] + [exchange(piece, at + 1) for at, piece in enumerate(pieces[1:])]


def add_all(pieces):
    total = pieces[0].astype(f32)
    for piece in pieces[1:]:
        total = total + piece.astype(f32)
    return total


def bit_order(turn):
    count = lax.axis_size("head").bit_length() - 1
    return [1 << ((turn + step) % count) for step in range(count)]


def gather_pieces(array, turn):
    pieces = {0: array}
    for bit in bit_order(turn):
        for offset in list(pieces):
            pieces[offset ^ bit] = exchange(pieces[offset], bit)
    return [pieces[offset] for offset in range(len(pieces))]


def scatter_pieces(pieces, turn):
    held = dict(enumerate(pieces))
    for bit in bit_order(turn):
        for offset in [item for item in held if item & bit]:
            piece = held.pop(offset).astype(bf16)
            arrived = exchange(piece, bit)
            held[offset ^ bit] = held[offset ^ bit].astype(f32) + arrived.astype(f32)
    return held[0]


def xor_order(array, axis):
    count = lax.axis_size("head")
    at = lax.axis_index("head")
    size = array.shape[axis] // count
    chunks = [
        lax.dynamic_slice_in_dim(array, (at ^ offset) * size, size, axis) for offset in range(count)
    ]
    return chunks


def xor_chunks(array, axis):
    return jnp.concatenate(xor_order(array, axis), axis=axis)


def absolute(pieces):
    at = lax.axis_index("head")
    result = []
    for place in range(len(pieces)):
        value = pieces[0]
        for offset in range(1, len(pieces)):
            value = jnp.where(at == place ^ offset, pieces[offset], value)
        result.append(value)
    return result


def move_rows(array, outer, inner, part):
    shaped = array.reshape(outer, inner, part, array.shape[1])
    return jnp.transpose(shaped, (1, 0, 2, 3)).reshape(array.shape)


def move_columns(array, outer, inner, part):
    shaped = array.reshape(array.shape[0], outer, inner, part)
    return jnp.transpose(shaped, (0, 2, 1, 3)).reshape(array.shape)


def layer(
    tokens,
    query_weight,
    key_weight,
    value_weight,
    output_weight,
    mixing_gain,
    query_gain,
    key_gain,
    routing_gain,
    router_weight,
    gate_weight,
    up_weight,
    down_weight,
    seq_lengths,
    dealt_order,
    expert_routes,
    slot_order,
    cotangent,
):
    heads_axis = lax.axis_size("head")
    blocks = lax.axis_size("blk")
    head_at = lax.axis_index("head")
    block_at = lax.axis_index("blk")
    rows, width = tokens.shape
    picks = expert_routes.shape[1]
    total_rows = dealt_order.shape[0]
    group = rows * heads_axis
    columns = width // heads_axis
    part = query_weight.shape[0]
    head_size = HDIM
    experts = router_weight.shape[1]
    local_experts = gate_weight.shape[0]
    capacity = 5 * rows * picks // (4 * experts)
    slots = blocks * capacity

    slices = [
        jnp.concatenate(chunks, axis=1)
        for chunks in zip(
            xor_order(key_weight, 1), xor_order(value_weight, 1), xor_order(query_weight, 1)
        )
    ]
    slices = head_turn(slices)
    output_rows = lax.all_gather(output_weight, "blk", axis=0, tiled=True)
    token_pieces = head_pieces(tokens)
    rows_here = jnp.stack(absolute(slices)).reshape(heads_axis * part, 3 * columns)
    pair_full = lax.all_gather(rows_here[:, : 2 * columns], "blk", axis=0, tiled=True)
    pair_full = move_rows(pair_full, blocks, heads_axis, part)
    query_full = lax.all_gather(rows_here[:, 2 * columns :], "blk", axis=0, tiled=True)
    query_full = move_rows(query_full, blocks, heads_axis, part)
    cot_all = lax.all_gather(cotangent, "blk", axis=0, tiled=True)

    small = jnp.concatenate(
        [
            mixing_gain[:, None],
            query_gain[:, None],
            key_gain[:, None],
            routing_gain[:, None],
            router_weight,
        ],
        axis=1,
    ).reshape(1, -1)
    codes = slot_codes(expert_routes, slot_order, experts, capacity).astype(bf16)
    sizes = small.shape[1]
    small = lax.all_gather(
        jnp.concatenate([small, codes.reshape(1, -1)], axis=1), "blk", axis=0, tiled=True
    )
    codes = small[:, sizes:].reshape(blocks, rows, experts).astype(jnp.int32)
    small = small[:, :sizes]
    small = jnp.stack(absolute(head_pieces(small))).reshape(width, 4 + experts)
    mixing_scale = small[:, 0].astype(f32)
    routing_scale = small[:, 3].astype(f32)
    query_scale = lax.dynamic_slice_in_dim(small[:, 1], head_at * columns, columns).astype(f32)
    key_scale = lax.dynamic_slice_in_dim(small[:, 2], head_at * columns, columns).astype(f32)
    router_full = small[:, 4:]
    codes_here = lax.dynamic_slice_in_dim(codes, block_at * local_experts, local_experts, 2)

    key_index = jnp.transpose(
        xor_chunks(dealt_order.reshape(heads_axis, blocks, rows), 0), (1, 0, 2)
    ).reshape(total_rows)
    key_seq = stream_layout(seq_lengths, key_index)[0]
    query_index = lax.dynamic_slice_in_dim(key_index, block_at * group, group)
    query_seq, query_position = stream_layout(seq_lengths, query_index)
    cosine, sine_part = rope_tables(query_position, head_size)
    tables = tile_lists(query_index, query_seq, key_index, key_seq, TILE)
    marks = attend_marks(
        query_index, query_index - query_position, key_index, TILE
    )
    marks = lax.optimization_barrier(marks)

    gates, ups, downs = (
        [gather_pieces(weight[item], item) for item in range(local_experts)]
        for weight in (gate_weight, up_weight, down_weight)
    )

    normed = norm_rows(token_pieces, mixing_scale)
    normed_moved = move_columns(normed, heads_axis, blocks, part)
    key_raw, key_square = project(normed, pair_full, columns)
    value_heads = jnp.dot(normed, pair_full[:, columns:], preferred_element_type=f32)
    value_heads = value_heads.astype(bf16)
    key_squares = head_pieces(key_square)
    pairs, key_factor = rope_forward(
        key_squares, key_raw, key_scale, cosine, sine_part, value_heads, width
    )
    query_raw, query_square = project(normed, query_full, columns)
    query_squares = head_pieces(query_square)
    query_heads, query_factor = rope_forward(
        query_squares, query_raw, query_scale, cosine, sine_part, None, width
    )
    pairs_all = lax.all_gather(pairs, "blk", axis=0, tiled=True)
    attended, context, totals = attend_forward(query_heads, pairs_all, marks, tables, TILE)
    branch = jnp.dot(context, output_rows, preferred_element_type=f32).astype(bf16)
    branch = head_turn([branch[piece * rows : (piece + 1) * rows] for piece in range(heads_axis)])
    own_tokens = tokens.astype(f32)
    middle = own_tokens + add_all(branch)
    middle_factor = rms_factor(jnp.sum(middle * middle, axis=-1, keepdims=True), width)
    routed = (middle * middle_factor * routing_scale).astype(bf16)

    routed_all = lax.all_gather(xor_chunks(routed, 1), "blk", axis=0, tiled=True)
    probs = jax.nn.softmax(jnp.dot(routed, router_full, preferred_element_type=f32), axis=-1)
    probs_all = jax.nn.softmax(
        jnp.dot(routed_all, xor_chunks(router_full, 0), preferred_element_type=f32), axis=-1
    )
    weight_here = lax.dynamic_slice_in_dim(
        probs_all, block_at * local_experts, local_experts, 1
    ).reshape(blocks, rows, local_experts)
    slot_ids = jnp.arange(capacity, dtype=jnp.int32)
    codes_here = jnp.transpose(codes_here, (2, 0, 1))
    weight_here = jnp.transpose(weight_here, (2, 0, 1))
    placed = codes_here[:, :, None, :] == slot_ids[None, None, :, None]
    place = placed.astype(bf16)

    def arrange(flat, weighed=True):
        lots_here = weight_here if weighed else jnp.zeros(codes_here.shape, f32)
        if capacity % 16 == 0:
            return dispatch(codes_here, lots_here, flat, capacity)
        shaped = flat.reshape(blocks, rows, width)
        lots = jnp.sum(jnp.where(placed, lots_here[:, :, None, :], 0.0), axis=-1)
        return (
            [
                jnp.einsum("srt,std->srd", item, shaped).reshape(slots, width)
                for item in place
            ],
            [item.reshape(slots, 1) for item in lots],
        )

    arrived_cot = arrange(cot_all, False)[0]
    gate_all, up_all, down_all = (
        [jnp.concatenate(pieces, axis=0) for pieces in group_pieces]
        for group_pieces in (gates, ups, downs)
    )
    arrived, slot_weight = arrange(routed_all)
    offsets = jnp.bitwise_xor(head_at, jnp.arange(heads_axis, dtype=jnp.int32))
    results = [
        run_expert(
            offsets,
            arrived[item],
            arrived_cot[item],
            slot_weight[item],
            gate_all[item],
            up_all[item],
            down_all[item],
        )
        for item in range(local_experts)
    ]

    def back_to_rows(which):
        arrays = [result[which] for result in results]
        if capacity % 16 == 0:
            return collect(codes_here, arrays, capacity)
        return sum(
            jnp.einsum(
                "srt,srd->std",
                place[item],
                arrays[item].reshape(blocks, capacity, width),
                preferred_element_type=f32,
            )
            for item in range(local_experts)
        ).astype(bf16)

    incoming = back_to_rows(5)
    combined = back_to_rows(3)
    slot_grad = jnp.stack([result[4][0] for result in results])
    slot_grad = slot_grad.reshape(local_experts, blocks, capacity, 1)
    weight_grads = jnp.sum(jnp.where(placed, slot_grad, 0.0), axis=2)
    weight_grads = jnp.transpose(weight_grads, (1, 2, 0))
    stores = [
        (arrived[item], results[item][6], results[item][0], results[item][1], results[item][2])
        for item in range(local_experts)
    ]
    routed_grad = lax.psum_scatter(
        incoming.reshape(blocks * rows, width),
        "blk",
        scatter_dimension=0,
        tiled=True,
    )
    combined = lax.psum_scatter(
        combined.reshape(blocks * rows, width),
        "blk",
        scatter_dimension=0,
        tiled=True,
    )
    block_output = (middle + combined.astype(f32)).astype(bf16)
    prob_grad = lax.all_to_all(
        weight_grads, "blk", split_axis=0, concat_axis=2, tiled=True
    ).reshape(rows, experts)

    def pieces_of(left, right):
        size = left.shape[1] // heads_axis
        products = []
        for offset in range(heads_axis):
            product = jnp.dot(
                left[:, offset * size : (offset + 1) * size].T,
                right,
                preferred_element_type=f32,
            )
            products.append(lax.optimization_barrier(product.astype(bf16)))
        return products

    def stacked(items):
        return jnp.stack(items).astype(f32)

    down_out, gate_out, up_out = (
        stacked(
            [
                scatter_pieces(pieces_of(store[left], store[right]), item)
                for item, store in enumerate(stores)
            ]
        )
        for left, right in ((2, 1), (0, 3), (0, 4))
    )

    logit_grad = (
        probs * (prob_grad - jnp.sum(probs * prob_grad, axis=1, keepdims=True))
    ).astype(bf16)
    router_sum = jnp.dot(routed.T, logit_grad, preferred_element_type=f32)
    routed_grad = xor_chunks(routed_grad, 1).astype(f32) + jnp.dot(
        logit_grad, router_full.T, preferred_element_type=f32
    )
    scaled = routed_grad * routing_scale
    inner = jnp.mean(scaled * middle, axis=-1, keepdims=True)
    middle_grad = (
        cotangent.astype(f32) + middle_factor * scaled - middle * (middle_factor**3 * inner)
    )
    routing_sum = jnp.sum(routed_grad * middle * middle_factor, axis=0)

    branch_grad = head_pieces(middle_grad.astype(bf16))
    branch_grad = jnp.concatenate(branch_grad, axis=0)
    context_grad = jnp.dot(branch_grad, output_rows.T, preferred_element_type=f32).astype(bf16)
    output_sum = jnp.dot(context.T, branch_grad, preferred_element_type=f32).astype(bf16)
    output_out = lax.psum_scatter(output_sum, "blk", scatter_dimension=0, tiled=True)
    query_back, pairs_back = attend_backward(
        query_heads, pairs_all, context_grad, attended, totals, marks, tables, TILE
    )
    pairs_back = lax.psum_scatter(pairs_back, "blk", scatter_dimension=0, tiled=True)
    query_scaled, query_inner, querynorm_sum = rope_backward(
        query_back, query_raw, query_factor, query_scale, cosine, sine_part, 1
    )
    query_inner = head_pieces(query_inner)
    query_raw_grad = raw_backward(query_inner, query_scaled, query_raw, query_factor, None, width)
    query_sum = jnp.dot(normed_moved.T, query_raw_grad, preferred_element_type=f32).astype(bf16)
    query_sum = lax.psum_scatter(query_sum, "blk", scatter_dimension=0, tiled=True)
    normed_part = jnp.dot(query_raw_grad, query_full.T, preferred_element_type=f32)
    key_scaled, key_inner, keynorm_sum = rope_backward(
        pairs_back, key_raw, key_factor, key_scale, cosine, sine_part, 2
    )
    key_inner = head_pieces(key_inner)
    pair_grad = raw_backward(key_inner, key_scaled, key_raw, key_factor, pairs_back, width)
    pair_sum = jnp.dot(normed_moved.T, pair_grad, preferred_element_type=f32).astype(bf16)
    pair_sum = lax.psum_scatter(pair_sum, "blk", scatter_dimension=0, tiled=True)
    normed_part = normed_part + jnp.dot(pair_grad, pair_full.T, preferred_element_type=f32)
    normed_part = normed_part.astype(bf16)
    normed_part = head_turn(
        [normed_part[piece * rows : (piece + 1) * rows] for piece in range(heads_axis)]
    )
    normed_grad = add_all(normed_part)
    own_factor = rms_factor(jnp.sum(own_tokens * own_tokens, axis=-1, keepdims=True), width)
    scaled = normed_grad * mixing_scale
    inner = jnp.mean(scaled * own_tokens, axis=-1, keepdims=True)
    tokens_grad = middle_grad + own_factor * scaled - own_tokens * (own_factor**3 * inner)
    mixing_sum = jnp.sum(normed_grad * own_tokens * own_factor, axis=0)

    def turned_back(array):
        return jnp.stack(
            [
                jnp.concatenate(absolute(list(pieces)), axis=1).astype(f32)
                for pieces in zip(
                    *(
                        [piece[:, at : at + columns] for at in range(0, piece.shape[1], columns)]
                        for piece in head_turn(xor_order(array, 0))
                    )
                )
            ]
        )

    query_out = turned_back(query_sum)[0]
    pair_out = turned_back(pair_sum)

    blank = jnp.zeros((heads_axis, columns), f32)
    query_line = lax.dynamic_update_slice(blank, querynorm_sum, (head_at, 0)).reshape(width)
    key_line = lax.dynamic_update_slice(blank, keynorm_sum, (head_at, 0)).reshape(width)
    lines = jnp.concatenate(
        [
            mixing_sum[:, None],
            query_line[:, None],
            key_line[:, None],
            routing_sum[:, None],
            router_sum,
        ],
        axis=1,
    ).reshape(heads_axis, -1)
    lines = add_all(head_turn(xor_order(lines, 0)))
    lines = lax.all_to_all(lines.reshape(blocks, -1), "blk", 0, 0, tiled=True)
    lines = jnp.sum(lines, axis=0).reshape(part, 4 + experts)
    return (
        block_output,
        tokens_grad,
        query_out,
        pair_out[0],
        pair_out[1],
        output_out.astype(f32),
        lines[:, 0],
        lines[:, 1],
        lines[:, 2],
        lines[:, 3],
        lines[:, 4:],
        gate_out,
        up_out,
        down_out,
    )


def solution(mesh):
    in_specs = (
        P(("head", "blk"), None),
        P(("head", "blk"), None),
        P(("head", "blk"), None),
        P(("head", "blk"), None),
        P(("head", "blk"), None),
        P(("head", "blk")),
        P(("head", "blk")),
        P(("head", "blk")),
        P(("head", "blk")),
        P(("head", "blk"), None),
        P("blk", "head", None),
        P("blk", "head", None),
        P("blk", "head", None),
        P(),
        P(),
        P(("head", "blk"), None),
        P(("head", "blk"), None),
        P(("head", "blk"), None),
    )
    out_specs = (
        P(("head", "blk"), None),
        P(("head", "blk"), None),
        P(("head", "blk"), None),
        P(("head", "blk"), None),
        P(("head", "blk"), None),
        P(("head", "blk"), None),
        P(("head", "blk")),
        P(("head", "blk")),
        P(("head", "blk")),
        P(("head", "blk")),
        P(("head", "blk"), None),
        P("blk", "head", None),
        P("blk", "head", None),
        P("blk", "head", None),
    )
    return jax.shard_map(layer, mesh=mesh, in_specs=in_specs, out_specs=out_specs, check_vma=False)
```

```python
from functools import partial
import math

import jax
import jax.numpy as jnp
import numpy as np
from jax import lax
from jax.experimental import pallas as pl
from jax.experimental.pallas import tpu as pltpu
from jax.sharding import PartitionSpec as P


HDIM = 128
TILE = 256
LOG2E = 1.4426950408889634
norm_eps = 1e-05
rope_base = 10000.0
f32 = jnp.float32
bf16 = jnp.bfloat16


def rms_factor(square_sum, width):
    return lax.rsqrt(square_sum / width + norm_eps)


def rope_tables(position, head_size):
    half = head_size // 2
    freqs = rope_base ** (-(np.arange(half, dtype=np.float64) * 2.0) / head_size)
    angles = position.astype(f32)[:, None] * jnp.asarray(freqs.astype(np.float32))[None, :]
    cosine = jnp.cos(angles)
    sine_part = jnp.sin(angles)
    return (
        jnp.concatenate([cosine, cosine], axis=1),
        jnp.concatenate([-sine_part, sine_part], axis=1),
    )


def column_of(pieces):
    count = len(pieces)
    rows = pieces[0].shape[1] // count
    total = pieces[0][...]
    for offset in range(1, count):
        parts = [
            pieces[offset][:, (at ^ offset) * rows : ((at ^ offset) + 1) * rows]
            for at in range(count)
        ]
        total = total + jnp.concatenate(parts, axis=1)
    return jnp.transpose(jnp.broadcast_to(total, (8, total.shape[1])))[:, :1]


def turned(value, cosine, sine_part):
    return value * cosine + pltpu.roll(value, HDIM // 2, 1) * sine_part


def rope_kernel(*refs, count, width, paired):
    squares = refs[:count]
    raw, scale, cosine, sine_part = refs[count : count + 4]
    out, factors = refs[-2:]
    factor = lax.rsqrt(column_of(squares) / width + norm_eps)
    factors[...] = jnp.broadcast_to(factor, factors.shape)
    for head in range(raw.shape[1] // HDIM):
        span = slice(head * HDIM, (head + 1) * HDIM)
        value = turned(raw[:, span] * factor * scale[:, span], cosine[...], sine_part[...])
        if paired:
            start = 2 * head * HDIM
            out[:, start : start + HDIM] = value.astype(jnp.bfloat16)
            out[:, start + HDIM : start + 2 * HDIM] = refs[count + 4][:, span]
        else:
            out[:, span] = value.astype(jnp.bfloat16)


def rope_forward(squares, raw, scale, cosine, sine_part, values, width):
    group, columns = raw.shape
    paired = values is not None
    extra = (values,) if paired else ()
    return pl.pallas_call(
        partial(rope_kernel, count=len(squares), width=width, paired=paired),
        out_shape=[
            jax.ShapeDtypeStruct((group, columns * (2 if paired else 1)), jnp.bfloat16),
            jax.ShapeDtypeStruct((group, HDIM), jnp.float32),
        ],
    )(*squares, raw, scale[None], cosine, sine_part, *extra)


def unrope_kernel(back, raw, factors, scale, cosine, sine_part, scaled, inner, gain, *, stride):
    group = raw.shape[0]
    total = jnp.zeros((group, HDIM), jnp.float32)
    for head in range(raw.shape[1] // HDIM):
        span = slice(head * HDIM, (head + 1) * HDIM)
        start = stride * head * HDIM
        grad = back[:, start : start + HDIM].astype(jnp.float32)
        turn = turned(grad, cosine[...], -sine_part[...])
        product = turn * raw[:, span]
        gain[:, span] = jnp.sum(product * factors[...], axis=0, keepdims=True)
        scaled[:, span] = turn * scale[:, span]
        total = total + product * scale[:, span]
    sums = jnp.broadcast_to(jnp.sum(total, axis=1, keepdims=True), (group, HDIM))
    inner[...] = jnp.transpose(sums)[:1, :]


def rope_backward(back, raw, factors, scale, cosine, sine_part, stride):
    group, columns = raw.shape
    return pl.pallas_call(
        partial(unrope_kernel, stride=stride),
        out_shape=[
            jax.ShapeDtypeStruct((group, columns), jnp.float32),
            jax.ShapeDtypeStruct((1, group), jnp.float32),
            jax.ShapeDtypeStruct((1, columns), jnp.float32),
        ],
    )(back, raw, factors, scale[None], cosine, sine_part)


def raw_kernel(*refs, count, width, paired):
    scaled, raw, factors = refs[count : count + 3]
    out = refs[-1]
    inner = column_of(refs[:count]) / width
    factor = factors[:, :1]
    columns = raw.shape[1]
    slope = factor * factor * factor * inner
    for head in range(columns // HDIM):
        span = slice(head * HDIM, (head + 1) * HDIM)
        out[:, span] = (factor * scaled[:, span] - raw[:, span] * slope).astype(jnp.bfloat16)
        if paired:
            start = (2 * head + 1) * HDIM
            out[:, columns + head * HDIM : columns + (head + 1) * HDIM] = refs[count + 3][
                :, start : start + HDIM
            ]


def raw_backward(inner, scaled, raw, factors, pairs_back, width):
    group, columns = raw.shape
    paired = pairs_back is not None
    extra = (pairs_back,) if paired else ()
    return pl.pallas_call(
        partial(raw_kernel, count=len(inner), width=width, paired=paired),
        out_shape=jax.ShapeDtypeStruct((group, columns * (2 if paired else 1)), jnp.bfloat16),
    )(*inner, scaled, raw, factors, *extra)


def norm_kernel(*refs, count):
    scale, out = refs[count], refs[count + 1]
    rows, width = refs[0].shape
    for place in range(count):
        value = refs[place][...].astype(jnp.float32)
        square = jnp.sum(value * value, axis=1, keepdims=True)
        factor = lax.rsqrt(square / width + norm_eps)
        out[place * rows : (place + 1) * rows, :] = (value * factor * scale[...]).astype(
            jnp.bfloat16
        )


def norm_rows(pieces, scale):
    rows, width = pieces[0].shape
    return pl.pallas_call(
        partial(norm_kernel, count=len(pieces)),
        out_shape=jax.ShapeDtypeStruct((rows * len(pieces), width), jnp.bfloat16),
        name="norm_rows",
    )(*pieces, scale[None])


def project_kernel(normed, weight, raw, square, total):
    step = pl.program_id(0)

    @pl.when(step == 0)
    def start():
        total[...] = jnp.zeros_like(total)

    value = jnp.dot(normed[...], weight[...], preferred_element_type=jnp.float32)
    raw[...] = value
    for at in range(0, value.shape[1], HDIM):
        total[...] += value[:, at : at + HDIM] * value[:, at : at + HDIM]

    @pl.when(step == pl.num_programs(0) - 1)
    def finish():
        sums = jnp.sum(total[...], axis=1, keepdims=True)
        square[...] = jnp.transpose(jnp.broadcast_to(sums, total.shape))[:1, :]


def project(normed, weight, columns):
    group, width = normed.shape
    block = min(columns, 256)
    return pl.pallas_call(
        project_kernel,
        grid=(columns // block,),
        in_specs=[
            pl.BlockSpec((group, width), lambda step: (0, 0)),
            pl.BlockSpec((width, block), lambda step: (0, step)),
        ],
        out_specs=[
            pl.BlockSpec((group, block), lambda step: (0, step)),
            pl.BlockSpec((1, group), lambda step: (0, 0)),
        ],
        out_shape=[
            jax.ShapeDtypeStruct((group, columns), jnp.float32),
            jax.ShapeDtypeStruct((1, group), jnp.float32),
        ],
        scratch_shapes=[pltpu.VMEM((group, HDIM), jnp.float32)],
    )(normed, weight)


def slot_codes(routes, ordering, experts, capacity):
    expert_ids = jnp.arange(experts, dtype=jnp.int32)
    absent = jnp.int32(1 << 30)
    chosen = routes[:, :, None] == expert_ids[None, None, :]
    order = jnp.min(jnp.where(chosen, ordering[:, :, None], absent), axis=1)
    rank = jnp.sum((order[None, :, :] < order[:, None, :]).astype(jnp.int32), axis=1)
    return jnp.where((order < absent) & (rank < capacity), rank, -1)


def stream_layout(seq_lengths, stream_index):
    ends = jnp.cumsum(seq_lengths)
    starts = ends - seq_lengths
    passed = (stream_index[:, None] >= ends[None, :]).astype(jnp.int32)
    sequence = jnp.sum(passed, axis=1)
    owner = sequence[:, None] == jnp.arange(seq_lengths.shape[0], dtype=jnp.int32)[None, :]
    opening = jnp.sum(jnp.where(owner, starts[None, :], 0), axis=1)
    return (sequence, stream_index - opening)


def tile_lists(query_index, query_seq, key_index, key_seq, tile):
    query_tiles = query_index.shape[0] // tile
    key_tiles = key_index.shape[0] // tile
    query_marks = query_index.reshape(query_tiles, tile)
    query_seqs = query_seq.reshape(query_tiles, tile)
    key_marks = key_index.reshape(key_tiles, tile)
    key_seqs = key_seq.reshape(key_tiles, tile)
    early = jnp.min(key_marks, axis=1)[None, :] <= jnp.max(query_marks, axis=1)[:, None]
    above = jnp.max(key_seqs, axis=1)[None, :] >= jnp.min(query_seqs, axis=1)[:, None]
    below = jnp.min(key_seqs, axis=1)[None, :] <= jnp.max(query_seqs, axis=1)[:, None]
    live = (early & above & below).astype(jnp.int32)
    order = jnp.cumsum(live, axis=1) - 1
    numbers = jnp.arange(key_tiles, dtype=jnp.int32)
    hits = (order[:, :, None] == numbers[None, None, :]) & (live[:, :, None] > 0)
    listed = jnp.sum(jnp.where(hits, numbers[None, :, None], 0), axis=1)
    return (listed.astype(jnp.int32), jnp.sum(live, axis=1).astype(jnp.int32), live)


def spread(vector):
    return jnp.broadcast_to(vector[:, None], (vector.shape[0], 128))


def twice(value, count):
    return value if count == 1 else jnp.concatenate([value] * count, axis=1)


def forward_kernel(
    listed, counts, query, pairs, at, opening, key_at, attended, context, totals, total, acc, *, tile
):
    lanes = 128
    copies = tile // lanes
    factor = LOG2E / math.sqrt(HDIM)
    for step in range(query.shape[0] // tile):
        span = slice(step * tile, (step + 1) * tile)
        acc[...] = jnp.zeros_like(acc)
        total[...] = jnp.zeros_like(total)

        def visit(turn, carry):
            number = listed[step, turn]
            start = pl.multiple_of(number * tile, tile)
            scores = lax.dot_general(
                query[span, :],
                pairs[pl.ds(start, tile), :HDIM],
                (((1,), (1,)), ((), ())),
                preferred_element_type=jnp.float32,
            )
            marks = key_at[pl.ds(number, 1), :]
            allowed = (marks <= twice(at[span, :], copies)) & (
                marks >= twice(opening[span, :], copies)
            )
            expo = jnp.where(allowed, jnp.exp2(scores * factor), 0.0)
            partial_sum = expo[:, :lanes]
            for copy in range(1, copies):
                partial_sum = partial_sum + expo[:, copy * lanes : (copy + 1) * lanes]
            total[...] += partial_sum
            acc[...] += jnp.dot(
                expo.astype(jnp.bfloat16),
                pairs[pl.ds(start, tile), HDIM:],
                preferred_element_type=jnp.float32,
            )
            return carry

        lax.fori_loop(0, counts[step], visit, 0)
        full = jnp.sum(total[...], axis=1, keepdims=True)
        result = acc[...] / full
        attended[span, :] = result
        context[span, :] = result.astype(jnp.bfloat16)
        totals[span, :] = jnp.broadcast_to(full, (tile, lanes))


def attend_forward(queries, pairs, marks, tables, tile):
    group, columns = queries.shape
    total_rows = pairs.shape[0]
    listed, counts, _ = tables
    at, opening, key_at = marks[0], marks[1], marks[2]
    heads = columns // HDIM
    lane = lambda rows: pl.BlockSpec((rows, HDIM), lambda h, *refs: (0, h))
    wide = pl.BlockSpec((total_rows, 2 * HDIM), lambda h, *refs: (0, h))
    fixed = lambda array: pl.BlockSpec(array.shape, lambda h, *refs: (0, 0))
    return pl.pallas_call(
        partial(forward_kernel, tile=tile),
        grid_spec=pltpu.PrefetchScalarGridSpec(
            num_scalar_prefetch=2,
            grid=(heads,),
            in_specs=[
                lane(group),
                wide,
                fixed(at),
                fixed(opening),
                fixed(key_at),
            ],
            out_specs=[lane(group), lane(group), lane(group)],
            scratch_shapes=[
                pltpu.VMEM((tile, HDIM), jnp.float32),
                pltpu.VMEM((tile, HDIM), jnp.float32),
            ],
        ),
        out_shape=[
            jax.ShapeDtypeStruct((group, columns), jnp.float32),
            jax.ShapeDtypeStruct((group, columns), jnp.bfloat16),
            jax.ShapeDtypeStruct((group, columns), jnp.float32),
        ],
        name="attend_forward",
    )(listed, counts, queries, pairs, at, opening, key_at)


def backward_kernel(
    live,
    query,
    pairs,
    grad,
    attended,
    totals,
    at_row,
    opening_row,
    key_col,
    query_out,
    pairs_out,
    scaled,
    offset,
    query_acc,
    key_acc,
    value_acc,
    *,
    tile,
):
    copies = tile // 128
    steps = query.shape[0] // tile
    factor = 1.0 / math.sqrt(HDIM)
    grads = grad[...].astype(jnp.float32)
    scaled[...] = (grads / totals[...]).astype(jnp.bfloat16)
    sums = jnp.sum(grads * attended[...], axis=1, keepdims=True) / totals[...]
    offset[...] = jnp.transpose(sums)[:8, :]
    query_acc[...] = jnp.zeros_like(query_acc)

    def visit(number, carry):
        start = pl.multiple_of(number * tile, tile)
        window = pl.ds(start, tile)
        key_acc[...] = jnp.zeros_like(key_acc)
        value_acc[...] = jnp.zeros_like(value_acc)
        for step in range(steps):
            span = slice(step * tile, (step + 1) * tile)

            @pl.when(live[step, number] > 0)
            def unused():
                scores = lax.dot_general(
                    pairs[window, :HDIM],
                    query[span, :],
                    (((1,), (1,)), ((), ())),
                    preferred_element_type=jnp.float32,
                )
                marks = twice(key_col[window, :], copies)
                allowed = (marks <= at_row[:, span]) & (marks >= opening_row[:, span])
                expo = jnp.where(allowed, jnp.exp2(scores * (factor * LOG2E)), 0.0)
                inner = lax.dot_general(
                    pairs[window, HDIM:],
                    scaled[span, :],
                    (((1,), (1,)), ((), ())),
                    preferred_element_type=jnp.float32,
                )
                back = (expo * (inner - offset[0:1, span])).astype(jnp.bfloat16)
                key_acc[...] += jnp.dot(back, query[span, :], preferred_element_type=jnp.float32)
                value_acc[...] += jnp.dot(
                    expo.astype(jnp.bfloat16), scaled[span, :], preferred_element_type=jnp.float32
                )
                query_acc[span, :] += lax.dot_general(
                    back,
                    pairs[window, :HDIM],
                    (((0,), (0,)), ((), ())),
                    preferred_element_type=jnp.float32,
                )

        pairs_out[window, :HDIM] = (key_acc[...] * factor).astype(jnp.bfloat16)
        pairs_out[window, HDIM:] = value_acc[...].astype(jnp.bfloat16)
        return carry

    lax.fori_loop(0, pairs.shape[0] // tile, visit, 0)
    query_out[...] = (query_acc[...] * factor).astype(jnp.bfloat16)


def attend_backward(queries, pairs, grads, attended, totals, marks, tables, tile):
    group, columns = queries.shape
    total_rows = pairs.shape[0]
    live = tables[2]
    at_row, opening_row, key_col = marks[3], marks[4], marks[5]
    heads = columns // HDIM
    lane = lambda rows: pl.BlockSpec((rows, HDIM), lambda h, *refs: (0, h))
    wide = pl.BlockSpec((total_rows, 2 * HDIM), lambda h, *refs: (0, h))
    fixed = lambda array: pl.BlockSpec(array.shape, lambda h, *refs: (0, 0))
    return pl.pallas_call(
        partial(backward_kernel, tile=tile),
        grid_spec=pltpu.PrefetchScalarGridSpec(
            num_scalar_prefetch=1,
            grid=(heads,),
            in_specs=[
                lane(group),
                wide,
                lane(group),
                lane(group),
                lane(group),
                fixed(at_row),
                fixed(opening_row),
                fixed(key_col),
            ],
            out_specs=[lane(group), wide],
            scratch_shapes=[
                pltpu.VMEM((group, HDIM), jnp.bfloat16),
                pltpu.VMEM((8, group), jnp.float32),
                pltpu.VMEM((group, HDIM), jnp.float32),
                pltpu.VMEM((tile, HDIM), jnp.float32),
                pltpu.VMEM((tile, HDIM), jnp.float32),
            ],
        ),
        out_shape=[
            jax.ShapeDtypeStruct((group, columns), jnp.bfloat16),
            jax.ShapeDtypeStruct((total_rows, 2 * columns), jnp.bfloat16),
        ],
        name="attend_backward",
    )(live, queries, pairs, grads, attended, totals, at_row, opening_row, key_col)


def attend_marks(query_index, query_start, key_index, tile):
    return (
        spread(query_index),
        spread(query_start),
        key_index.reshape(-1, tile),
        query_index[None, :],
        query_start[None, :],
        spread(key_index),
    )


def expert_kernel(
    perm,
    arrived,
    cot,
    weight,
    gate_weight,
    up_weight,
    down_weight,
    active,
    gate_grad,
    up_grad,
    weighted,
    inner,
    incoming,
    produced_grad,
    out_acc,
    in_acc,
):
    step = pl.program_id(0)

    @pl.when(step == 0)
    def start():
        produced_grad[...] = (weight[...] * cot[...].astype(jnp.float32)).astype(jnp.bfloat16)
        out_acc[...] = jnp.zeros_like(out_acc)
        in_acc[...] = jnp.zeros_like(in_acc)

    gate = jnp.dot(arrived[...], gate_weight[...], preferred_element_type=jnp.float32)
    upward = jnp.dot(arrived[...], up_weight[...], preferred_element_type=jnp.float32)
    active_grad = lax.dot_general(
        produced_grad[...],
        down_weight[...],
        (((1,), (1,)), ((), ())),
        preferred_element_type=jnp.float32,
    )
    sigmoid = 1.0 / (1.0 + jnp.exp(-gate))
    silu = gate * sigmoid
    hidden = (silu * upward).astype(jnp.bfloat16)
    active[...] = hidden
    gate_back = (active_grad * upward * sigmoid * (1.0 + gate * (1.0 - sigmoid))).astype(
        jnp.bfloat16
    )
    up_back = (active_grad * silu).astype(jnp.bfloat16)
    gate_grad[...] = gate_back
    up_grad[...] = up_back
    out_acc[...] += jnp.dot(hidden, down_weight[...], preferred_element_type=jnp.float32)
    in_acc[...] += lax.dot_general(
        jnp.concatenate([gate_back, up_back], axis=1),
        jnp.concatenate([gate_weight[...], up_weight[...]], axis=1),
        (((1,), (1,)), ((), ())),
        preferred_element_type=jnp.float32,
    )

    @pl.when(step == pl.num_programs(0) - 1)
    def finish():
        produced = out_acc[...].astype(jnp.bfloat16).astype(jnp.float32)
        weighted[...] = (weight[...] * produced).astype(jnp.bfloat16)
        sums = jnp.sum(cot[...].astype(jnp.float32) * produced, axis=1, keepdims=True)
        inner[...] = jnp.transpose(jnp.broadcast_to(sums, (sums.shape[0], 128)))[:8, :]
        incoming[...] = in_acc[...].astype(jnp.bfloat16)


def run_expert(perm, arrived, cot, weight, gate_all, up_all, down_all):
    slots, width = arrived.shape
    hidden = gate_all.shape[1]
    steps = perm.shape[0]
    chunk = hidden // steps
    rows = pl.BlockSpec((slots, width), lambda c, perm: (0, 0))
    natural = pl.BlockSpec((slots, chunk), lambda c, perm: (0, perm[c]))
    turned_in = pl.BlockSpec((width, chunk), lambda c, perm: (0, perm[c]))
    wide = jax.ShapeDtypeStruct((slots, width), jnp.bfloat16)
    thin = jax.ShapeDtypeStruct((slots, hidden), jnp.bfloat16)
    return pl.pallas_call(
        expert_kernel,
        grid_spec=pltpu.PrefetchScalarGridSpec(
            num_scalar_prefetch=1,
            grid=(steps,),
            in_specs=[
                rows,
                rows,
                pl.BlockSpec((slots, 1), lambda c, perm: (0, 0)),
                turned_in,
                turned_in,
                pl.BlockSpec((chunk, width), lambda c, perm: (c, 0)),
            ],
            out_specs=[
                pl.BlockSpec((slots, chunk), lambda c, perm: (0, c)),
                natural,
                natural,
                rows,
                pl.BlockSpec((8, slots), lambda c, perm: (0, 0)),
                rows,
                rows,
            ],
            scratch_shapes=[
                pltpu.VMEM((slots, width), jnp.float32),
                pltpu.VMEM((slots, width), jnp.float32),
            ],
        ),
        out_shape=[
            thin,
            thin,
            thin,
            wide,
            jax.ShapeDtypeStruct((8, slots), jnp.float32),
            wide,
            wide,
        ],
        name="run_expert",
    )(perm, arrived, cot, weight, gate_all, up_all, down_all)


def dispatch_kernel(codes, chosen_weights, rows, *outs, capacity, experts):
    blocks, tokens = codes.shape[1:]
    numbers = lax.broadcasted_iota(jnp.int32, (capacity, tokens), 0)
    for block in range(blocks):
        span = slice(block * capacity, (block + 1) * capacity)
        placed = [
            (numbers == codes[item, block : block + 1, :]).astype(jnp.bfloat16)
            for item in range(experts)
        ]
        found = jnp.dot(
            jnp.concatenate(placed, axis=0),
            rows[block * tokens : (block + 1) * tokens, :],
            preferred_element_type=jnp.float32,
        ).astype(jnp.bfloat16)
        for item in range(experts):
            outs[item][span, :] = found[item * capacity : (item + 1) * capacity, :]

    @pl.when(pl.program_id(0) == 0)
    def weigh():
        for item in range(experts):
            for block in range(blocks):
                placed = numbers == codes[item, block : block + 1, :]
                span = slice(block * capacity, (block + 1) * capacity)
                row = chosen_weights[item, block : block + 1, :]
                outs[experts + item][span, :] = jnp.sum(
                    jnp.where(placed, row, 0.0), axis=1, keepdims=True
                )


def dispatch(codes, chosen_weights, rows, capacity):
    experts, blocks, _ = codes.shape
    slots = blocks * capacity
    width = rows.shape[1]
    block = min(width, 512)
    whole = pl.BlockSpec(codes.shape, lambda step: (0, 0, 0))
    results = pl.pallas_call(
        partial(dispatch_kernel, capacity=capacity, experts=experts),
        grid=(width // block,),
        in_specs=[whole, whole, pl.BlockSpec((rows.shape[0], block), lambda step: (0, step))],
        out_specs=[pl.BlockSpec((slots, block), lambda step: (0, step))] * experts
        + [pl.BlockSpec((slots, 1), lambda step: (0, 0))] * experts,
        out_shape=[jax.ShapeDtypeStruct((slots, width), jnp.bfloat16)] * experts
        + [jax.ShapeDtypeStruct((slots, 1), jnp.float32)] * experts,
    )(codes, chosen_weights, rows)
    return results[:experts], results[experts:]


def collect_kernel(codes, *refs, capacity, experts):
    out = refs[-1]
    blocks, tokens = codes.shape[1:]
    numbers = lax.broadcasted_iota(jnp.int32, (capacity, tokens), 0)
    for block in range(blocks):
        span = slice(block * capacity, (block + 1) * capacity)
        placed = [
            (numbers == codes[item, block : block + 1, :]).astype(jnp.bfloat16)
            for item in range(experts)
        ]
        total = lax.dot_general(
            jnp.concatenate(placed, axis=0),
            jnp.concatenate([refs[item][span, :] for item in range(experts)], axis=0),
            (((0,), (0,)), ((), ())),
            preferred_element_type=jnp.float32,
        )
        out[block * tokens : (block + 1) * tokens, :] = total.astype(jnp.bfloat16)


def collect(codes, arrays, capacity):
    experts, blocks, tokens = codes.shape
    slots, width = arrays[0].shape
    block = min(width, 512)
    return pl.pallas_call(
        partial(collect_kernel, capacity=capacity, experts=experts),
        grid=(width // block,),
        in_specs=[pl.BlockSpec(codes.shape, lambda step: (0, 0, 0))]
        + [pl.BlockSpec((slots, block), lambda step: (0, step))] * experts,
        out_specs=pl.BlockSpec((blocks * tokens, block), lambda step: (0, step)),
        out_shape=jax.ShapeDtypeStruct((blocks * tokens, width), jnp.bfloat16),
    )(codes, *arrays)


def exchange(array, offset):
    count = lax.axis_size("head")
    return lax.ppermute(array, "head", [(at, at ^ offset) for at in range(count)])


def head_pieces(array):
    return [array] + [exchange(array, offset) for offset in range(1, lax.axis_size("head"))]


def head_turn(pieces):
    return [pieces[0]] + [exchange(piece, at + 1) for at, piece in enumerate(pieces[1:])]


def add_all(pieces):
    total = pieces[0].astype(f32)
    for piece in pieces[1:]:
        total = total + piece.astype(f32)
    return total


def bit_order(turn):
    count = lax.axis_size("head").bit_length() - 1
    return [1 << ((turn + step) % count) for step in range(count)]


def gather_pieces(array, turn):
    pieces = {0: array}
    for bit in bit_order(turn):
        for offset in list(pieces):
            pieces[offset ^ bit] = exchange(pieces[offset], bit)
    return [pieces[offset] for offset in range(len(pieces))]


def scatter_pieces(pieces, turn):
    held = dict(enumerate(pieces))
    for bit in bit_order(turn):
        for offset in [item for item in held if item & bit]:
            piece = held.pop(offset).astype(bf16)
            arrived = exchange(piece, bit)
            held[offset ^ bit] = held[offset ^ bit].astype(f32) + arrived.astype(f32)
    return held[0]


def xor_order(array, axis):
    count = lax.axis_size("head")
    at = lax.axis_index("head")
    size = array.shape[axis] // count
    chunks = [
        lax.dynamic_slice_in_dim(array, (at ^ offset) * size, size, axis) for offset in range(count)
    ]
    return chunks


def xor_chunks(array, axis):
    return jnp.concatenate(xor_order(array, axis), axis=axis)


def absolute(pieces):
    at = lax.axis_index("head")
    result = []
    for place in range(len(pieces)):
        value = pieces[0]
        for offset in range(1, len(pieces)):
            value = jnp.where(at == place ^ offset, pieces[offset], value)
        result.append(value)
    return result


def move_rows(array, outer, inner, part):
    shaped = array.reshape(outer, inner, part, array.shape[1])
    return jnp.transpose(shaped, (1, 0, 2, 3)).reshape(array.shape)


def move_columns(array, outer, inner, part):
    shaped = array.reshape(array.shape[0], outer, inner, part)
    return jnp.transpose(shaped, (0, 2, 1, 3)).reshape(array.shape)


def layer(
    tokens,
    query_weight,
    key_weight,
    value_weight,
    output_weight,
    mixing_gain,
    query_gain,
    key_gain,
    routing_gain,
    router_weight,
    gate_weight,
    up_weight,
    down_weight,
    seq_lengths,
    dealt_order,
    expert_routes,
    slot_order,
    cotangent,
):
    heads_axis = lax.axis_size("head")
    blocks = lax.axis_size("blk")
    head_at = lax.axis_index("head")
    block_at = lax.axis_index("blk")
    rows, width = tokens.shape
    picks = expert_routes.shape[1]
    total_rows = dealt_order.shape[0]
    group = rows * heads_axis
    columns = width // heads_axis
    part = query_weight.shape[0]
    head_size = HDIM
    experts = router_weight.shape[1]
    local_experts = gate_weight.shape[0]
    capacity = 5 * rows * picks // (4 * experts)
    slots = blocks * capacity

    slices = [
        jnp.concatenate(chunks, axis=1)
        for chunks in zip(
            xor_order(key_weight, 1), xor_order(value_weight, 1), xor_order(query_weight, 1)
        )
    ]
    slices = head_turn(slices)
    token_pieces = head_pieces(tokens)
    rows_here = jnp.stack(absolute(slices)).reshape(heads_axis * part, 3 * columns)
    pair_full = lax.all_gather(rows_here[:, : 2 * columns], "blk", axis=0, tiled=True)
    pair_full = move_rows(pair_full, blocks, heads_axis, part)
    query_output = jnp.concatenate(
        [rows_here[:, 2 * columns :], output_weight.reshape(heads_axis * part, columns)], axis=0
    )
    query_output = lax.all_gather(query_output, "blk", axis=0, tiled=False)
    query_full = move_rows(
        query_output[:, : heads_axis * part].reshape(width, columns), blocks, heads_axis, part
    )
    output_rows = query_output[:, heads_axis * part :].reshape(columns, width)
    cot_all = lax.all_gather(cotangent, "blk", axis=0, tiled=True)

    small = jnp.concatenate(
        [
            mixing_gain[:, None],
            query_gain[:, None],
            key_gain[:, None],
            routing_gain[:, None],
            router_weight,
        ],
        axis=1,
    ).reshape(1, -1)
    codes = slot_codes(expert_routes, slot_order, experts, capacity).astype(bf16)
    sizes = small.shape[1]
    small = lax.all_gather(
        jnp.concatenate([small, codes.reshape(1, -1)], axis=1), "blk", axis=0, tiled=True
    )
    codes = small[:, sizes:].reshape(blocks, rows, experts).astype(jnp.int32)
    small = small[:, :sizes]
    small = jnp.stack(absolute(head_pieces(small))).reshape(width, 4 + experts)
    mixing_scale = small[:, 0].astype(f32)
    routing_scale = small[:, 3].astype(f32)
    query_scale = lax.dynamic_slice_in_dim(small[:, 1], head_at * columns, columns).astype(f32)
    key_scale = lax.dynamic_slice_in_dim(small[:, 2], head_at * columns, columns).astype(f32)
    router_full = small[:, 4:]
    codes_here = lax.dynamic_slice_in_dim(codes, block_at * local_experts, local_experts, 2)

    key_index = jnp.transpose(
        xor_chunks(dealt_order.reshape(heads_axis, blocks, rows), 0), (1, 0, 2)
    ).reshape(total_rows)
    key_seq = stream_layout(seq_lengths, key_index)[0]
    query_index = lax.dynamic_slice_in_dim(key_index, block_at * group, group)
    query_seq, query_position = stream_layout(seq_lengths, query_index)
    cosine, sine_part = rope_tables(query_position, head_size)
    tables = tile_lists(query_index, query_seq, key_index, key_seq, TILE)
    marks = attend_marks(
        query_index, query_index - query_position, key_index, TILE
    )
    marks = lax.optimization_barrier(marks)

    gates, ups, downs = (
        [gather_pieces(weight[item], item) for item in range(local_experts)]
        for weight in (gate_weight, up_weight, down_weight)
    )

    normed = norm_rows(token_pieces, mixing_scale)
    normed_moved = move_columns(normed, heads_axis, blocks, part)
    key_raw, key_square = project(normed, pair_full, columns)
    value_heads = jnp.dot(normed, pair_full[:, columns:], preferred_element_type=f32)
    value_heads = value_heads.astype(bf16)
    key_squares = head_pieces(key_square)
    pairs, key_factor = rope_forward(
        key_squares, key_raw, key_scale, cosine, sine_part, value_heads, width
    )
    query_raw, query_square = project(normed, query_full, columns)
    query_squares = head_pieces(query_square)
    query_heads, query_factor = rope_forward(
        query_squares, query_raw, query_scale, cosine, sine_part, None, width
    )
    pairs_all = lax.all_gather(pairs, "blk", axis=0, tiled=True)
    attended, context, totals = attend_forward(query_heads, pairs_all, marks, tables, TILE)
    branch = jnp.dot(context, output_rows, preferred_element_type=f32).astype(bf16)
    branch = head_turn([branch[piece * rows : (piece + 1) * rows] for piece in range(heads_axis)])
    own_tokens = tokens.astype(f32)
    middle = own_tokens + add_all(branch)
    middle_factor = rms_factor(jnp.sum(middle * middle, axis=-1, keepdims=True), width)
    routed = (middle * middle_factor * routing_scale).astype(bf16)

    routed_all = lax.all_gather(xor_chunks(routed, 1), "blk", axis=0, tiled=True)
    probs = jax.nn.softmax(jnp.dot(routed, router_full, preferred_element_type=f32), axis=-1)
    probs_all = jax.nn.softmax(
        jnp.dot(routed_all, xor_chunks(router_full, 0), preferred_element_type=f32), axis=-1
    )
    weight_here = lax.dynamic_slice_in_dim(
        probs_all, block_at * local_experts, local_experts, 1
    ).reshape(blocks, rows, local_experts)
    slot_ids = jnp.arange(capacity, dtype=jnp.int32)
    codes_here = jnp.transpose(codes_here, (2, 0, 1))
    weight_here = jnp.transpose(weight_here, (2, 0, 1))
    placed = codes_here[:, :, None, :] == slot_ids[None, None, :, None]
    place = placed.astype(bf16)

    def arrange(flat, weighed=True):
        lots_here = weight_here if weighed else jnp.zeros(codes_here.shape, f32)
        if capacity % 16 == 0:
            return dispatch(codes_here, lots_here, flat, capacity)
        shaped = flat.reshape(blocks, rows, width)
        lots = jnp.sum(jnp.where(placed, lots_here[:, :, None, :], 0.0), axis=-1)
        return (
            [
                jnp.einsum("srt,std->srd", item, shaped).reshape(slots, width)
                for item in place
            ],
            [item.reshape(slots, 1) for item in lots],
        )

    arrived_cot = arrange(cot_all, False)[0]
    gate_all, up_all, down_all = (
        [jnp.concatenate(pieces, axis=0) for pieces in group_pieces]
        for group_pieces in (gates, ups, downs)
    )
    arrived, slot_weight = arrange(routed_all)
    offsets = jnp.bitwise_xor(head_at, jnp.arange(heads_axis, dtype=jnp.int32))
    results = [
        run_expert(
            offsets,
            arrived[item],
            arrived_cot[item],
            slot_weight[item],
            gate_all[item],
            up_all[item],
            down_all[item],
        )
        for item in range(local_experts)
    ]

    def back_to_rows(which):
        arrays = [result[which] for result in results]
        if capacity % 16 == 0:
            return collect(codes_here, arrays, capacity)
        return sum(
            jnp.einsum(
                "srt,srd->std",
                place[item],
                arrays[item].reshape(blocks, capacity, width),
                preferred_element_type=f32,
            )
            for item in range(local_experts)
        ).astype(bf16)

    incoming = back_to_rows(5)
    combined = back_to_rows(3)
    slot_grad = jnp.stack([result[4][0] for result in results])
    slot_grad = slot_grad.reshape(local_experts, blocks, capacity, 1)
    weight_grads = jnp.sum(jnp.where(placed, slot_grad, 0.0), axis=2)
    weight_grads = jnp.transpose(weight_grads, (1, 2, 0))
    stores = [
        (arrived[item], results[item][6], results[item][0], results[item][1], results[item][2])
        for item in range(local_experts)
    ]
    routed_grad = lax.psum_scatter(
        incoming.reshape(blocks * rows, width),
        "blk",
        scatter_dimension=0,
        tiled=True,
    )
    combined = lax.psum_scatter(
        combined.reshape(blocks * rows, width),
        "blk",
        scatter_dimension=0,
        tiled=True,
    )
    block_output = (middle + combined.astype(f32)).astype(bf16)
    prob_grad = lax.all_to_all(
        weight_grads, "blk", split_axis=0, concat_axis=2, tiled=True
    ).reshape(rows, experts)

    def pieces_of(left, right):
        size = left.shape[1] // heads_axis
        products = []
        for offset in range(heads_axis):
            product = jnp.dot(
                left[:, offset * size : (offset + 1) * size].T,
                right,
                preferred_element_type=f32,
            )
            products.append(lax.optimization_barrier(product.astype(bf16)))
        return products

    def stacked(items):
        return jnp.stack(items).astype(f32)

    down_out, gate_out, up_out = (
        stacked(
            [
                scatter_pieces(pieces_of(store[left], store[right]), item)
                for item, store in enumerate(stores)
            ]
        )
        for left, right in ((2, 1), (0, 3), (0, 4))
    )

    logit_grad = (
        probs * (prob_grad - jnp.sum(probs * prob_grad, axis=1, keepdims=True))
    ).astype(bf16)
    router_sum = jnp.dot(routed.T, logit_grad, preferred_element_type=f32)
    routed_grad = xor_chunks(routed_grad, 1).astype(f32) + jnp.dot(
        logit_grad, router_full.T, preferred_element_type=f32
    )
    scaled = routed_grad * routing_scale
    inner = jnp.mean(scaled * middle, axis=-1, keepdims=True)
    middle_grad = (
        cotangent.astype(f32) + middle_factor * scaled - middle * (middle_factor**3 * inner)
    )
    routing_sum = jnp.sum(routed_grad * middle * middle_factor, axis=0)

    branch_grad = head_pieces(middle_grad.astype(bf16))
    branch_grad = jnp.concatenate(branch_grad, axis=0)
    context_grad = jnp.dot(branch_grad, output_rows.T, preferred_element_type=f32).astype(bf16)
    output_sum = jnp.dot(context.T, branch_grad, preferred_element_type=f32).astype(bf16)
    output_out = lax.psum_scatter(output_sum, "blk", scatter_dimension=0, tiled=True)
    query_back, pairs_back = attend_backward(
        query_heads, pairs_all, context_grad, attended, totals, marks, tables, TILE
    )
    pairs_back = lax.psum_scatter(pairs_back, "blk", scatter_dimension=0, tiled=True)
    query_scaled, query_inner, querynorm_sum = rope_backward(
        query_back, query_raw, query_factor, query_scale, cosine, sine_part, 1
    )
    query_inner = head_pieces(query_inner)
    query_raw_grad = raw_backward(query_inner, query_scaled, query_raw, query_factor, None, width)
    query_sum = jnp.dot(normed_moved.T, query_raw_grad, preferred_element_type=f32).astype(bf16)
    query_sum = lax.psum_scatter(query_sum, "blk", scatter_dimension=0, tiled=True)
    normed_part = jnp.dot(query_raw_grad, query_full.T, preferred_element_type=f32)
    key_scaled, key_inner, keynorm_sum = rope_backward(
        pairs_back, key_raw, key_factor, key_scale, cosine, sine_part, 2
    )
    key_inner = head_pieces(key_inner)
    pair_grad = raw_backward(key_inner, key_scaled, key_raw, key_factor, pairs_back, width)
    pair_sum = jnp.dot(normed_moved.T, pair_grad, preferred_element_type=f32).astype(bf16)
    pair_sum = lax.psum_scatter(pair_sum, "blk", scatter_dimension=0, tiled=True)
    normed_part = normed_part + jnp.dot(pair_grad, pair_full.T, preferred_element_type=f32)
    normed_part = normed_part.astype(bf16)
    normed_part = head_turn(
        [normed_part[piece * rows : (piece + 1) * rows] for piece in range(heads_axis)]
    )
    normed_grad = add_all(normed_part)
    own_factor = rms_factor(jnp.sum(own_tokens * own_tokens, axis=-1, keepdims=True), width)
    scaled = normed_grad * mixing_scale
    inner = jnp.mean(scaled * own_tokens, axis=-1, keepdims=True)
    tokens_grad = middle_grad + own_factor * scaled - own_tokens * (own_factor**3 * inner)
    mixing_sum = jnp.sum(normed_grad * own_tokens * own_factor, axis=0)

    def turned_back(array):
        return jnp.stack(
            [
                jnp.concatenate(absolute(list(pieces)), axis=1).astype(f32)
                for pieces in zip(
                    *(
                        [piece[:, at : at + columns] for at in range(0, piece.shape[1], columns)]
                        for piece in head_turn(xor_order(array, 0))
                    )
                )
            ]
        )

    query_out = turned_back(query_sum)[0]
    pair_out = turned_back(pair_sum)

    blank = jnp.zeros((heads_axis, columns), f32)
    query_line = lax.dynamic_update_slice(blank, querynorm_sum, (head_at, 0)).reshape(width)
    key_line = lax.dynamic_update_slice(blank, keynorm_sum, (head_at, 0)).reshape(width)
    lines = jnp.concatenate(
        [
            mixing_sum[:, None],
            query_line[:, None],
            key_line[:, None],
            routing_sum[:, None],
            router_sum,
        ],
        axis=1,
    ).reshape(heads_axis, -1)
    lines = add_all(head_turn(xor_order(lines, 0)))
    lines = lax.all_to_all(lines.reshape(blocks, -1), "blk", 0, 0, tiled=True)
    lines = jnp.sum(lines, axis=0).reshape(part, 4 + experts)
    return (
        block_output,
        tokens_grad,
        query_out,
        pair_out[0],
        pair_out[1],
        output_out.astype(f32),
        lines[:, 0],
        lines[:, 1],
        lines[:, 2],
        lines[:, 3],
        lines[:, 4:],
        gate_out,
        up_out,
        down_out,
    )


def solution(mesh):
    in_specs = (
        P(("head", "blk"), None),
        P(("head", "blk"), None),
        P(("head", "blk"), None),
        P(("head", "blk"), None),
        P(("head", "blk"), None),
        P(("head", "blk")),
        P(("head", "blk")),
        P(("head", "blk")),
        P(("head", "blk")),
        P(("head", "blk"), None),
        P("blk", "head", None),
        P("blk", "head", None),
        P("blk", "head", None),
        P(),
        P(),
        P(("head", "blk"), None),
        P(("head", "blk"), None),
        P(("head", "blk"), None),
    )
    out_specs = (
        P(("head", "blk"), None),
        P(("head", "blk"), None),
        P(("head", "blk"), None),
        P(("head", "blk"), None),
        P(("head", "blk"), None),
        P(("head", "blk"), None),
        P(("head", "blk")),
        P(("head", "blk")),
        P(("head", "blk")),
        P(("head", "blk")),
        P(("head", "blk"), None),
        P("blk", "head", None),
        P("blk", "head", None),
        P("blk", "head", None),
    )
    return jax.shard_map(layer, mesh=mesh, in_specs=in_specs, out_specs=out_specs, check_vma=False)
```

```python
from functools import partial
import math

import jax
import jax.numpy as jnp
import numpy as np
from jax import lax
from jax.experimental import pallas as pl
from jax.experimental.pallas import tpu as pltpu
from jax.sharding import PartitionSpec as P


HDIM = 128
TILE = 256
LOG2E = 1.4426950408889634
norm_eps = 1e-05
rope_base = 10000.0
f32 = jnp.float32
bf16 = jnp.bfloat16


def rms_factor(square_sum, width):
    return lax.rsqrt(square_sum / width + norm_eps)


def rope_tables(position, head_size):
    half = head_size // 2
    freqs = rope_base ** (-(np.arange(half, dtype=np.float64) * 2.0) / head_size)
    angles = position.astype(f32)[:, None] * jnp.asarray(freqs.astype(np.float32))[None, :]
    cosine = jnp.cos(angles)
    sine_part = jnp.sin(angles)
    return (
        jnp.concatenate([cosine, cosine], axis=1),
        jnp.concatenate([-sine_part, sine_part], axis=1),
    )


def column_of(pieces):
    count = len(pieces)
    rows = pieces[0].shape[1] // count
    total = pieces[0][...]
    for offset in range(1, count):
        parts = [
            pieces[offset][:, (at ^ offset) * rows : ((at ^ offset) + 1) * rows]
            for at in range(count)
        ]
        total = total + jnp.concatenate(parts, axis=1)
    return jnp.transpose(jnp.broadcast_to(total, (8, total.shape[1])))[:, :1]


def turned(value, cosine, sine_part):
    return value * cosine + pltpu.roll(value, HDIM // 2, 1) * sine_part


def rope_kernel(*refs, count, width, paired):
    squares = refs[:count]
    raw, scale, cosine, sine_part = refs[count : count + 4]
    out, factors = refs[-2:]
    factor = lax.rsqrt(column_of(squares) / width + norm_eps)
    factors[...] = jnp.broadcast_to(factor, factors.shape)
    for head in range(raw.shape[1] // HDIM):
        span = slice(head * HDIM, (head + 1) * HDIM)
        value = turned(raw[:, span] * factor * scale[:, span], cosine[...], sine_part[...])
        if paired:
            start = 2 * head * HDIM
            out[:, start : start + HDIM] = value.astype(jnp.bfloat16)
            out[:, start + HDIM : start + 2 * HDIM] = refs[count + 4][:, span]
        else:
            out[:, span] = value.astype(jnp.bfloat16)


def rope_forward(squares, raw, scale, cosine, sine_part, values, width):
    group, columns = raw.shape
    paired = values is not None
    extra = (values,) if paired else ()
    return pl.pallas_call(
        partial(rope_kernel, count=len(squares), width=width, paired=paired),
        out_shape=[
            jax.ShapeDtypeStruct((group, columns * (2 if paired else 1)), jnp.bfloat16),
            jax.ShapeDtypeStruct((group, HDIM), jnp.float32),
        ],
    )(*squares, raw, scale[None], cosine, sine_part, *extra)


def unrope_kernel(back, raw, factors, scale, cosine, sine_part, scaled, inner, gain, *, stride):
    group = raw.shape[0]
    total = jnp.zeros((group, HDIM), jnp.float32)
    for head in range(raw.shape[1] // HDIM):
        span = slice(head * HDIM, (head + 1) * HDIM)
        start = stride * head * HDIM
        grad = back[:, start : start + HDIM].astype(jnp.float32)
        turn = turned(grad, cosine[...], -sine_part[...])
        product = turn * raw[:, span]
        gain[:, span] = jnp.sum(product * factors[...], axis=0, keepdims=True)
        scaled[:, span] = turn * scale[:, span]
        total = total + product * scale[:, span]
    sums = jnp.broadcast_to(jnp.sum(total, axis=1, keepdims=True), (group, HDIM))
    inner[...] = jnp.transpose(sums)[:1, :]


def rope_backward(back, raw, factors, scale, cosine, sine_part, stride):
    group, columns = raw.shape
    return pl.pallas_call(
        partial(unrope_kernel, stride=stride),
        out_shape=[
            jax.ShapeDtypeStruct((group, columns), jnp.float32),
            jax.ShapeDtypeStruct((1, group), jnp.float32),
            jax.ShapeDtypeStruct((1, columns), jnp.float32),
        ],
    )(back, raw, factors, scale[None], cosine, sine_part)


def raw_kernel(*refs, count, width, paired):
    scaled, raw, factors = refs[count : count + 3]
    out = refs[-1]
    inner = column_of(refs[:count]) / width
    factor = factors[:, :1]
    columns = raw.shape[1]
    slope = factor * factor * factor * inner
    for head in range(columns // HDIM):
        span = slice(head * HDIM, (head + 1) * HDIM)
        out[:, span] = (factor * scaled[:, span] - raw[:, span] * slope).astype(jnp.bfloat16)
        if paired:
            start = (2 * head + 1) * HDIM
            out[:, columns + head * HDIM : columns + (head + 1) * HDIM] = refs[count + 3][
                :, start : start + HDIM
            ]


def raw_backward(inner, scaled, raw, factors, pairs_back, width):
    group, columns = raw.shape
    paired = pairs_back is not None
    extra = (pairs_back,) if paired else ()
    return pl.pallas_call(
        partial(raw_kernel, count=len(inner), width=width, paired=paired),
        out_shape=jax.ShapeDtypeStruct((group, columns * (2 if paired else 1)), jnp.bfloat16),
    )(*inner, scaled, raw, factors, *extra)


def norm_kernel(*refs, count):
    scale, out = refs[count], refs[count + 1]
    rows, width = refs[0].shape
    for place in range(count):
        value = refs[place][...].astype(jnp.float32)
        square = jnp.sum(value * value, axis=1, keepdims=True)
        factor = lax.rsqrt(square / width + norm_eps)
        out[place * rows : (place + 1) * rows, :] = (value * factor * scale[...]).astype(
            jnp.bfloat16
        )


def norm_rows(pieces, scale):
    rows, width = pieces[0].shape
    return pl.pallas_call(
        partial(norm_kernel, count=len(pieces)),
        out_shape=jax.ShapeDtypeStruct((rows * len(pieces), width), jnp.bfloat16),
        name="norm_rows",
    )(*pieces, scale[None])


def project_kernel(normed, weight, raw, square, total):
    step = pl.program_id(0)

    @pl.when(step == 0)
    def start():
        total[...] = jnp.zeros_like(total)

    value = jnp.dot(normed[...], weight[...], preferred_element_type=jnp.float32)
    raw[...] = value
    for at in range(0, value.shape[1], HDIM):
        total[...] += value[:, at : at + HDIM] * value[:, at : at + HDIM]

    @pl.when(step == pl.num_programs(0) - 1)
    def finish():
        sums = jnp.sum(total[...], axis=1, keepdims=True)
        square[...] = jnp.transpose(jnp.broadcast_to(sums, total.shape))[:1, :]


def project(normed, weight, columns):
    group, width = normed.shape
    block = min(columns, 256)
    return pl.pallas_call(
        project_kernel,
        grid=(columns // block,),
        in_specs=[
            pl.BlockSpec((group, width), lambda step: (0, 0)),
            pl.BlockSpec((width, block), lambda step: (0, step)),
        ],
        out_specs=[
            pl.BlockSpec((group, block), lambda step: (0, step)),
            pl.BlockSpec((1, group), lambda step: (0, 0)),
        ],
        out_shape=[
            jax.ShapeDtypeStruct((group, columns), jnp.float32),
            jax.ShapeDtypeStruct((1, group), jnp.float32),
        ],
        scratch_shapes=[pltpu.VMEM((group, HDIM), jnp.float32)],
    )(normed, weight)


def slot_codes(routes, ordering, experts, capacity):
    expert_ids = jnp.arange(experts, dtype=jnp.int32)
    absent = jnp.int32(1 << 30)
    chosen = routes[:, :, None] == expert_ids[None, None, :]
    order = jnp.min(jnp.where(chosen, ordering[:, :, None], absent), axis=1)
    rank = jnp.sum((order[None, :, :] < order[:, None, :]).astype(jnp.int32), axis=1)
    return jnp.where((order < absent) & (rank < capacity), rank, -1)


def stream_layout(seq_lengths, stream_index):
    ends = jnp.cumsum(seq_lengths)
    starts = ends - seq_lengths
    passed = (stream_index[:, None] >= ends[None, :]).astype(jnp.int32)
    sequence = jnp.sum(passed, axis=1)
    owner = sequence[:, None] == jnp.arange(seq_lengths.shape[0], dtype=jnp.int32)[None, :]
    opening = jnp.sum(jnp.where(owner, starts[None, :], 0), axis=1)
    return (sequence, stream_index - opening)


def tile_lists(query_index, query_seq, key_index, key_seq, tile):
    query_tiles = query_index.shape[0] // tile
    key_tiles = key_index.shape[0] // tile
    query_marks = query_index.reshape(query_tiles, tile)
    query_seqs = query_seq.reshape(query_tiles, tile)
    key_marks = key_index.reshape(key_tiles, tile)
    key_seqs = key_seq.reshape(key_tiles, tile)
    early = jnp.min(key_marks, axis=1)[None, :] <= jnp.max(query_marks, axis=1)[:, None]
    above = jnp.max(key_seqs, axis=1)[None, :] >= jnp.min(query_seqs, axis=1)[:, None]
    below = jnp.min(key_seqs, axis=1)[None, :] <= jnp.max(query_seqs, axis=1)[:, None]
    live = (early & above & below).astype(jnp.int32)
    order = jnp.cumsum(live, axis=1) - 1
    numbers = jnp.arange(key_tiles, dtype=jnp.int32)
    hits = (order[:, :, None] == numbers[None, None, :]) & (live[:, :, None] > 0)
    listed = jnp.sum(jnp.where(hits, numbers[None, :, None], 0), axis=1)
    return (listed.astype(jnp.int32), jnp.sum(live, axis=1).astype(jnp.int32), live)


def spread(vector):
    return jnp.broadcast_to(vector[:, None], (vector.shape[0], 128))


def twice(value, count):
    return value if count == 1 else jnp.concatenate([value] * count, axis=1)


def forward_kernel(
    listed, counts, query, pairs, at, opening, key_at, attended, context, totals, total, acc, *, tile
):
    lanes = 128
    copies = tile // lanes
    factor = LOG2E / math.sqrt(HDIM)
    for step in range(query.shape[0] // tile):
        span = slice(step * tile, (step + 1) * tile)
        acc[...] = jnp.zeros_like(acc)
        total[...] = jnp.zeros_like(total)

        def visit(turn, carry):
            number = listed[step, turn]
            start = pl.multiple_of(number * tile, tile)
            scores = lax.dot_general(
                query[span, :],
                pairs[pl.ds(start, tile), :HDIM],
                (((1,), (1,)), ((), ())),
                preferred_element_type=jnp.float32,
            )
            marks = key_at[pl.ds(number, 1), :]
            allowed = (marks <= twice(at[span, :], copies)) & (
                marks >= twice(opening[span, :], copies)
            )
            expo = jnp.where(allowed, jnp.exp2(scores * factor), 0.0)
            partial_sum = expo[:, :lanes]
            for copy in range(1, copies):
                partial_sum = partial_sum + expo[:, copy * lanes : (copy + 1) * lanes]
            total[...] += partial_sum
            acc[...] += jnp.dot(
                expo.astype(jnp.bfloat16),
                pairs[pl.ds(start, tile), HDIM:],
                preferred_element_type=jnp.float32,
            )
            return carry

        lax.fori_loop(0, counts[step], visit, 0)
        full = jnp.sum(total[...], axis=1, keepdims=True)
        result = acc[...] / full
        attended[span, :] = result
        context[span, :] = result.astype(jnp.bfloat16)
        totals[span, :] = jnp.broadcast_to(full, (tile, lanes))


def attend_forward(queries, pairs, marks, tables, tile):
    group, columns = queries.shape
    total_rows = pairs.shape[0]
    listed, counts, _ = tables
    at, opening, key_at = marks[0], marks[1], marks[2]
    heads = columns // HDIM
    lane = lambda rows: pl.BlockSpec((rows, HDIM), lambda h, *refs: (0, h))
    wide = pl.BlockSpec((total_rows, 2 * HDIM), lambda h, *refs: (0, h))
    fixed = lambda array: pl.BlockSpec(array.shape, lambda h, *refs: (0, 0))
    return pl.pallas_call(
        partial(forward_kernel, tile=tile),
        grid_spec=pltpu.PrefetchScalarGridSpec(
            num_scalar_prefetch=2,
            grid=(heads,),
            in_specs=[
                lane(group),
                wide,
                fixed(at),
                fixed(opening),
                fixed(key_at),
            ],
            out_specs=[lane(group), lane(group), lane(group)],
            scratch_shapes=[
                pltpu.VMEM((tile, HDIM), jnp.float32),
                pltpu.VMEM((tile, HDIM), jnp.float32),
            ],
        ),
        out_shape=[
            jax.ShapeDtypeStruct((group, columns), jnp.float32),
            jax.ShapeDtypeStruct((group, columns), jnp.bfloat16),
            jax.ShapeDtypeStruct((group, columns), jnp.float32),
        ],
        name="attend_forward",
    )(listed, counts, queries, pairs, at, opening, key_at)


def backward_kernel(
    live,
    query,
    pairs,
    grad,
    attended,
    totals,
    at_row,
    opening_row,
    key_col,
    query_out,
    pairs_out,
    scaled,
    offset,
    query_acc,
    key_acc,
    value_acc,
    *,
    tile,
):
    copies = tile // 128
    steps = query.shape[0] // tile
    factor = 1.0 / math.sqrt(HDIM)
    grads = grad[...].astype(jnp.float32)
    scaled[...] = (grads / totals[...]).astype(jnp.bfloat16)
    sums = jnp.sum(grads * attended[...], axis=1, keepdims=True) / totals[...]
    offset[...] = jnp.transpose(sums)[:8, :]
    query_acc[...] = jnp.zeros_like(query_acc)

    def visit(number, carry):
        start = pl.multiple_of(number * tile, tile)
        window = pl.ds(start, tile)
        key_acc[...] = jnp.zeros_like(key_acc)
        value_acc[...] = jnp.zeros_like(value_acc)
        for step in range(steps):
            span = slice(step * tile, (step + 1) * tile)

            @pl.when(live[step, number] > 0)
            def unused():
                scores = lax.dot_general(
                    pairs[window, :HDIM],
                    query[span, :],
                    (((1,), (1,)), ((), ())),
                    preferred_element_type=jnp.float32,
                )
                marks = twice(key_col[window, :], copies)
                allowed = (marks <= at_row[:, span]) & (marks >= opening_row[:, span])
                expo = jnp.where(allowed, jnp.exp2(scores * (factor * LOG2E)), 0.0)
                inner = lax.dot_general(
                    pairs[window, HDIM:],
                    scaled[span, :],
                    (((1,), (1,)), ((), ())),
                    preferred_element_type=jnp.float32,
                )
                back = (expo * (inner - offset[0:1, span])).astype(jnp.bfloat16)
                key_acc[...] += jnp.dot(back, query[span, :], preferred_element_type=jnp.float32)
                value_acc[...] += jnp.dot(
                    expo.astype(jnp.bfloat16), scaled[span, :], preferred_element_type=jnp.float32
                )
                query_acc[span, :] += lax.dot_general(
                    back,
                    pairs[window, :HDIM],
                    (((0,), (0,)), ((), ())),
                    preferred_element_type=jnp.float32,
                )

        pairs_out[window, :HDIM] = (key_acc[...] * factor).astype(jnp.bfloat16)
        pairs_out[window, HDIM:] = value_acc[...].astype(jnp.bfloat16)
        return carry

    lax.fori_loop(0, pairs.shape[0] // tile, visit, 0)
    query_out[...] = (query_acc[...] * factor).astype(jnp.bfloat16)


def attend_backward(queries, pairs, grads, attended, totals, marks, tables, tile):
    group, columns = queries.shape
    total_rows = pairs.shape[0]
    live = tables[2]
    at_row, opening_row, key_col = marks[3], marks[4], marks[5]
    heads = columns // HDIM
    lane = lambda rows: pl.BlockSpec((rows, HDIM), lambda h, *refs: (0, h))
    wide = pl.BlockSpec((total_rows, 2 * HDIM), lambda h, *refs: (0, h))
    fixed = lambda array: pl.BlockSpec(array.shape, lambda h, *refs: (0, 0))
    return pl.pallas_call(
        partial(backward_kernel, tile=tile),
        grid_spec=pltpu.PrefetchScalarGridSpec(
            num_scalar_prefetch=1,
            grid=(heads,),
            in_specs=[
                lane(group),
                wide,
                lane(group),
                lane(group),
                lane(group),
                fixed(at_row),
                fixed(opening_row),
                fixed(key_col),
            ],
            out_specs=[lane(group), wide],
            scratch_shapes=[
                pltpu.VMEM((group, HDIM), jnp.bfloat16),
                pltpu.VMEM((8, group), jnp.float32),
                pltpu.VMEM((group, HDIM), jnp.float32),
                pltpu.VMEM((tile, HDIM), jnp.float32),
                pltpu.VMEM((tile, HDIM), jnp.float32),
            ],
        ),
        out_shape=[
            jax.ShapeDtypeStruct((group, columns), jnp.bfloat16),
            jax.ShapeDtypeStruct((total_rows, 2 * columns), jnp.bfloat16),
        ],
        name="attend_backward",
    )(live, queries, pairs, grads, attended, totals, at_row, opening_row, key_col)


def attend_marks(query_index, query_start, key_index, tile):
    return (
        spread(query_index),
        spread(query_start),
        key_index.reshape(-1, tile),
        query_index[None, :],
        query_start[None, :],
        spread(key_index),
    )


def expert_kernel(
    perm,
    arrived,
    cot,
    weight,
    gate_weight,
    up_weight,
    down_weight,
    active,
    gate_grad,
    up_grad,
    weighted,
    inner,
    incoming,
    produced_grad,
    out_acc,
    in_acc,
):
    step = pl.program_id(0)

    @pl.when(step == 0)
    def start():
        produced_grad[...] = (weight[...] * cot[...].astype(jnp.float32)).astype(jnp.bfloat16)
        out_acc[...] = jnp.zeros_like(out_acc)
        in_acc[...] = jnp.zeros_like(in_acc)

    gate = jnp.dot(arrived[...], gate_weight[...], preferred_element_type=jnp.float32)
    upward = jnp.dot(arrived[...], up_weight[...], preferred_element_type=jnp.float32)
    active_grad = lax.dot_general(
        produced_grad[...],
        down_weight[...],
        (((1,), (1,)), ((), ())),
        preferred_element_type=jnp.float32,
    )
    sigmoid = 1.0 / (1.0 + jnp.exp(-gate))
    silu = gate * sigmoid
    hidden = (silu * upward).astype(jnp.bfloat16)
    active[...] = hidden
    gate_back = (active_grad * upward * sigmoid * (1.0 + gate * (1.0 - sigmoid))).astype(
        jnp.bfloat16
    )
    up_back = (active_grad * silu).astype(jnp.bfloat16)
    gate_grad[...] = gate_back
    up_grad[...] = up_back
    out_acc[...] += jnp.dot(hidden, down_weight[...], preferred_element_type=jnp.float32)
    in_acc[...] += lax.dot_general(
        jnp.concatenate([gate_back, up_back], axis=1),
        jnp.concatenate([gate_weight[...], up_weight[...]], axis=1),
        (((1,), (1,)), ((), ())),
        preferred_element_type=jnp.float32,
    )

    @pl.when(step == pl.num_programs(0) - 1)
    def finish():
        produced = out_acc[...].astype(jnp.bfloat16).astype(jnp.float32)
        weighted[...] = (weight[...] * produced).astype(jnp.bfloat16)
        sums = jnp.sum(cot[...].astype(jnp.float32) * produced, axis=1, keepdims=True)
        inner[...] = jnp.transpose(jnp.broadcast_to(sums, (sums.shape[0], 128)))[:8, :]
        incoming[...] = in_acc[...].astype(jnp.bfloat16)


def run_expert(perm, arrived, cot, weight, gate_all, up_all, down_all):
    slots, width = arrived.shape
    hidden = gate_all.shape[1]
    steps = perm.shape[0]
    chunk = hidden // steps
    rows = pl.BlockSpec((slots, width), lambda c, perm: (0, 0))
    natural = pl.BlockSpec((slots, chunk), lambda c, perm: (0, perm[c]))
    turned_in = pl.BlockSpec((width, chunk), lambda c, perm: (0, perm[c]))
    wide = jax.ShapeDtypeStruct((slots, width), jnp.bfloat16)
    thin = jax.ShapeDtypeStruct((slots, hidden), jnp.bfloat16)
    return pl.pallas_call(
        expert_kernel,
        grid_spec=pltpu.PrefetchScalarGridSpec(
            num_scalar_prefetch=1,
            grid=(steps,),
            in_specs=[
                rows,
                rows,
                pl.BlockSpec((slots, 1), lambda c, perm: (0, 0)),
                turned_in,
                turned_in,
                pl.BlockSpec((chunk, width), lambda c, perm: (c, 0)),
            ],
            out_specs=[
                pl.BlockSpec((slots, chunk), lambda c, perm: (0, c)),
                natural,
                natural,
                rows,
                pl.BlockSpec((8, slots), lambda c, perm: (0, 0)),
                rows,
                rows,
            ],
            scratch_shapes=[
                pltpu.VMEM((slots, width), jnp.float32),
                pltpu.VMEM((slots, width), jnp.float32),
            ],
        ),
        out_shape=[
            thin,
            thin,
            thin,
            wide,
            jax.ShapeDtypeStruct((8, slots), jnp.float32),
            wide,
            wide,
        ],
        name="run_expert",
    )(perm, arrived, cot, weight, gate_all, up_all, down_all)


def dispatch_kernel(codes, chosen_weights, rows, *outs, capacity, experts):
    blocks, tokens = codes.shape[1:]
    numbers = lax.broadcasted_iota(jnp.int32, (capacity, tokens), 0)
    for block in range(blocks):
        span = slice(block * capacity, (block + 1) * capacity)
        placed = [
            (numbers == codes[item, block : block + 1, :]).astype(jnp.bfloat16)
            for item in range(experts)
        ]
        found = jnp.dot(
            jnp.concatenate(placed, axis=0),
            rows[block * tokens : (block + 1) * tokens, :],
            preferred_element_type=jnp.float32,
        ).astype(jnp.bfloat16)
        for item in range(experts):
            outs[item][span, :] = found[item * capacity : (item + 1) * capacity, :]

    @pl.when(pl.program_id(0) == 0)
    def weigh():
        for item in range(experts):
            for block in range(blocks):
                placed = numbers == codes[item, block : block + 1, :]
                span = slice(block * capacity, (block + 1) * capacity)
                row = chosen_weights[item, block : block + 1, :]
                outs[experts + item][span, :] = jnp.sum(
                    jnp.where(placed, row, 0.0), axis=1, keepdims=True
                )


def dispatch(codes, chosen_weights, rows, capacity):
    experts, blocks, _ = codes.shape
    slots = blocks * capacity
    width = rows.shape[1]
    block = min(width, 512)
    whole = pl.BlockSpec(codes.shape, lambda step: (0, 0, 0))
    results = pl.pallas_call(
        partial(dispatch_kernel, capacity=capacity, experts=experts),
        grid=(width // block,),
        in_specs=[whole, whole, pl.BlockSpec((rows.shape[0], block), lambda step: (0, step))],
        out_specs=[pl.BlockSpec((slots, block), lambda step: (0, step))] * experts
        + [pl.BlockSpec((slots, 1), lambda step: (0, 0))] * experts,
        out_shape=[jax.ShapeDtypeStruct((slots, width), jnp.bfloat16)] * experts
        + [jax.ShapeDtypeStruct((slots, 1), jnp.float32)] * experts,
    )(codes, chosen_weights, rows)
    return results[:experts], results[experts:]


def collect_kernel(codes, *refs, capacity, experts):
    out = refs[-1]
    blocks, tokens = codes.shape[1:]
    numbers = lax.broadcasted_iota(jnp.int32, (capacity, tokens), 0)
    for block in range(blocks):
        span = slice(block * capacity, (block + 1) * capacity)
        placed = [
            (numbers == codes[item, block : block + 1, :]).astype(jnp.bfloat16)
            for item in range(experts)
        ]
        total = lax.dot_general(
            jnp.concatenate(placed, axis=0),
            jnp.concatenate([refs[item][span, :] for item in range(experts)], axis=0),
            (((0,), (0,)), ((), ())),
            preferred_element_type=jnp.float32,
        )
        out[block * tokens : (block + 1) * tokens, :] = total.astype(jnp.bfloat16)


def collect(codes, arrays, capacity):
    experts, blocks, tokens = codes.shape
    slots, width = arrays[0].shape
    block = min(width, 512)
    return pl.pallas_call(
        partial(collect_kernel, capacity=capacity, experts=experts),
        grid=(width // block,),
        in_specs=[pl.BlockSpec(codes.shape, lambda step: (0, 0, 0))]
        + [pl.BlockSpec((slots, block), lambda step: (0, step))] * experts,
        out_specs=pl.BlockSpec((blocks * tokens, block), lambda step: (0, step)),
        out_shape=jax.ShapeDtypeStruct((blocks * tokens, width), jnp.bfloat16),
    )(codes, *arrays)


def exchange(array, offset):
    count = lax.axis_size("head")
    return lax.ppermute(array, "head", [(at, at ^ offset) for at in range(count)])


def head_pieces(array):
    return [array] + [exchange(array, offset) for offset in range(1, lax.axis_size("head"))]


def head_turn(pieces):
    return [pieces[0]] + [exchange(piece, at + 1) for at, piece in enumerate(pieces[1:])]


def add_all(pieces):
    total = pieces[0].astype(f32)
    for piece in pieces[1:]:
        total = total + piece.astype(f32)
    return total


def bit_order(turn):
    count = lax.axis_size("head").bit_length() - 1
    return [1 << ((turn + step) % count) for step in range(count)]


def gather_pieces(array, turn):
    pieces = {0: array}
    for bit in bit_order(turn):
        for offset in list(pieces):
            pieces[offset ^ bit] = exchange(pieces[offset], bit)
    return [pieces[offset] for offset in range(len(pieces))]


def scatter_pieces(pieces, turn):
    held = dict(enumerate(pieces))
    for bit in bit_order(turn):
        for offset in [item for item in held if item & bit]:
            piece = held.pop(offset).astype(bf16)
            arrived = exchange(piece, bit)
            held[offset ^ bit] = held[offset ^ bit].astype(f32) + arrived.astype(f32)
    return held[0]


def xor_order(array, axis):
    count = lax.axis_size("head")
    at = lax.axis_index("head")
    size = array.shape[axis] // count
    chunks = [
        lax.dynamic_slice_in_dim(array, (at ^ offset) * size, size, axis) for offset in range(count)
    ]
    return chunks


def xor_chunks(array, axis):
    return jnp.concatenate(xor_order(array, axis), axis=axis)


def absolute(pieces):
    at = lax.axis_index("head")
    result = []
    for place in range(len(pieces)):
        value = pieces[0]
        for offset in range(1, len(pieces)):
            value = jnp.where(at == place ^ offset, pieces[offset], value)
        result.append(value)
    return result


def move_rows(array, outer, inner, part):
    shaped = array.reshape(outer, inner, part, array.shape[1])
    return jnp.transpose(shaped, (1, 0, 2, 3)).reshape(array.shape)


def move_columns(array, outer, inner, part):
    shaped = array.reshape(array.shape[0], outer, inner, part)
    return jnp.transpose(shaped, (0, 2, 1, 3)).reshape(array.shape)


def layer(
    tokens,
    query_weight,
    key_weight,
    value_weight,
    output_weight,
    mixing_gain,
    query_gain,
    key_gain,
    routing_gain,
    router_weight,
    gate_weight,
    up_weight,
    down_weight,
    seq_lengths,
    dealt_order,
    expert_routes,
    slot_order,
    cotangent,
):
    heads_axis = lax.axis_size("head")
    blocks = lax.axis_size("blk")
    head_at = lax.axis_index("head")
    block_at = lax.axis_index("blk")
    rows, width = tokens.shape
    picks = expert_routes.shape[1]
    total_rows = dealt_order.shape[0]
    group = rows * heads_axis
    columns = width // heads_axis
    part = query_weight.shape[0]
    head_size = HDIM
    experts = router_weight.shape[1]
    local_experts = gate_weight.shape[0]
    capacity = 5 * rows * picks // (4 * experts)
    slots = blocks * capacity

    slices = [
        jnp.concatenate(chunks, axis=1)
        for chunks in zip(
            xor_order(key_weight, 1), xor_order(value_weight, 1), xor_order(query_weight, 1)
        )
    ]
    slices = head_turn(slices)
    token_pieces = head_pieces(tokens)
    rows_here = jnp.stack(absolute(slices)).reshape(heads_axis * part, 3 * columns)
    pair_full = lax.all_gather(rows_here[:, : 2 * columns], "blk", axis=0, tiled=True)
    pair_full = move_rows(pair_full, blocks, heads_axis, part)
    query_output = jnp.concatenate(
        [rows_here[:, 2 * columns :], output_weight.reshape(heads_axis * part, columns)], axis=0
    )
    query_output = lax.all_gather(query_output, "blk", axis=0, tiled=False)
    query_full = move_rows(
        query_output[:, : heads_axis * part].reshape(width, columns), blocks, heads_axis, part
    )
    output_rows = query_output[:, heads_axis * part :].reshape(columns, width)
    cot_all = lax.all_gather(cotangent, "blk", axis=0, tiled=True)

    small = jnp.concatenate(
        [
            mixing_gain[:, None],
            query_gain[:, None],
            key_gain[:, None],
            routing_gain[:, None],
            router_weight,
        ],
        axis=1,
    ).reshape(1, -1)
    codes = slot_codes(expert_routes, slot_order, experts, capacity).astype(bf16)
    sizes = small.shape[1]
    small = lax.all_gather(
        jnp.concatenate([small, codes.reshape(1, -1)], axis=1), "blk", axis=0, tiled=True
    )
    codes = small[:, sizes:].reshape(blocks, rows, experts).astype(jnp.int32)
    small = small[:, :sizes]
    small = jnp.stack(absolute(head_pieces(small))).reshape(width, 4 + experts)
    mixing_scale = small[:, 0].astype(f32)
    routing_scale = small[:, 3].astype(f32)
    query_scale = lax.dynamic_slice_in_dim(small[:, 1], head_at * columns, columns).astype(f32)
    key_scale = lax.dynamic_slice_in_dim(small[:, 2], head_at * columns, columns).astype(f32)
    router_full = small[:, 4:]
    codes_here = lax.dynamic_slice_in_dim(codes, block_at * local_experts, local_experts, 2)

    key_index = jnp.transpose(
        xor_chunks(dealt_order.reshape(heads_axis, blocks, rows), 0), (1, 0, 2)
    ).reshape(total_rows)
    key_seq = stream_layout(seq_lengths, key_index)[0]
    query_index = lax.dynamic_slice_in_dim(key_index, block_at * group, group)
    query_seq, query_position = stream_layout(seq_lengths, query_index)
    cosine, sine_part = rope_tables(query_position, head_size)
    tables = tile_lists(query_index, query_seq, key_index, key_seq, TILE)
    marks = attend_marks(
        query_index, query_index - query_position, key_index, TILE
    )
    marks = lax.optimization_barrier(marks)

    gates, ups, downs = (
        [gather_pieces(weight[item], item) for item in range(local_experts)]
        for weight in (gate_weight, up_weight, down_weight)
    )

    normed = norm_rows(token_pieces, mixing_scale)
    normed_moved = move_columns(normed, heads_axis, blocks, part)
    key_raw, key_square = project(normed, pair_full, columns)
    value_heads = jnp.dot(normed, pair_full[:, columns:], preferred_element_type=f32)
    value_heads = value_heads.astype(bf16)
    key_squares = head_pieces(key_square)
    pairs, key_factor = rope_forward(
        key_squares, key_raw, key_scale, cosine, sine_part, value_heads, width
    )
    query_raw, query_square = project(normed, query_full, columns)
    query_squares = head_pieces(query_square)
    query_heads, query_factor = rope_forward(
        query_squares, query_raw, query_scale, cosine, sine_part, None, width
    )
    pairs_all = lax.all_gather(pairs, "blk", axis=0, tiled=True)
    attended, context, totals = attend_forward(query_heads, pairs_all, marks, tables, TILE)
    branch = jnp.dot(context, output_rows, preferred_element_type=f32).astype(bf16)
    branch = head_turn([branch[piece * rows : (piece + 1) * rows] for piece in range(heads_axis)])
    own_tokens = tokens.astype(f32)
    middle = own_tokens + add_all(branch)
    middle_factor = rms_factor(jnp.sum(middle * middle, axis=-1, keepdims=True), width)
    routed = (middle * middle_factor * routing_scale).astype(bf16)

    routed_all = lax.all_gather(xor_chunks(routed, 1), "blk", axis=0, tiled=True)
    probs = jax.nn.softmax(jnp.dot(routed, router_full, preferred_element_type=f32), axis=-1)
    probs_all = jax.nn.softmax(
        jnp.dot(routed_all, xor_chunks(router_full, 0), preferred_element_type=f32), axis=-1
    )
    weight_here = lax.dynamic_slice_in_dim(
        probs_all, block_at * local_experts, local_experts, 1
    ).reshape(blocks, rows, local_experts)
    slot_ids = jnp.arange(capacity, dtype=jnp.int32)
    codes_here = jnp.transpose(codes_here, (2, 0, 1))
    weight_here = jnp.transpose(weight_here, (2, 0, 1))
    placed = codes_here[:, :, None, :] == slot_ids[None, None, :, None]
    place = placed.astype(bf16)

    def arrange(flat, weighed=True):
        lots_here = weight_here if weighed else jnp.zeros(codes_here.shape, f32)
        if capacity % 16 == 0:
            return dispatch(codes_here, lots_here, flat, capacity)
        shaped = flat.reshape(blocks, rows, width)
        lots = jnp.sum(jnp.where(placed, lots_here[:, :, None, :], 0.0), axis=-1)
        return (
            [
                jnp.einsum("srt,std->srd", item, shaped).reshape(slots, width)
                for item in place
            ],
            [item.reshape(slots, 1) for item in lots],
        )

    arrived_cot = arrange(cot_all, False)[0]
    gate_all, up_all, down_all = (
        [jnp.concatenate(pieces, axis=0) for pieces in group_pieces]
        for group_pieces in (gates, ups, downs)
    )
    arrived, slot_weight = arrange(routed_all)
    offsets = jnp.bitwise_xor(head_at, jnp.arange(heads_axis, dtype=jnp.int32))
    results = [
        run_expert(
            offsets,
            arrived[item],
            arrived_cot[item],
            slot_weight[item],
            gate_all[item],
            up_all[item],
            down_all[item],
        )
        for item in range(local_experts)
    ]

    def back_to_rows(which):
        arrays = [result[which] for result in results]
        if capacity % 16 == 0:
            return collect(codes_here, arrays, capacity)
        return sum(
            jnp.einsum(
                "srt,srd->std",
                place[item],
                arrays[item].reshape(blocks, capacity, width),
                preferred_element_type=f32,
            )
            for item in range(local_experts)
        ).astype(bf16)

    incoming = back_to_rows(5)
    combined = back_to_rows(3)
    slot_grad = jnp.stack([result[4][0] for result in results])
    slot_grad = slot_grad.reshape(local_experts, blocks, capacity, 1)
    weight_grads = jnp.sum(jnp.where(placed, slot_grad, 0.0), axis=2)
    weight_grads = jnp.transpose(weight_grads, (1, 2, 0))
    stores = [
        (arrived[item], results[item][6], results[item][0], results[item][1], results[item][2])
        for item in range(local_experts)
    ]
    routed_grad = lax.psum_scatter(
        incoming.reshape(blocks * rows, width),
        "blk",
        scatter_dimension=0,
        tiled=True,
    )
    combined = lax.psum_scatter(
        combined.reshape(blocks * rows, width),
        "blk",
        scatter_dimension=0,
        tiled=True,
    )
    block_output = (middle + combined.astype(f32)).astype(bf16)
    prob_grad = lax.all_to_all(
        weight_grads, "blk", split_axis=0, concat_axis=2, tiled=True
    ).reshape(rows, experts)

    def pieces_of(left, right):
        size = left.shape[1] // heads_axis
        products = []
        for offset in range(heads_axis):
            product = jnp.dot(
                left[:, offset * size : (offset + 1) * size].T,
                right,
                preferred_element_type=f32,
            )
            products.append(lax.optimization_barrier(product.astype(bf16)))
        return products

    def stacked(items):
        return jnp.stack(items).astype(f32)

    down_out, gate_out, up_out = (
        stacked(
            [
                scatter_pieces(pieces_of(store[left], store[right]), item)
                for item, store in enumerate(stores)
            ]
        )
        for left, right in ((2, 1), (0, 3), (0, 4))
    )

    logit_grad = (
        probs * (prob_grad - jnp.sum(probs * prob_grad, axis=1, keepdims=True))
    ).astype(bf16)
    router_sum = jnp.dot(routed.T, logit_grad, preferred_element_type=f32)
    routed_grad = xor_chunks(routed_grad, 1).astype(f32) + jnp.dot(
        logit_grad, router_full.T, preferred_element_type=f32
    )
    scaled = routed_grad * routing_scale
    inner = jnp.mean(scaled * middle, axis=-1, keepdims=True)
    middle_grad = (
        cotangent.astype(f32) + middle_factor * scaled - middle * (middle_factor**3 * inner)
    )
    routing_sum = jnp.sum(routed_grad * middle * middle_factor, axis=0)

    branch_grad = head_pieces(middle_grad.astype(bf16))
    branch_grad = jnp.concatenate(branch_grad, axis=0)
    context_grad = jnp.dot(branch_grad, output_rows.T, preferred_element_type=f32).astype(bf16)
    output_sum = jnp.dot(context.T, branch_grad, preferred_element_type=f32).astype(bf16)
    query_back, pairs_back = attend_backward(
        query_heads, pairs_all, context_grad, attended, totals, marks, tables, TILE
    )
    pairs_back = lax.psum_scatter(pairs_back, "blk", scatter_dimension=0, tiled=True)
    query_scaled, query_inner, querynorm_sum = rope_backward(
        query_back, query_raw, query_factor, query_scale, cosine, sine_part, 1
    )
    query_inner = head_pieces(query_inner)
    query_raw_grad = raw_backward(query_inner, query_scaled, query_raw, query_factor, None, width)
    query_sum = jnp.dot(normed_moved.T, query_raw_grad, preferred_element_type=f32).astype(bf16)
    query_output_sum = jnp.concatenate(
        [
            query_sum.reshape(blocks, heads_axis * part, columns),
            output_sum.reshape(blocks, heads_axis * part, columns),
        ],
        axis=1,
    ).reshape(blocks * 2 * heads_axis * part, columns)
    query_output_sum = lax.psum_scatter(query_output_sum, "blk", scatter_dimension=0, tiled=True)
    query_sum = query_output_sum[: heads_axis * part]
    output_out = query_output_sum[heads_axis * part :].reshape(part, width)
    normed_part = jnp.dot(query_raw_grad, query_full.T, preferred_element_type=f32)
    key_scaled, key_inner, keynorm_sum = rope_backward(
        pairs_back, key_raw, key_factor, key_scale, cosine, sine_part, 2
    )
    key_inner = head_pieces(key_inner)
    pair_grad = raw_backward(key_inner, key_scaled, key_raw, key_factor, pairs_back, width)
    pair_sum = jnp.dot(normed_moved.T, pair_grad, preferred_element_type=f32).astype(bf16)
    pair_sum = lax.psum_scatter(pair_sum, "blk", scatter_dimension=0, tiled=True)
    normed_part = normed_part + jnp.dot(pair_grad, pair_full.T, preferred_element_type=f32)
    normed_part = normed_part.astype(bf16)
    normed_part = head_turn(
        [normed_part[piece * rows : (piece + 1) * rows] for piece in range(heads_axis)]
    )
    normed_grad = add_all(normed_part)
    own_factor = rms_factor(jnp.sum(own_tokens * own_tokens, axis=-1, keepdims=True), width)
    scaled = normed_grad * mixing_scale
    inner = jnp.mean(scaled * own_tokens, axis=-1, keepdims=True)
    tokens_grad = middle_grad + own_factor * scaled - own_tokens * (own_factor**3 * inner)
    mixing_sum = jnp.sum(normed_grad * own_tokens * own_factor, axis=0)

    def turned_back(array):
        return jnp.stack(
            [
                jnp.concatenate(absolute(list(pieces)), axis=1).astype(f32)
                for pieces in zip(
                    *(
                        [piece[:, at : at + columns] for at in range(0, piece.shape[1], columns)]
                        for piece in head_turn(xor_order(array, 0))
                    )
                )
            ]
        )

    query_out = turned_back(query_sum)[0]
    pair_out = turned_back(pair_sum)

    blank = jnp.zeros((heads_axis, columns), f32)
    query_line = lax.dynamic_update_slice(blank, querynorm_sum, (head_at, 0)).reshape(width)
    key_line = lax.dynamic_update_slice(blank, keynorm_sum, (head_at, 0)).reshape(width)
    lines = jnp.concatenate(
        [
            mixing_sum[:, None],
            query_line[:, None],
            key_line[:, None],
            routing_sum[:, None],
            router_sum,
        ],
        axis=1,
    ).reshape(heads_axis, -1)
    lines = add_all(head_turn(xor_order(lines, 0)))
    lines = lax.all_to_all(lines.reshape(blocks, -1), "blk", 0, 0, tiled=True)
    lines = jnp.sum(lines, axis=0).reshape(part, 4 + experts)
    return (
        block_output,
        tokens_grad,
        query_out,
        pair_out[0],
        pair_out[1],
        output_out.astype(f32),
        lines[:, 0],
        lines[:, 1],
        lines[:, 2],
        lines[:, 3],
        lines[:, 4:],
        gate_out,
        up_out,
        down_out,
    )


def solution(mesh):
    in_specs = (
        P(("head", "blk"), None),
        P(("head", "blk"), None),
        P(("head", "blk"), None),
        P(("head", "blk"), None),
        P(("head", "blk"), None),
        P(("head", "blk")),
        P(("head", "blk")),
        P(("head", "blk")),
        P(("head", "blk")),
        P(("head", "blk"), None),
        P("blk", "head", None),
        P("blk", "head", None),
        P("blk", "head", None),
        P(),
        P(),
        P(("head", "blk"), None),
        P(("head", "blk"), None),
        P(("head", "blk"), None),
    )
    out_specs = (
        P(("head", "blk"), None),
        P(("head", "blk"), None),
        P(("head", "blk"), None),
        P(("head", "blk"), None),
        P(("head", "blk"), None),
        P(("head", "blk"), None),
        P(("head", "blk")),
        P(("head", "blk")),
        P(("head", "blk")),
        P(("head", "blk")),
        P(("head", "blk"), None),
        P("blk", "head", None),
        P("blk", "head", None),
        P("blk", "head", None),
    )
    return jax.shard_map(layer, mesh=mesh, in_specs=in_specs, out_specs=out_specs, check_vma=False)
```

```python
from functools import partial
import math

import jax
import jax.numpy as jnp
import numpy as np
from jax import lax
from jax.experimental import pallas as pl
from jax.experimental.pallas import tpu as pltpu
from jax.sharding import PartitionSpec as P


HDIM = 128
TILE = 256
LOG2E = 1.4426950408889634
norm_eps = 1e-05
rope_base = 10000.0
f32 = jnp.float32
bf16 = jnp.bfloat16


def rms_factor(square_sum, width):
    return lax.rsqrt(square_sum / width + norm_eps)


def rope_tables(position, head_size):
    half = head_size // 2
    freqs = rope_base ** (-(np.arange(half, dtype=np.float64) * 2.0) / head_size)
    angles = position.astype(f32)[:, None] * jnp.asarray(freqs.astype(np.float32))[None, :]
    cosine = jnp.cos(angles)
    sine_part = jnp.sin(angles)
    return (
        jnp.concatenate([cosine, cosine], axis=1),
        jnp.concatenate([-sine_part, sine_part], axis=1),
    )


def column_of(pieces):
    count = len(pieces)
    rows = pieces[0].shape[1] // count
    total = pieces[0][...]
    for offset in range(1, count):
        parts = [
            pieces[offset][:, (at ^ offset) * rows : ((at ^ offset) + 1) * rows]
            for at in range(count)
        ]
        total = total + jnp.concatenate(parts, axis=1)
    return jnp.transpose(jnp.broadcast_to(total, (8, total.shape[1])))[:, :1]


def turned(value, cosine, sine_part):
    return value * cosine + pltpu.roll(value, HDIM // 2, 1) * sine_part


def rope_kernel(*refs, count, width, paired):
    squares = refs[:count]
    raw, scale, cosine, sine_part = refs[count : count + 4]
    out, factors = refs[-2:]
    factor = lax.rsqrt(column_of(squares) / width + norm_eps)
    factors[...] = jnp.broadcast_to(factor, factors.shape)
    for head in range(raw.shape[1] // HDIM):
        span = slice(head * HDIM, (head + 1) * HDIM)
        value = turned(raw[:, span] * factor * scale[:, span], cosine[...], sine_part[...])
        if paired:
            start = 2 * head * HDIM
            out[:, start : start + HDIM] = value.astype(jnp.bfloat16)
            out[:, start + HDIM : start + 2 * HDIM] = refs[count + 4][:, span]
        else:
            out[:, span] = value.astype(jnp.bfloat16)


def rope_forward(squares, raw, scale, cosine, sine_part, values, width):
    group, columns = raw.shape
    paired = values is not None
    extra = (values,) if paired else ()
    return pl.pallas_call(
        partial(rope_kernel, count=len(squares), width=width, paired=paired),
        out_shape=[
            jax.ShapeDtypeStruct((group, columns * (2 if paired else 1)), jnp.bfloat16),
            jax.ShapeDtypeStruct((group, HDIM), jnp.float32),
        ],
    )(*squares, raw, scale[None], cosine, sine_part, *extra)


def unrope_kernel(back, raw, factors, scale, cosine, sine_part, scaled, inner, gain, *, stride):
    group = raw.shape[0]
    total = jnp.zeros((group, HDIM), jnp.float32)
    for head in range(raw.shape[1] // HDIM):
        span = slice(head * HDIM, (head + 1) * HDIM)
        start = stride * head * HDIM
        grad = back[:, start : start + HDIM].astype(jnp.float32)
        turn = turned(grad, cosine[...], -sine_part[...])
        product = turn * raw[:, span]
        gain[:, span] = jnp.sum(product * factors[...], axis=0, keepdims=True)
        scaled[:, span] = turn * scale[:, span]
        total = total + product * scale[:, span]
    sums = jnp.broadcast_to(jnp.sum(total, axis=1, keepdims=True), (group, HDIM))
    inner[...] = jnp.transpose(sums)[:1, :]


def rope_backward(back, raw, factors, scale, cosine, sine_part, stride):
    group, columns = raw.shape
    return pl.pallas_call(
        partial(unrope_kernel, stride=stride),
        out_shape=[
            jax.ShapeDtypeStruct((group, columns), jnp.float32),
            jax.ShapeDtypeStruct((1, group), jnp.float32),
            jax.ShapeDtypeStruct((1, columns), jnp.float32),
        ],
    )(back, raw, factors, scale[None], cosine, sine_part)


def raw_kernel(*refs, count, width, paired):
    scaled, raw, factors = refs[count : count + 3]
    out = refs[-1]
    inner = column_of(refs[:count]) / width
    factor = factors[:, :1]
    columns = raw.shape[1]
    slope = factor * factor * factor * inner
    for head in range(columns // HDIM):
        span = slice(head * HDIM, (head + 1) * HDIM)
        out[:, span] = (factor * scaled[:, span] - raw[:, span] * slope).astype(jnp.bfloat16)
        if paired:
            start = (2 * head + 1) * HDIM
            out[:, columns + head * HDIM : columns + (head + 1) * HDIM] = refs[count + 3][
                :, start : start + HDIM
            ]


def raw_backward(inner, scaled, raw, factors, pairs_back, width):
    group, columns = raw.shape
    paired = pairs_back is not None
    extra = (pairs_back,) if paired else ()
    return pl.pallas_call(
        partial(raw_kernel, count=len(inner), width=width, paired=paired),
        out_shape=jax.ShapeDtypeStruct((group, columns * (2 if paired else 1)), jnp.bfloat16),
    )(*inner, scaled, raw, factors, *extra)


def norm_kernel(*refs, count):
    scale, out = refs[count], refs[count + 1]
    rows, width = refs[0].shape
    for place in range(count):
        value = refs[place][...].astype(jnp.float32)
        square = jnp.sum(value * value, axis=1, keepdims=True)
        factor = lax.rsqrt(square / width + norm_eps)
        out[place * rows : (place + 1) * rows, :] = (value * factor * scale[...]).astype(
            jnp.bfloat16
        )


def norm_rows(pieces, scale):
    rows, width = pieces[0].shape
    return pl.pallas_call(
        partial(norm_kernel, count=len(pieces)),
        out_shape=jax.ShapeDtypeStruct((rows * len(pieces), width), jnp.bfloat16),
        name="norm_rows",
    )(*pieces, scale[None])


def project_kernel(normed, weight, raw, square, total):
    step = pl.program_id(0)

    @pl.when(step == 0)
    def start():
        total[...] = jnp.zeros_like(total)

    value = jnp.dot(normed[...], weight[...], preferred_element_type=jnp.float32)
    raw[...] = value
    for at in range(0, value.shape[1], HDIM):
        total[...] += value[:, at : at + HDIM] * value[:, at : at + HDIM]

    @pl.when(step == pl.num_programs(0) - 1)
    def finish():
        sums = jnp.sum(total[...], axis=1, keepdims=True)
        square[...] = jnp.transpose(jnp.broadcast_to(sums, total.shape))[:1, :]


def project(normed, weight, columns):
    group, width = normed.shape
    block = min(columns, 256)
    return pl.pallas_call(
        project_kernel,
        grid=(columns // block,),
        in_specs=[
            pl.BlockSpec((group, width), lambda step: (0, 0)),
            pl.BlockSpec((width, block), lambda step: (0, step)),
        ],
        out_specs=[
            pl.BlockSpec((group, block), lambda step: (0, step)),
            pl.BlockSpec((1, group), lambda step: (0, 0)),
        ],
        out_shape=[
            jax.ShapeDtypeStruct((group, columns), jnp.float32),
            jax.ShapeDtypeStruct((1, group), jnp.float32),
        ],
        scratch_shapes=[pltpu.VMEM((group, HDIM), jnp.float32)],
    )(normed, weight)


def slot_codes(routes, ordering, experts, capacity):
    expert_ids = jnp.arange(experts, dtype=jnp.int32)
    absent = jnp.int32(1 << 30)
    chosen = routes[:, :, None] == expert_ids[None, None, :]
    order = jnp.min(jnp.where(chosen, ordering[:, :, None], absent), axis=1)
    rank = jnp.sum((order[None, :, :] < order[:, None, :]).astype(jnp.int32), axis=1)
    return jnp.where((order < absent) & (rank < capacity), rank, -1)


def stream_layout(seq_lengths, stream_index):
    ends = jnp.cumsum(seq_lengths)
    starts = ends - seq_lengths
    passed = (stream_index[:, None] >= ends[None, :]).astype(jnp.int32)
    sequence = jnp.sum(passed, axis=1)
    owner = sequence[:, None] == jnp.arange(seq_lengths.shape[0], dtype=jnp.int32)[None, :]
    opening = jnp.sum(jnp.where(owner, starts[None, :], 0), axis=1)
    return (sequence, stream_index - opening)


def tile_lists(query_index, query_seq, key_index, key_seq, tile):
    query_tiles = query_index.shape[0] // tile
    key_tiles = key_index.shape[0] // tile
    query_marks = query_index.reshape(query_tiles, tile)
    query_seqs = query_seq.reshape(query_tiles, tile)
    key_marks = key_index.reshape(key_tiles, tile)
    key_seqs = key_seq.reshape(key_tiles, tile)
    early = jnp.min(key_marks, axis=1)[None, :] <= jnp.max(query_marks, axis=1)[:, None]
    above = jnp.max(key_seqs, axis=1)[None, :] >= jnp.min(query_seqs, axis=1)[:, None]
    below = jnp.min(key_seqs, axis=1)[None, :] <= jnp.max(query_seqs, axis=1)[:, None]
    live = (early & above & below).astype(jnp.int32)
    order = jnp.cumsum(live, axis=1) - 1
    numbers = jnp.arange(key_tiles, dtype=jnp.int32)
    hits = (order[:, :, None] == numbers[None, None, :]) & (live[:, :, None] > 0)
    listed = jnp.sum(jnp.where(hits, numbers[None, :, None], 0), axis=1)
    return (listed.astype(jnp.int32), jnp.sum(live, axis=1).astype(jnp.int32), live)


def spread(vector):
    return jnp.broadcast_to(vector[:, None], (vector.shape[0], 128))


def twice(value, count):
    return value if count == 1 else jnp.concatenate([value] * count, axis=1)


def forward_kernel(
    listed, counts, query, pairs, at, opening, key_at, attended, context, totals, total, acc, *, tile
):
    lanes = 128
    copies = tile // lanes
    factor = LOG2E / math.sqrt(HDIM)
    for step in range(query.shape[0] // tile):
        span = slice(step * tile, (step + 1) * tile)
        acc[...] = jnp.zeros_like(acc)
        total[...] = jnp.zeros_like(total)

        def visit(turn, carry):
            number = listed[step, turn]
            start = pl.multiple_of(number * tile, tile)
            scores = lax.dot_general(
                query[span, :],
                pairs[pl.ds(start, tile), :HDIM],
                (((1,), (1,)), ((), ())),
                preferred_element_type=jnp.float32,
            )
            marks = key_at[pl.ds(number, 1), :]
            allowed = (marks <= twice(at[span, :], copies)) & (
                marks >= twice(opening[span, :], copies)
            )
            expo = jnp.where(allowed, jnp.exp2(scores * factor), 0.0)
            partial_sum = expo[:, :lanes]
            for copy in range(1, copies):
                partial_sum = partial_sum + expo[:, copy * lanes : (copy + 1) * lanes]
            total[...] += partial_sum
            acc[...] += jnp.dot(
                expo.astype(jnp.bfloat16),
                pairs[pl.ds(start, tile), HDIM:],
                preferred_element_type=jnp.float32,
            )
            return carry

        lax.fori_loop(0, counts[step], visit, 0)
        full = jnp.sum(total[...], axis=1, keepdims=True)
        result = acc[...] / full
        attended[span, :] = result
        context[span, :] = result.astype(jnp.bfloat16)
        totals[span, :] = jnp.broadcast_to(full, (tile, lanes))


def attend_forward(queries, pairs, marks, tables, tile):
    group, columns = queries.shape
    total_rows = pairs.shape[0]
    listed, counts, _ = tables
    at, opening, key_at = marks[0], marks[1], marks[2]
    heads = columns // HDIM
    lane = lambda rows: pl.BlockSpec((rows, HDIM), lambda h, *refs: (0, h))
    wide = pl.BlockSpec((total_rows, 2 * HDIM), lambda h, *refs: (0, h))
    fixed = lambda array: pl.BlockSpec(array.shape, lambda h, *refs: (0, 0))
    return pl.pallas_call(
        partial(forward_kernel, tile=tile),
        grid_spec=pltpu.PrefetchScalarGridSpec(
            num_scalar_prefetch=2,
            grid=(heads,),
            in_specs=[
                lane(group),
                wide,
                fixed(at),
                fixed(opening),
                fixed(key_at),
            ],
            out_specs=[lane(group), lane(group), lane(group)],
            scratch_shapes=[
                pltpu.VMEM((tile, HDIM), jnp.float32),
                pltpu.VMEM((tile, HDIM), jnp.float32),
            ],
        ),
        out_shape=[
            jax.ShapeDtypeStruct((group, columns), jnp.float32),
            jax.ShapeDtypeStruct((group, columns), jnp.bfloat16),
            jax.ShapeDtypeStruct((group, columns), jnp.float32),
        ],
        name="attend_forward",
    )(listed, counts, queries, pairs, at, opening, key_at)


def backward_kernel(
    live,
    query,
    pairs,
    grad,
    attended,
    totals,
    at_row,
    opening_row,
    key_col,
    query_out,
    pairs_out,
    scaled,
    offset,
    query_acc,
    key_acc,
    value_acc,
    *,
    tile,
):
    copies = tile // 128
    steps = query.shape[0] // tile
    factor = 1.0 / math.sqrt(HDIM)
    grads = grad[...].astype(jnp.float32)
    scaled[...] = (grads / totals[...]).astype(jnp.bfloat16)
    sums = jnp.sum(grads * attended[...], axis=1, keepdims=True) / totals[...]
    offset[...] = jnp.transpose(sums)[:8, :]
    query_acc[...] = jnp.zeros_like(query_acc)

    def visit(number, carry):
        start = pl.multiple_of(number * tile, tile)
        window = pl.ds(start, tile)
        key_acc[...] = jnp.zeros_like(key_acc)
        value_acc[...] = jnp.zeros_like(value_acc)
        for step in range(steps):
            span = slice(step * tile, (step + 1) * tile)

            @pl.when(live[step, number] > 0)
            def unused():
                scores = lax.dot_general(
                    pairs[window, :HDIM],
                    query[span, :],
                    (((1,), (1,)), ((), ())),
                    preferred_element_type=jnp.float32,
                )
                marks = twice(key_col[window, :], copies)
                allowed = (marks <= at_row[:, span]) & (marks >= opening_row[:, span])
                expo = jnp.where(allowed, jnp.exp2(scores * (factor * LOG2E)), 0.0)
                inner = lax.dot_general(
                    pairs[window, HDIM:],
                    scaled[span, :],
                    (((1,), (1,)), ((), ())),
                    preferred_element_type=jnp.float32,
                )
                back = (expo * (inner - offset[0:1, span])).astype(jnp.bfloat16)
                key_acc[...] += jnp.dot(back, query[span, :], preferred_element_type=jnp.float32)
                value_acc[...] += jnp.dot(
                    expo.astype(jnp.bfloat16), scaled[span, :], preferred_element_type=jnp.float32
                )
                query_acc[span, :] += lax.dot_general(
                    back,
                    pairs[window, :HDIM],
                    (((0,), (0,)), ((), ())),
                    preferred_element_type=jnp.float32,
                )

        pairs_out[window, :HDIM] = (key_acc[...] * factor).astype(jnp.bfloat16)
        pairs_out[window, HDIM:] = value_acc[...].astype(jnp.bfloat16)
        return carry

    lax.fori_loop(0, pairs.shape[0] // tile, visit, 0)
    query_out[...] = (query_acc[...] * factor).astype(jnp.bfloat16)


def attend_backward(queries, pairs, grads, attended, totals, marks, tables, tile):
    group, columns = queries.shape
    total_rows = pairs.shape[0]
    live = tables[2]
    at_row, opening_row, key_col = marks[3], marks[4], marks[5]
    heads = columns // HDIM
    lane = lambda rows: pl.BlockSpec((rows, HDIM), lambda h, *refs: (0, h))
    wide = pl.BlockSpec((total_rows, 2 * HDIM), lambda h, *refs: (0, h))
    fixed = lambda array: pl.BlockSpec(array.shape, lambda h, *refs: (0, 0))
    return pl.pallas_call(
        partial(backward_kernel, tile=tile),
        grid_spec=pltpu.PrefetchScalarGridSpec(
            num_scalar_prefetch=1,
            grid=(heads,),
            in_specs=[
                lane(group),
                wide,
                lane(group),
                lane(group),
                lane(group),
                fixed(at_row),
                fixed(opening_row),
                fixed(key_col),
            ],
            out_specs=[lane(group), wide],
            scratch_shapes=[
                pltpu.VMEM((group, HDIM), jnp.bfloat16),
                pltpu.VMEM((8, group), jnp.float32),
                pltpu.VMEM((group, HDIM), jnp.float32),
                pltpu.VMEM((tile, HDIM), jnp.float32),
                pltpu.VMEM((tile, HDIM), jnp.float32),
            ],
        ),
        out_shape=[
            jax.ShapeDtypeStruct((group, columns), jnp.bfloat16),
            jax.ShapeDtypeStruct((total_rows, 2 * columns), jnp.bfloat16),
        ],
        name="attend_backward",
    )(live, queries, pairs, grads, attended, totals, at_row, opening_row, key_col)


def attend_marks(query_index, query_start, key_index, tile):
    return (
        spread(query_index),
        spread(query_start),
        key_index.reshape(-1, tile),
        query_index[None, :],
        query_start[None, :],
        spread(key_index),
    )


def expert_kernel(
    perm,
    arrived,
    cot,
    weight,
    gate_weight,
    up_weight,
    down_weight,
    active,
    gate_grad,
    up_grad,
    weighted,
    inner,
    incoming,
    produced_grad,
    out_acc,
    in_acc,
):
    step = pl.program_id(0)

    @pl.when(step == 0)
    def start():
        produced_grad[...] = (weight[...] * cot[...].astype(jnp.float32)).astype(jnp.bfloat16)
        out_acc[...] = jnp.zeros_like(out_acc)
        in_acc[...] = jnp.zeros_like(in_acc)

    gate = jnp.dot(arrived[...], gate_weight[...], preferred_element_type=jnp.float32)
    upward = jnp.dot(arrived[...], up_weight[...], preferred_element_type=jnp.float32)
    active_grad = lax.dot_general(
        produced_grad[...],
        down_weight[...],
        (((1,), (1,)), ((), ())),
        preferred_element_type=jnp.float32,
    )
    sigmoid = 1.0 / (1.0 + jnp.exp(-gate))
    silu = gate * sigmoid
    hidden = (silu * upward).astype(jnp.bfloat16)
    active[...] = hidden
    gate_back = (active_grad * upward * sigmoid * (1.0 + gate * (1.0 - sigmoid))).astype(
        jnp.bfloat16
    )
    up_back = (active_grad * silu).astype(jnp.bfloat16)
    gate_grad[...] = gate_back
    up_grad[...] = up_back
    out_acc[...] += jnp.dot(hidden, down_weight[...], preferred_element_type=jnp.float32)
    in_acc[...] += lax.dot_general(
        jnp.concatenate([gate_back, up_back], axis=1),
        jnp.concatenate([gate_weight[...], up_weight[...]], axis=1),
        (((1,), (1,)), ((), ())),
        preferred_element_type=jnp.float32,
    )

    @pl.when(step == pl.num_programs(0) - 1)
    def finish():
        produced = out_acc[...].astype(jnp.bfloat16).astype(jnp.float32)
        weighted[...] = (weight[...] * produced).astype(jnp.bfloat16)
        sums = jnp.sum(cot[...].astype(jnp.float32) * produced, axis=1, keepdims=True)
        inner[...] = jnp.transpose(jnp.broadcast_to(sums, (sums.shape[0], 128)))[:8, :]
        incoming[...] = in_acc[...].astype(jnp.bfloat16)


def run_expert(perm, arrived, cot, weight, gate_all, up_all, down_all):
    slots, width = arrived.shape
    hidden = gate_all.shape[1]
    steps = perm.shape[0]
    chunk = hidden // steps
    rows = pl.BlockSpec((slots, width), lambda c, perm: (0, 0))
    natural = pl.BlockSpec((slots, chunk), lambda c, perm: (0, perm[c]))
    turned_in = pl.BlockSpec((width, chunk), lambda c, perm: (0, perm[c]))
    wide = jax.ShapeDtypeStruct((slots, width), jnp.bfloat16)
    thin = jax.ShapeDtypeStruct((slots, hidden), jnp.bfloat16)
    return pl.pallas_call(
        expert_kernel,
        grid_spec=pltpu.PrefetchScalarGridSpec(
            num_scalar_prefetch=1,
            grid=(steps,),
            in_specs=[
                rows,
                rows,
                pl.BlockSpec((slots, 1), lambda c, perm: (0, 0)),
                turned_in,
                turned_in,
                pl.BlockSpec((chunk, width), lambda c, perm: (c, 0)),
            ],
            out_specs=[
                pl.BlockSpec((slots, chunk), lambda c, perm: (0, c)),
                natural,
                natural,
                rows,
                pl.BlockSpec((8, slots), lambda c, perm: (0, 0)),
                rows,
                rows,
            ],
            scratch_shapes=[
                pltpu.VMEM((slots, width), jnp.float32),
                pltpu.VMEM((slots, width), jnp.float32),
            ],
        ),
        out_shape=[
            thin,
            thin,
            thin,
            wide,
            jax.ShapeDtypeStruct((8, slots), jnp.float32),
            wide,
            wide,
        ],
        name="run_expert",
    )(perm, arrived, cot, weight, gate_all, up_all, down_all)


def dispatch_kernel(codes, chosen_weights, rows, *outs, capacity, experts):
    blocks, tokens = codes.shape[1:]
    numbers = lax.broadcasted_iota(jnp.int32, (capacity, tokens), 0)
    for block in range(blocks):
        span = slice(block * capacity, (block + 1) * capacity)
        placed = [
            (numbers == codes[item, block : block + 1, :]).astype(jnp.bfloat16)
            for item in range(experts)
        ]
        found = jnp.dot(
            jnp.concatenate(placed, axis=0),
            rows[block * tokens : (block + 1) * tokens, :],
            preferred_element_type=jnp.float32,
        ).astype(jnp.bfloat16)
        for item in range(experts):
            outs[item][span, :] = found[item * capacity : (item + 1) * capacity, :]

    @pl.when(pl.program_id(0) == 0)
    def weigh():
        for item in range(experts):
            for block in range(blocks):
                placed = numbers == codes[item, block : block + 1, :]
                span = slice(block * capacity, (block + 1) * capacity)
                row = chosen_weights[item, block : block + 1, :]
                outs[experts + item][span, :] = jnp.sum(
                    jnp.where(placed, row, 0.0), axis=1, keepdims=True
                )


def dispatch(codes, chosen_weights, rows, capacity):
    experts, blocks, _ = codes.shape
    slots = blocks * capacity
    width = rows.shape[1]
    block = min(width, 512)
    whole = pl.BlockSpec(codes.shape, lambda step: (0, 0, 0))
    results = pl.pallas_call(
        partial(dispatch_kernel, capacity=capacity, experts=experts),
        grid=(width // block,),
        in_specs=[whole, whole, pl.BlockSpec((rows.shape[0], block), lambda step: (0, step))],
        out_specs=[pl.BlockSpec((slots, block), lambda step: (0, step))] * experts
        + [pl.BlockSpec((slots, 1), lambda step: (0, 0))] * experts,
        out_shape=[jax.ShapeDtypeStruct((slots, width), jnp.bfloat16)] * experts
        + [jax.ShapeDtypeStruct((slots, 1), jnp.float32)] * experts,
    )(codes, chosen_weights, rows)
    return results[:experts], results[experts:]


def collect_kernel(codes, *refs, capacity, experts):
    out = refs[-1]
    blocks, tokens = codes.shape[1:]
    numbers = lax.broadcasted_iota(jnp.int32, (capacity, tokens), 0)
    for block in range(blocks):
        span = slice(block * capacity, (block + 1) * capacity)
        placed = [
            (numbers == codes[item, block : block + 1, :]).astype(jnp.bfloat16)
            for item in range(experts)
        ]
        total = lax.dot_general(
            jnp.concatenate(placed, axis=0),
            jnp.concatenate([refs[item][span, :] for item in range(experts)], axis=0),
            (((0,), (0,)), ((), ())),
            preferred_element_type=jnp.float32,
        )
        out[block * tokens : (block + 1) * tokens, :] = total.astype(jnp.bfloat16)


def collect(codes, arrays, capacity):
    experts, blocks, tokens = codes.shape
    slots, width = arrays[0].shape
    block = min(width, 512)
    return pl.pallas_call(
        partial(collect_kernel, capacity=capacity, experts=experts),
        grid=(width // block,),
        in_specs=[pl.BlockSpec(codes.shape, lambda step: (0, 0, 0))]
        + [pl.BlockSpec((slots, block), lambda step: (0, step))] * experts,
        out_specs=pl.BlockSpec((blocks * tokens, block), lambda step: (0, step)),
        out_shape=jax.ShapeDtypeStruct((blocks * tokens, width), jnp.bfloat16),
    )(codes, *arrays)


def exchange(array, offset):
    count = lax.axis_size("head")
    return lax.ppermute(array, "head", [(at, at ^ offset) for at in range(count)])


def head_pieces(array):
    return [array] + [exchange(array, offset) for offset in range(1, lax.axis_size("head"))]


def head_turn(pieces):
    return [pieces[0]] + [exchange(piece, at + 1) for at, piece in enumerate(pieces[1:])]


def add_all(pieces):
    total = pieces[0].astype(f32)
    for piece in pieces[1:]:
        total = total + piece.astype(f32)
    return total


def bit_order(turn):
    count = lax.axis_size("head").bit_length() - 1
    return [1 << ((turn + step) % count) for step in range(count)]


def gather_pieces(array, turn):
    pieces = {0: array}
    for bit in bit_order(turn):
        for offset in list(pieces):
            pieces[offset ^ bit] = exchange(pieces[offset], bit)
    return [pieces[offset] for offset in range(len(pieces))]


def scatter_pieces(pieces, turn):
    held = dict(enumerate(pieces))
    for bit in bit_order(turn):
        for offset in [item for item in held if item & bit]:
            piece = held.pop(offset).astype(bf16)
            arrived = exchange(piece, bit)
            held[offset ^ bit] = held[offset ^ bit].astype(f32) + arrived.astype(f32)
    return held[0]


def xor_order(array, axis):
    count = lax.axis_size("head")
    at = lax.axis_index("head")
    size = array.shape[axis] // count
    chunks = [
        lax.dynamic_slice_in_dim(array, (at ^ offset) * size, size, axis) for offset in range(count)
    ]
    return chunks


def xor_chunks(array, axis):
    return jnp.concatenate(xor_order(array, axis), axis=axis)


def absolute(pieces):
    at = lax.axis_index("head")
    result = []
    for place in range(len(pieces)):
        value = pieces[0]
        for offset in range(1, len(pieces)):
            value = jnp.where(at == place ^ offset, pieces[offset], value)
        result.append(value)
    return result


def move_rows(array, outer, inner, part):
    shaped = array.reshape(outer, inner, part, array.shape[1])
    return jnp.transpose(shaped, (1, 0, 2, 3)).reshape(array.shape)


def move_columns(array, outer, inner, part):
    shaped = array.reshape(array.shape[0], outer, inner, part)
    return jnp.transpose(shaped, (0, 2, 1, 3)).reshape(array.shape)


def layer(
    tokens,
    query_weight,
    key_weight,
    value_weight,
    output_weight,
    mixing_gain,
    query_gain,
    key_gain,
    routing_gain,
    router_weight,
    gate_weight,
    up_weight,
    down_weight,
    seq_lengths,
    dealt_order,
    expert_routes,
    slot_order,
    cotangent,
):
    heads_axis = lax.axis_size("head")
    blocks = lax.axis_size("blk")
    head_at = lax.axis_index("head")
    block_at = lax.axis_index("blk")
    rows, width = tokens.shape
    picks = expert_routes.shape[1]
    total_rows = dealt_order.shape[0]
    group = rows * heads_axis
    columns = width // heads_axis
    part = query_weight.shape[0]
    head_size = HDIM
    experts = router_weight.shape[1]
    local_experts = gate_weight.shape[0]
    capacity = 5 * rows * picks // (4 * experts)
    slots = blocks * capacity

    slices = [
        jnp.concatenate(chunks, axis=1)
        for chunks in zip(
            xor_order(key_weight, 1), xor_order(value_weight, 1), xor_order(query_weight, 1)
        )
    ]
    slices = head_turn(slices)
    token_pieces = head_pieces(tokens)
    rows_here = jnp.stack(absolute(slices)).reshape(heads_axis * part, 3 * columns)
    pair_full = lax.all_gather(rows_here[:, : 2 * columns], "blk", axis=0, tiled=True)
    pair_full = move_rows(pair_full, blocks, heads_axis, part)
    query_output = jnp.concatenate(
        [rows_here[:, 2 * columns :], output_weight.reshape(heads_axis * part, columns)], axis=0
    )
    query_output = lax.all_gather(query_output, "blk", axis=0, tiled=False)
    query_full = move_rows(
        query_output[:, : heads_axis * part].reshape(width, columns), blocks, heads_axis, part
    )
    output_rows = query_output[:, heads_axis * part :].reshape(columns, width)
    cot_all = lax.all_gather(cotangent, "blk", axis=0, tiled=True)

    small = jnp.concatenate(
        [
            mixing_gain[:, None],
            query_gain[:, None],
            key_gain[:, None],
            routing_gain[:, None],
            router_weight,
        ],
        axis=1,
    ).reshape(1, -1)
    codes = slot_codes(expert_routes, slot_order, experts, capacity).astype(bf16)
    sizes = small.shape[1]
    small = lax.all_gather(
        jnp.concatenate([small, codes.reshape(1, -1)], axis=1), "blk", axis=0, tiled=True
    )
    codes = small[:, sizes:].reshape(blocks, rows, experts).astype(jnp.int32)
    small = small[:, :sizes]
    small = jnp.stack(absolute(head_pieces(small))).reshape(width, 4 + experts)
    mixing_scale = small[:, 0].astype(f32)
    routing_scale = small[:, 3].astype(f32)
    query_scale = lax.dynamic_slice_in_dim(small[:, 1], head_at * columns, columns).astype(f32)
    key_scale = lax.dynamic_slice_in_dim(small[:, 2], head_at * columns, columns).astype(f32)
    router_full = small[:, 4:]
    codes_here = lax.dynamic_slice_in_dim(codes, block_at * local_experts, local_experts, 2)

    key_index = jnp.transpose(
        xor_chunks(dealt_order.reshape(heads_axis, blocks, rows), 0), (1, 0, 2)
    ).reshape(total_rows)
    key_seq = stream_layout(seq_lengths, key_index)[0]
    query_index = lax.dynamic_slice_in_dim(key_index, block_at * group, group)
    query_seq, query_position = stream_layout(seq_lengths, query_index)
    cosine, sine_part = rope_tables(query_position, head_size)
    tables = tile_lists(query_index, query_seq, key_index, key_seq, TILE)
    marks = attend_marks(
        query_index, query_index - query_position, key_index, TILE
    )
    marks = lax.optimization_barrier(marks)

    gates, ups, downs = (
        [gather_pieces(weight[item], item) for item in range(local_experts)]
        for weight in (gate_weight, up_weight, down_weight)
    )

    normed = norm_rows(token_pieces, mixing_scale)
    normed_moved = move_columns(normed, heads_axis, blocks, part)
    key_raw, key_square = project(normed, pair_full, columns)
    value_heads = jnp.dot(normed, pair_full[:, columns:], preferred_element_type=f32)
    value_heads = value_heads.astype(bf16)
    key_squares = head_pieces(key_square)
    pairs, key_factor = rope_forward(
        key_squares, key_raw, key_scale, cosine, sine_part, value_heads, width
    )
    query_raw, query_square = project(normed, query_full, columns)
    query_squares = head_pieces(query_square)
    query_heads, query_factor = rope_forward(
        query_squares, query_raw, query_scale, cosine, sine_part, None, width
    )
    pairs_all = lax.all_gather(pairs, "blk", axis=0, tiled=True)
    attended, context, totals = attend_forward(query_heads, pairs_all, marks, tables, TILE)
    branch = jnp.dot(context, output_rows, preferred_element_type=f32).astype(bf16)
    branch = head_turn([branch[piece * rows : (piece + 1) * rows] for piece in range(heads_axis)])
    own_tokens = tokens.astype(f32)
    middle = own_tokens + add_all(branch)
    middle_factor = rms_factor(jnp.sum(middle * middle, axis=-1, keepdims=True), width)
    routed = (middle * middle_factor * routing_scale).astype(bf16)

    routed_all = lax.all_gather(xor_chunks(routed, 1), "blk", axis=0, tiled=True)
    probs = jax.nn.softmax(jnp.dot(routed, router_full, preferred_element_type=f32), axis=-1)
    probs_all = jax.nn.softmax(
        jnp.dot(routed_all, xor_chunks(router_full, 0), preferred_element_type=f32), axis=-1
    )
    weight_here = lax.dynamic_slice_in_dim(
        probs_all, block_at * local_experts, local_experts, 1
    ).reshape(blocks, rows, local_experts)
    slot_ids = jnp.arange(capacity, dtype=jnp.int32)
    codes_here = jnp.transpose(codes_here, (2, 0, 1))
    weight_here = jnp.transpose(weight_here, (2, 0, 1))
    placed = codes_here[:, :, None, :] == slot_ids[None, None, :, None]
    place = placed.astype(bf16)

    def arrange(flat, weighed=True):
        lots_here = weight_here if weighed else jnp.zeros(codes_here.shape, f32)
        if capacity % 16 == 0:
            return dispatch(codes_here, lots_here, flat, capacity)
        shaped = flat.reshape(blocks, rows, width)
        lots = jnp.sum(jnp.where(placed, lots_here[:, :, None, :], 0.0), axis=-1)
        return (
            [
                jnp.einsum("srt,std->srd", item, shaped).reshape(slots, width)
                for item in place
            ],
            [item.reshape(slots, 1) for item in lots],
        )

    arrived_cot = arrange(cot_all, False)[0]
    gate_all, up_all, down_all = (
        [jnp.concatenate(pieces, axis=0) for pieces in group_pieces]
        for group_pieces in (gates, ups, downs)
    )
    arrived, slot_weight = arrange(routed_all)
    offsets = jnp.bitwise_xor(head_at, jnp.arange(heads_axis, dtype=jnp.int32))
    results = [
        run_expert(
            offsets,
            arrived[item],
            arrived_cot[item],
            slot_weight[item],
            gate_all[item],
            up_all[item],
            down_all[item],
        )
        for item in range(local_experts)
    ]

    def back_to_rows(which):
        arrays = [result[which] for result in results]
        if capacity % 16 == 0:
            return collect(codes_here, arrays, capacity)
        return sum(
            jnp.einsum(
                "srt,srd->std",
                place[item],
                arrays[item].reshape(blocks, capacity, width),
                preferred_element_type=f32,
            )
            for item in range(local_experts)
        ).astype(bf16)

    incoming = back_to_rows(5)
    combined = back_to_rows(3)
    slot_grad = jnp.stack([result[4][0] for result in results])
    slot_grad = slot_grad.reshape(local_experts, blocks, capacity, 1)
    weight_grads = jnp.sum(jnp.where(placed, slot_grad, 0.0), axis=2)
    weight_grads = jnp.transpose(weight_grads, (1, 2, 0))
    stores = [
        (arrived[item], results[item][6], results[item][0], results[item][1], results[item][2])
        for item in range(local_experts)
    ]
    routed_grad = lax.psum_scatter(
        incoming.reshape(blocks * rows, width),
        "blk",
        scatter_dimension=0,
        tiled=True,
    )
    combined = lax.psum_scatter(
        combined.reshape(blocks * rows, width),
        "blk",
        scatter_dimension=0,
        tiled=True,
    )
    block_output = (middle + combined.astype(f32)).astype(bf16)
    prob_grad = lax.all_to_all(
        weight_grads, "blk", split_axis=0, concat_axis=2, tiled=True
    ).reshape(rows, experts)

    def pieces_of(left, right):
        size = left.shape[1] // heads_axis
        products = []
        for offset in range(heads_axis):
            product = jnp.dot(
                left[:, offset * size : (offset + 1) * size].T,
                right,
                preferred_element_type=f32,
            )
            products.append(lax.optimization_barrier(product.astype(bf16)))
        return products

    def stacked(items):
        return jnp.stack(items).astype(f32)

    down_out, gate_out, up_out = (
        stacked(
            [
                scatter_pieces(pieces_of(store[left], store[right]), item)
                for item, store in enumerate(stores)
            ],
        )
        for left, right in ((2, 1), (0, 3), (0, 4))
    )

    logit_grad = (
        probs * (prob_grad - jnp.sum(probs * prob_grad, axis=1, keepdims=True))
    ).astype(bf16)
    router_sum = jnp.dot(routed.T, logit_grad, preferred_element_type=f32)
    routed_grad = xor_chunks(routed_grad, 1).astype(f32) + jnp.dot(
        logit_grad, router_full.T, preferred_element_type=f32
    )
    scaled = routed_grad * routing_scale
    inner = jnp.mean(scaled * middle, axis=-1, keepdims=True)
    middle_grad = (
        cotangent.astype(f32) + middle_factor * scaled - middle * (middle_factor**3 * inner)
    )
    routing_sum = jnp.sum(routed_grad * middle * middle_factor, axis=0)

    branch_grad = head_pieces(middle_grad.astype(bf16))
    branch_grad = jnp.concatenate(branch_grad, axis=0)
    context_grad = jnp.dot(branch_grad, output_rows.T, preferred_element_type=f32).astype(bf16)
    output_sum = jnp.dot(context.T, branch_grad, preferred_element_type=f32).astype(bf16)
    query_back, pairs_back = attend_backward(
        query_heads, pairs_all, context_grad, attended, totals, marks, tables, TILE
    )
    pairs_back = lax.psum_scatter(pairs_back, "blk", scatter_dimension=0, tiled=True)
    query_scaled, query_inner, querynorm_sum = rope_backward(
        query_back, query_raw, query_factor, query_scale, cosine, sine_part, 1
    )
    query_inner = head_pieces(query_inner)
    query_raw_grad = raw_backward(query_inner, query_scaled, query_raw, query_factor, None, width)
    query_sum = jnp.dot(normed_moved.T, query_raw_grad, preferred_element_type=f32).astype(bf16)
    query_output_sum = jnp.concatenate(
        [
            query_sum.reshape(blocks, heads_axis * part, columns),
            output_sum.reshape(blocks, heads_axis * part, columns),
        ],
        axis=1,
    ).reshape(blocks * 2 * heads_axis * part, columns)
    query_output_sum = lax.psum_scatter(query_output_sum, "blk", scatter_dimension=0, tiled=True)
    query_sum = query_output_sum[: heads_axis * part]
    output_out = query_output_sum[heads_axis * part :].reshape(part, width)
    normed_part = jnp.dot(query_raw_grad, query_full.T, preferred_element_type=f32)
    key_scaled, key_inner, keynorm_sum = rope_backward(
        pairs_back, key_raw, key_factor, key_scale, cosine, sine_part, 2
    )
    key_inner = head_pieces(key_inner)
    pair_grad = raw_backward(key_inner, key_scaled, key_raw, key_factor, pairs_back, width)
    pair_sum = jnp.dot(normed_moved.T, pair_grad, preferred_element_type=f32).astype(bf16)
    pair_sum = lax.psum_scatter(pair_sum, "blk", scatter_dimension=0, tiled=True)
    normed_part = normed_part + jnp.dot(pair_grad, pair_full.T, preferred_element_type=f32)
    normed_part = normed_part.astype(bf16)
    normed_part = head_turn(
        [normed_part[piece * rows : (piece + 1) * rows] for piece in range(heads_axis)]
    )
    normed_grad = add_all(normed_part)
    own_factor = rms_factor(jnp.sum(own_tokens * own_tokens, axis=-1, keepdims=True), width)
    scaled = normed_grad * mixing_scale
    inner = jnp.mean(scaled * own_tokens, axis=-1, keepdims=True)
    mixing_sum = jnp.sum(normed_grad * own_tokens * own_factor, axis=0)
    tokens_grad = middle_grad + own_factor * scaled - own_tokens * (own_factor**3 * inner)

    def turned_back(array):
        return jnp.stack(
            [
                jnp.concatenate(absolute(list(pieces)), axis=1).astype(f32)
                for pieces in zip(
                    *(
                        [piece[:, at : at + columns] for at in range(0, piece.shape[1], columns)]
                        for piece in head_turn(xor_order(array, 0))
                    )
                )
            ]
        )

    query_out = turned_back(query_sum)[0]
    pair_out = turned_back(pair_sum)

    blank = jnp.zeros((heads_axis, columns), f32)
    query_line = lax.dynamic_update_slice(blank, querynorm_sum, (head_at, 0)).reshape(width)
    key_line = lax.dynamic_update_slice(blank, keynorm_sum, (head_at, 0)).reshape(width)
    lines = jnp.concatenate(
        [
            mixing_sum[:, None],
            query_line[:, None],
            key_line[:, None],
            routing_sum[:, None],
            router_sum,
        ],
        axis=1,
    ).reshape(heads_axis, -1)
    lines = xor_order(lines, 0)
    lines = add_all(head_turn(lines))
    lines = lax.all_to_all(lines.reshape(blocks, -1), "blk", 0, 0, tiled=True)
    lines = jnp.sum(lines, axis=0).reshape(part, 4 + experts)
    return (
        block_output,
        tokens_grad,
        query_out,
        pair_out[0],
        pair_out[1],
        output_out.astype(f32),
        lines[:, 0],
        lines[:, 1],
        lines[:, 2],
        lines[:, 3],
        lines[:, 4:],
        gate_out,
        up_out,
        down_out,
    )


def solution(mesh):
    in_specs = (
        P(("head", "blk"), None),
        P(("head", "blk"), None),
        P(("head", "blk"), None),
        P(("head", "blk"), None),
        P(("head", "blk"), None),
        P(("head", "blk")),
        P(("head", "blk")),
        P(("head", "blk")),
        P(("head", "blk")),
        P(("head", "blk"), None),
        P("blk", "head", None),
        P("blk", "head", None),
        P("blk", "head", None),
        P(),
        P(),
        P(("head", "blk"), None),
        P(("head", "blk"), None),
        P(("head", "blk"), None),
    )
    out_specs = (
        P(("head", "blk"), None),
        P(("head", "blk"), None),
        P(("head", "blk"), None),
        P(("head", "blk"), None),
        P(("head", "blk"), None),
        P(("head", "blk"), None),
        P(("head", "blk")),
        P(("head", "blk")),
        P(("head", "blk")),
        P(("head", "blk")),
        P(("head", "blk"), None),
        P("blk", "head", None),
        P("blk", "head", None),
        P("blk", "head", None),
    )
    return jax.shard_map(layer, mesh=mesh, in_specs=in_specs, out_specs=out_specs, check_vma=False)
```
